512 devices in a mesh: ctx: 32 (over y, z_lo), head: 4 (over x), batch: 4 (over z_hi, core).
Axes of the slice: x: 4, y: 8, z: 8 (z_hi: 2, z_lo: 4; z = z_hi * 4 + z_lo), core: 2. Of those that a mesh axis runs over, the one named last changes fastest.
Arguments:
- queries: bfloat16 [4, 4096, 20, 128], P('batch', 'ctx', 'head'), may hold values from -64 to 64
- key_rows: bfloat16 [4, 4096, 4, 128], P('batch', 'ctx', 'head'), may hold values from -8 to 8
- block_order: int32 [64], replicated, may hold values from 0 to 63, each once
- conv_len: int32 [4], replicated, may hold values from 2048 to 4096
- gate_wq: float32 [128, 128], replicated, may hold values from -32 to 32
- gate_wk: float32 [384, 128], replicated, may hold values from -32 to 32
Outputs:
- teacher_map: float32 [4, 20, 64, 64], P('batch', 'head', 'ctx')
- grad_wq: float32 [128, 128], replicated
- grad_wk: float32 [384, 128], replicated
The draws below stay inside these ranges and needn't reach their ends.
All inputs are finite; a program needn't handle non-finite values.
Results may differ from the reference program's by a relative error of at most 0.0003.
Values may be sent and summed in bfloat16 or wider, within the bound.
No kernel may reach another device: no remote copies, remote signals or barrier semaphores. Data moves between devices by JAX's collectives and lax.ppermute only.
A program may use at most 64 MiB of HBM per device.

```python
import math
import jax
import jax.numpy as jnp
from jax import lax

D_HEAD = 128
HQ = 20
KVH = 4
GD = 128
BLK = 64
SEQ = 4096
NBLK = 64
BATCH = 4


def pair_draw(key):
    base_key = jax.random.fold_in(key, 11)
    subkeys = jax.random.split(base_key, 2)
    query_shape = (BATCH, SEQ, HQ, D_HEAD)
    key_shape = (BATCH, SEQ, KVH, D_HEAD)
    key_vals = jax.random.truncated_normal(subkeys[0], -6.0, 6.0, key_shape, jnp.float32)
    query_vals = jax.random.truncated_normal(subkeys[1], -6.0, 6.0, query_shape, jnp.float32)
    return (query_vals, key_vals)


def draw_queries(key, part):
    return pair_draw(key)[0].astype(jnp.bfloat16)


def draw_key_rows(key, part):
    return pair_draw(key)[1].astype(jnp.bfloat16)


def weight_draw(key, rows_in, cols_out):
    subkeys = jax.random.split(jax.random.fold_in(key, 5), 2)
    column_scale = jnp.exp(jax.random.uniform(subkeys[0], (1, cols_out), jnp.float32, 0.0, math.log(10.0)))
    values = jax.random.truncated_normal(subkeys[1], -4.0, 4.0, (rows_in, cols_out), jnp.float32)
    return values * column_scale / math.sqrt(rows_in)


def draw_gate_wq(key, part):
    return weight_draw(key, D_HEAD, GD)


def draw_gate_wk(key, part):
    return weight_draw(key, 3 * D_HEAD, GD)


def set_ends(values, own_key, low, top_value):
    longest = values.shape.index(max(values.shape))
    spots = []
    for shift in (0, 1):
        where = [jax.random.randint(jax.random.fold_in(own_key, axis), (), 0, length) for axis, length in enumerate(values.shape)]
        where[longest] = (where[longest] + shift) % values.shape[longest]
        spots.append(tuple(where))
    return values.at[spots[0]].set(low).at[spots[1]].set(top_value)


def setup_inputs(seed: int = 0) -> dict:
    keys = jax.random.split(jax.random.key(seed), 7)
    return {
        "queries": draw_queries(jax.random.fold_in(keys[6], 71), 0),
        "key_rows": draw_key_rows(jax.random.fold_in(keys[6], 71), 0),
        "block_order": jax.random.permutation(keys[2], NBLK).astype(jnp.int32),
        "conv_len": set_ends(jax.random.randint(keys[3], (BATCH,), SEQ // 2, SEQ + 1), jax.random.fold_in(keys[3], 1), SEQ // 2, SEQ).astype(jnp.int32),
        "gate_wq": draw_gate_wq(jax.random.fold_in(keys[6], 71), 0),
        "gate_wk": draw_gate_wk(jax.random.fold_in(keys[6], 71), 0),
    }


masked_value = -1e+30
norm_epsilon = 1e-06

def positions(block_order):
    slot_index = jnp.arange(SEQ, dtype=jnp.int32)
    return block_order[slot_index // BLK] * BLK + slot_index % BLK

def teacher_rows(query_block, key_all, query_pos, key_pos, length):
    row_count = query_block.shape[0]
    kv_heads = key_all.shape[1]
    group_size = query_block.shape[1] // kv_heads
    query_float = query_block.astype(jnp.float32).reshape(row_count, kv_heads, group_size, D_HEAD)
    scores = jnp.einsum('rgqd,kgd->gqrk', query_float, key_all.astype(jnp.float32)) / math.sqrt(D_HEAD)
    allowed = (key_pos[None, :] <= query_pos[:, None]) & (key_pos[None, :] < length)
    masked = jnp.where(allowed, scores, masked_value)
    highest = lax.optimization_barrier(jnp.max(masked, axis=-1, keepdims=True))
    summed = lax.optimization_barrier(jnp.sum(jnp.where(allowed, jnp.exp(masked - highest), 0.0), axis=-1, keepdims=True))
    log_total = highest + jnp.log(summed)
    valid_row = (query_pos < length)[:, None]
    probs = jnp.where(valid_row, jnp.exp(masked - log_total), 0.0)
    pooled = probs.reshape(kv_heads, group_size, row_count // BLK, BLK, NBLK, BLK).max(axis=(3, 5))
    return pooled.reshape(kv_heads * group_size, row_count // BLK, NBLK)

def teacher_single(query_conv, key_conv, block_order, length):
    pos_all = positions(block_order)
    row_block = math.gcd(SEQ, 512)
    count_blocks = SEQ // row_block
    query_split = query_conv.reshape(count_blocks, row_block, HQ, D_HEAD)
    pos_split = pos_all.reshape(count_blocks, row_block)

    def one_block(inputs_pair):
        return teacher_rows(inputs_pair[0], key_conv, inputs_pair[1], pos_all, length)
    pooled = lax.map(one_block, (query_split, pos_split))
    pooled = jnp.transpose(pooled, (1, 0, 2, 3)).reshape(HQ, NBLK, NBLK)
    starts = block_order * BLK
    valid = (starts < length)[None, :, None]
    totals = lax.optimization_barrier(jnp.sum(pooled, axis=-1, keepdims=True))
    return jnp.where(valid, pooled / jnp.where(valid, totals, 1.0), 0.0)

def pool_queries(query_conv):
    shaped = query_conv.reshape(query_conv.shape[0] // BLK, BLK, query_conv.shape[1], query_conv.shape[2])
    return lax.optimization_barrier(jnp.mean(shaped, axis=1, dtype=jnp.float32))

def pool_keys(key_conv):
    shaped = key_conv.reshape(key_conv.shape[0] // BLK, BLK, key_conv.shape[1], key_conv.shape[2])
    largest = lax.optimization_barrier(jnp.max(shaped, axis=1)).astype(jnp.float32)
    smallest = lax.optimization_barrier(jnp.min(shaped, axis=1)).astype(jnp.float32)
    average = lax.optimization_barrier(jnp.mean(shaped, axis=1, dtype=jnp.float32))
    return jnp.concatenate([largest, smallest, average], axis=-1)

def gate_loss(weight_query, weight_key, pooled_query, pooled_key, target_map, query_starts, key_starts, length):
    kv_heads = pooled_key.shape[1]
    group_size = pooled_query.shape[1] // kv_heads
    width_gate = weight_query.shape[1]
    proj_query = jnp.einsum('bhd,de->bhe', pooled_query, weight_query, precision=lax.Precision.HIGHEST)
    proj_key = jnp.einsum('bgd,de->bge', pooled_key, weight_key, precision=lax.Precision.HIGHEST)
    unit_query = proj_query * lax.rsqrt(lax.optimization_barrier(jnp.mean(proj_query * proj_query, axis=-1, keepdims=True)) + norm_epsilon)
    unit_key = proj_key * lax.rsqrt(lax.optimization_barrier(jnp.mean(proj_key * proj_key, axis=-1, keepdims=True)) + norm_epsilon)
    query_count = unit_query.shape[0]
    unit_query = unit_query.reshape(query_count, kv_heads, group_size, width_gate)
    logits = jnp.einsum('igqe,jge->gqij', unit_query, unit_key, precision=lax.Precision.HIGHEST) / math.sqrt(width_gate)
    logits = logits.reshape(kv_heads * group_size, query_count, unit_key.shape[0])
    allowed = (key_starts[None, :] <= query_starts[:, None]) & (key_starts[None, :] < length)
    weights_exp = jnp.where(allowed[None], jnp.exp(logits), 0.0)
    log_norm = jnp.log(lax.optimization_barrier(jnp.sum(weights_exp, axis=-1, keepdims=True)))
    positive = target_map > 0
    entropy_part = jnp.where(positive, target_map * jnp.log(jnp.where(positive, target_map, 1.0)), 0.0)
    divergence = entropy_part - target_map * (logits - log_norm)
    return jnp.sum(divergence)

def reference(queries, key_rows, block_order, conv_len, gate_wq, gate_wk):
    maps_list = []
    pooled_query_list = []
    pooled_key_list = []
    for conv_index in range(BATCH):
        length = conv_len[conv_index]
        maps_list.append(teacher_single(queries[conv_index], key_rows[conv_index], block_order, length))
        pooled_query_list.append(pool_queries(queries[conv_index]))
        pooled_key_list.append(pool_keys(key_rows[conv_index]))
    teacher_map = jnp.stack(maps_list)
    starts = block_order * BLK

    def total_loss(weight_query, weight_key):
        accum = jnp.zeros((), jnp.float32)
        for conv_index in range(BATCH):
            accum = accum + gate_loss(weight_query, weight_key, pooled_query_list[conv_index], pooled_key_list[conv_index], maps_list[conv_index], starts, starts, conv_len[conv_index])
        return accum
    grad_wq, grad_wk = jax.grad(total_loss, argnums=(0, 1))(gate_wq, gate_wk)
    return (teacher_map, grad_wq, grad_wk)
```

```python
import functools
import math

import jax
import jax.numpy as jnp
from jax import lax
from jax.experimental import pallas as pl
from jax.experimental.pallas import tpu as pltpu
from jax.sharding import Mesh
from jax.sharding import PartitionSpec as P

BLK = 64
LANES = 128
MASKED = -1e30
EPS = 1e-06
FAR = 1 << 20
HIGHEST = lax.Precision.HIGHEST

CTX = ("y", "zl")
SCATTER = ("c", "x", "y")
REST = ("zh", "zl")


def dot(a, b, dims):
    return lax.dot_general(
        a, b, (dims, ((), ())), precision=HIGHEST, preferred_element_type=jnp.float32
    )


def kernel(group, blocks, scal, order, q_ref, k_ref, ordv, wq, wk, t_ref, g_ref, m_ref, pk_ref):
    rows = q_ref.shape[0]
    dim = q_ref.shape[1]
    toks = rows // group
    own = toks // BLK
    length = scal[0]
    qb = [scal[1 + i] for i in range(own)]
    tok = lax.rem(lax.broadcasted_iota(jnp.int32, (1, rows), 1), toks)
    pos = lax.rem(tok, BLK)
    part = tok // BLK
    start = jnp.zeros_like(tok)
    for i in range(own):
        start = jnp.where(part == i, qb[i] * BLK, start)
    pos = pos + start
    limit = jnp.minimum(pos, length - 1)
    sub = lax.broadcasted_iota(jnp.int32, (BLK, rows), 0)
    scale = math.log2(math.e) / math.sqrt(dim)
    step = 8
    width = step * BLK
    q = q_ref[...]
    m_ref[...] = jnp.full(m_ref.shape, MASKED, jnp.float32)
    pk_ref[...] = jnp.zeros(pk_ref.shape, jnp.float32)

    def chunk(c, carry):
        high, total = carry
        k = k_ref[pl.ds(pl.multiple_of(c * width, width), width), :]
        s = lax.dot_general(k, q, (((1,), (1,)), ((), ())), preferred_element_type=jnp.float32)
        kf = k.astype(jnp.float32).reshape(step, BLK, dim)
        at = pl.ds(pl.multiple_of(c * step, step), step)
        pk_ref[at, 0:dim] = jnp.max(kf, axis=1)
        pk_ref[at, dim : 2 * dim] = jnp.min(kf, axis=1)
        pk_ref[at, 2 * dim : 3 * dim] = jnp.sum(kf, axis=1) * (1.0 / BLK)
        tiles = []
        tops = []
        for j in range(step):
            ok = sub <= limit - order[c * step + j] * BLK
            tile = jnp.where(ok, s[j * BLK : (j + 1) * BLK] * scale, MASKED)
            tiles.append(tile)
            tops.append(jnp.max(tile, axis=0, keepdims=True))
        top = jnp.concatenate(tops, axis=0)
        m_ref[at, :] = top
        new = jnp.maximum(high, jnp.max(top, axis=0, keepdims=True))
        fresh = jnp.zeros((8, rows), jnp.float32)
        for j in range(step):
            e = jnp.exp2(tiles[j] - new)
            fresh = fresh + jnp.sum(e.reshape(BLK // 8, 8, rows), axis=0)
        total = total * jnp.exp2(high - new) + fresh
        return new, total

    high, total = lax.fori_loop(
        0,
        blocks // step,
        chunk,
        (jnp.full((1, rows), MASKED, jnp.float32), jnp.zeros((8, rows), jnp.float32)),
    )
    log_total = high + jnp.log2(jnp.sum(total, axis=0, keepdims=True))
    depth = jnp.where(pos < length, m_ref[...] - log_total, MASKED)
    depth = jnp.max(jnp.transpose(depth).reshape(group * own, BLK, LANES), axis=1)
    count = t_ref.shape[0]
    pad = count - group * own
    depth = jnp.concatenate([depth, jnp.full((pad, LANES), MASKED, jnp.float32)], axis=0)
    pooled = jnp.exp2(depth)
    row = lax.broadcasted_iota(jnp.int32, (count, 1), 0)
    qstart = jnp.zeros((count, 1), jnp.int32)
    for i in range(own):
        qstart = jnp.where(lax.rem(row, own) == i, qb[i] * BLK, qstart)
    good = (qstart < length) & (row < group * own)
    totals = jnp.sum(pooled, axis=1, keepdims=True)
    target = jnp.where(good, pooled / jnp.where(good, totals, 1.0), 0.0)
    t_ref[...] = target

    pq = jnp.sum(q.astype(jnp.float32).reshape(group * own, BLK, dim), axis=1) * (1.0 / BLK)
    pq = jnp.concatenate([pq, jnp.zeros((pad, dim), jnp.float32)], axis=0)
    pk = pk_ref[...]
    xq = dot(pq, wq[...], ((1,), (0,)))
    xk = dot(pk, wk[...], ((1,), (0,)))
    width_gate = xq.shape[1]
    rq = lax.rsqrt(jnp.mean(xq * xq, axis=1, keepdims=True) + EPS)
    rk = lax.rsqrt(jnp.mean(xk * xk, axis=1, keepdims=True) + EPS)
    uq = xq * rq
    uk = xk * rk
    gate_scale = 1.0 / math.sqrt(width_gate)
    logits = dot(uq, uk, ((1,), (1,))) * gate_scale
    kstart = ordv[...] * BLK
    allowed = (kstart <= qstart) & (kstart < length)
    weights = jnp.where(allowed, jnp.exp(logits), 0.0)
    soft = weights / jnp.sum(weights, axis=1, keepdims=True)
    dl = (soft * jnp.sum(target, axis=1, keepdims=True) - target) * gate_scale
    duq = dot(dl, uk, ((1,), (0,)))
    duk = dot(dl, uq, ((0,), (0,)))
    dxq = rq * (duq - uq * jnp.mean(duq * uq, axis=1, keepdims=True))
    dxk = rk * (duk - uk * jnp.mean(duk * uk, axis=1, keepdims=True))
    g_ref[0:dim, :] = dot(pq, dxq, ((0,), (0,)))
    g_ref[dim : 4 * dim, :] = dot(pk, dxk, ((0,), (0,)))


def body(queries, key_rows, block_order, conv_len, gate_wq, gate_wk):
    toks = queries.shape[1]
    group = queries.shape[2]
    dim = queries.shape[3]
    own = toks // BLK
    blocks = block_order.shape[0]
    ctx = lax.axis_size(CTX)
    keys = lax.all_to_all(
        jnp.broadcast_to(key_rows[0, :, 0, :][None], (ctx, toks, dim)), CTX, 0, 0, tiled=True
    ).reshape(ctx * toks, dim)
    length = lax.dynamic_index_in_dim(conv_len, lax.axis_index(("zh", "c")))
    mine = lax.dynamic_slice_in_dim(block_order, lax.axis_index(CTX) * own, own)
    scal = jnp.concatenate([length, mine])
    q = jnp.transpose(queries[0], (1, 0, 2)).reshape(group * toks, dim)
    ordv = jnp.concatenate([block_order, jnp.full((LANES - blocks,), FAR, jnp.int32)])[None]
    count = 16
    width = gate_wq.shape[1]
    smem = pl.BlockSpec(memory_space=pltpu.SMEM)
    vmem = pl.BlockSpec(memory_space=pltpu.VMEM)
    target, grads = pl.pallas_call(
        functools.partial(kernel, group, blocks),
        out_shape=(
            jax.ShapeDtypeStruct((count, LANES), jnp.float32),
            jax.ShapeDtypeStruct((4 * dim, width), jnp.float32),
        ),
        in_specs=[smem, smem, vmem, vmem, vmem, vmem, vmem],
        out_specs=(vmem, vmem),
        scratch_shapes=[
            pltpu.VMEM((LANES, group * toks), jnp.float32),
            pltpu.VMEM((LANES, 3 * dim), jnp.float32),
        ],
        name="teacher_gate",
    )(scal, block_order, q, keys, ordv, gate_wq, gate_wk)

    parts = lax.axis_size(SCATTER)
    rest = lax.axis_size(REST)
    piece = 4 * dim // parts
    mineg = lax.all_to_all(grads.reshape(parts, piece, width), SCATTER, 0, 0, tiled=True)
    mineg = jnp.sum(mineg, axis=0)
    mineg = lax.all_to_all(
        jnp.broadcast_to(mineg[None], (rest, piece, width)), REST, 0, 0, tiled=True
    )
    mineg = jnp.sum(mineg, axis=0)
    grads = lax.all_to_all(
        jnp.broadcast_to(mineg[None], (parts, piece, width)), SCATTER, 0, 0, tiled=True
    ).reshape(4 * dim, width)
    target = target[: group * own, :blocks].reshape(1, group, own, blocks)
    return target, grads[:dim], grads[dim:]


def solution(mesh):
    fine = Mesh(mesh.devices.reshape(8, 4, 4, 2, 2), ("y", "zl", "x", "zh", "c"))
    rows = P(("zh", "c"), CTX, "x", None)
    return jax.shard_map(
        body,
        mesh=fine,
        in_specs=(rows, rows, P(), P(), P(), P()),
        out_specs=(P(("zh", "c"), "x", CTX, None), P(), P()),
        check_vma=False,
    )
```

```python
import functools
import math

import jax
import jax.numpy as jnp
from jax import lax
from jax.experimental import pallas as pl
from jax.experimental.pallas import tpu as pltpu
from jax.sharding import Mesh
from jax.sharding import PartitionSpec as P

BLK = 64
LANES = 128
COUNT = 16
STEP = 8
MASKED = -1e30
EPS = 1e-06
HIGHEST = lax.Precision.HIGHEST

CTX = ("y", "zl")
SCATTER = ("x", "y")
REST = ("zh", "zl", "c")


def dot(a, b, dims):
    return lax.dot_general(
        a, b, (dims, ((), ())), precision=HIGHEST, preferred_element_type=jnp.float32
    )


def scores(k, q):
    return lax.dot_general(k, q, (((1,), (1,)), ((), ())), preferred_element_type=jnp.float32)


def lane_part(rows, toks):
    tok = lax.rem(lax.broadcasted_iota(jnp.int32, (1, rows), 1), toks)
    return tok // BLK, lax.rem(tok, BLK)


def lane_block(scal, part, own):
    block = jnp.zeros_like(part)
    for i in range(own):
        block = jnp.where(part == i, scal[1 + i], block)
    return block


def tile_sum(s, new, scale):
    e = jnp.exp2((s - new) * scale)
    return jnp.sum(e.reshape(s.shape[0] // 8, 8, s.shape[1]), axis=0)


def first_kernel(group, q_ref, k_ref, wq, high_ref, total_ref, pq_ref, xq_ref):
    rows, dim = q_ref.shape
    toks = rows // group
    own = toks // BLK
    scale = math.log2(math.e) / math.sqrt(dim)
    part, pos = lane_part(rows, toks)
    q = q_ref[...]
    s = scores(k_ref[...], q)
    tile = s[0:BLK]
    for i in range(1, own):
        tile = jnp.where(part == i, s[i * BLK : (i + 1) * BLK], tile)
    tile = jnp.where(lax.broadcasted_iota(jnp.int32, (BLK, rows), 0) <= pos, tile, MASKED)
    high = jnp.max(tile, axis=0, keepdims=True)
    high_ref[...] = high
    total_ref[...] = tile_sum(tile, high, scale)
    pq = jnp.sum(q.astype(jnp.float32).reshape(group * own, BLK, dim), axis=1) * (1.0 / BLK)
    pq = jnp.concatenate([pq, jnp.zeros((COUNT - group * own, dim), jnp.float32)], axis=0)
    pq_ref[...] = pq
    xq_ref[...] = dot(pq, wq[...], ((1,), (0,)))


def kernel(
    group, blocks, scal, order, q_ref, k_ref, ordv, high_ref, total_ref, pq_ref, xq_ref, wk,
    t_ref, g_ref, m_ref, pk_ref, s0, s1,
):
    rows, dim = q_ref.shape
    toks = rows // group
    own = toks // BLK
    length = scal[0]
    scale = math.log2(math.e) / math.sqrt(dim)
    width = STEP * BLK
    part, pos = lane_part(rows, toks)
    block = lane_block(scal, part, own)
    q = q_ref[...]
    diag = high_ref[...]
    m_ref[blocks:, :] = jnp.full((m_ref.shape[0] - blocks, rows), MASKED, jnp.float32)

    def fill(c, s_ref):
        k = k_ref[pl.ds(pl.multiple_of(c * width, width), width), :]
        s = scores(k, q)
        s_ref[...] = s
        tops = []
        for j in range(STEP):
            top = jnp.max(s[j * BLK : (j + 1) * BLK], axis=0, keepdims=True)
            kb = order[c * STEP + j]
            tops.append(jnp.where(block > kb, top, jnp.where(block == kb, diag, MASKED)))
        top = jnp.concatenate(tops, axis=0)
        at = pl.ds(pl.multiple_of(c * STEP, STEP), STEP)
        m_ref[at, :] = top
        kf = k.astype(jnp.float32).reshape(STEP, BLK, dim)
        pk_ref[at, 0:dim] = jnp.max(kf, axis=1)
        pk_ref[at, dim : 2 * dim] = jnp.min(kf, axis=1)
        pk_ref[at, 2 * dim : 3 * dim] = jnp.sum(kf, axis=1) * (1.0 / BLK)
        return jnp.max(top, axis=0, keepdims=True)

    def drain(c, s_ref, top, high, total):
        new = jnp.maximum(high, top)
        total = total * jnp.exp2((high - new) * scale)
        for j in range(STEP):
            fresh = tile_sum(s_ref[j * BLK : (j + 1) * BLK, :], new, scale)
            total = total + jnp.where(block > order[c * STEP + j], fresh, 0.0)
        return new, total

    def pair(p, carry):
        high, total, top = carry
        c = 2 * p
        high, total = drain(c, s0, top, high, total)
        top = fill(c + 1, s1)
        high, total = drain(c + 1, s1, top, high, total)
        top = fill(c + 2, s0)
        return high, total, top

    chunks = blocks // STEP
    top = fill(0, s0)
    high, total, top = lax.fori_loop(0, chunks // 2 - 1, pair, (diag, total_ref[...], top))
    high, total = drain(chunks - 2, s0, top, high, total)
    top = fill(chunks - 1, s1)
    high, total = drain(chunks - 1, s1, top, high, total)

    log_total = jnp.log2(jnp.sum(total, axis=0, keepdims=True))
    depth = jnp.where(pos + block * BLK < length, (m_ref[...] - high) * scale - log_total, MASKED)
    depth = jnp.max(jnp.transpose(depth).reshape(group * own, BLK, LANES), axis=1)[:, :blocks]
    pad = COUNT - group * own
    depth = jnp.concatenate([depth, jnp.full((pad, blocks), MASKED, jnp.float32)], axis=0)
    pooled = jnp.exp2(depth)
    row = lax.broadcasted_iota(jnp.int32, (COUNT, 1), 0)
    qblock = lane_block(scal, lax.rem(row, own), own)
    good = (qblock * BLK < length) & (row < group * own)
    totals = jnp.sum(pooled, axis=1, keepdims=True)
    target = jnp.where(good, pooled / jnp.where(good, totals, 1.0), 0.0)
    t_ref[...] = target

    pq = pq_ref[...]
    xq = xq_ref[...]
    pk = pk_ref[...]
    xk = dot(pk, wk[...], ((1,), (0,)))
    rq = lax.rsqrt(jnp.mean(xq * xq, axis=1, keepdims=True) + EPS)
    rk = lax.rsqrt(jnp.mean(xk * xk, axis=1, keepdims=True) + EPS)
    uq = xq * rq
    uk = xk * rk
    gate_scale = 1.0 / math.sqrt(xq.shape[1])
    logits = dot(uq, uk, ((1,), (1,))) * gate_scale
    kblock = ordv[...]
    allowed = (kblock <= qblock) & (kblock * BLK < length)
    weights = jnp.where(allowed, jnp.exp(logits), 0.0)
    soft = weights / jnp.sum(weights, axis=1, keepdims=True)
    dl = (soft * jnp.sum(target, axis=1, keepdims=True) - target) * gate_scale
    duq = dot(dl, uk, ((1,), (0,)))
    duk = dot(dl, uq, ((0,), (0,)))
    dxq = rq * (duq - uq * jnp.mean(duq * uq, axis=1, keepdims=True))
    dxk = rk * (duk - uk * jnp.mean(duk * uk, axis=1, keepdims=True))
    g_ref[0:dim, :] = dot(pq, dxq, ((0,), (0,)))
    g_ref[dim : 4 * dim, :] = dot(pk, dxk, ((0,), (0,)))


def body(queries, key_rows, block_order, conv_len, gate_wq, gate_wk):
    toks = queries.shape[1]
    group = queries.shape[2]
    dim = queries.shape[3]
    own = toks // BLK
    rows = group * toks
    blocks = block_order.shape[0]
    width = gate_wq.shape[1]
    ctx = lax.axis_size(CTX)
    key_own = key_rows[0, :, 0, :]
    keys = lax.all_to_all(
        jnp.broadcast_to(key_own[None], (ctx, toks, dim)), CTX, 0, 0, tiled=True
    ).reshape(ctx * toks, dim)
    length = lax.dynamic_index_in_dim(conv_len, lax.axis_index(("zh", "c")))
    mine = lax.dynamic_slice_in_dim(block_order, lax.axis_index(CTX) * own, own)
    scal = jnp.concatenate([length, mine])
    q = jnp.transpose(queries[0], (1, 0, 2)).reshape(rows, dim)
    smem = pl.BlockSpec(memory_space=pltpu.SMEM)
    vmem = pl.BlockSpec(memory_space=pltpu.VMEM)

    def f32(*shape):
        return jax.ShapeDtypeStruct(shape, jnp.float32)

    first = pl.pallas_call(
        functools.partial(first_kernel, group),
        out_shape=(f32(1, rows), f32(8, rows), f32(COUNT, dim), f32(COUNT, width)),
        in_specs=[vmem] * 3,
        out_specs=(vmem,) * 4,
        name="own_block",
    )(q, key_own, gate_wq)
    target, grads = pl.pallas_call(
        functools.partial(kernel, group, blocks),
        out_shape=(f32(COUNT, blocks), f32(4 * dim, width)),
        in_specs=[smem, smem] + [vmem] * 8,
        out_specs=(vmem, vmem),
        scratch_shapes=[
            pltpu.VMEM((LANES, rows), jnp.float32),
            pltpu.VMEM((blocks, 3 * dim), jnp.float32),
            pltpu.VMEM((STEP * BLK, rows), jnp.float32),
            pltpu.VMEM((STEP * BLK, rows), jnp.float32),
        ],
        name="teacher_gate",
    )(scal, block_order, q, keys, block_order[None], *first, gate_wk)

    parts = lax.axis_size(SCATTER)
    rest = lax.axis_size(REST)
    piece = 4 * dim // parts
    share = lax.all_to_all(grads.reshape(parts, piece, width), SCATTER, 0, 0, tiled=True)
    share = jnp.sum(share, axis=0)
    share = lax.all_to_all(
        jnp.broadcast_to(share[None], (rest, piece, width)), REST, 0, 0, tiled=True
    )
    share = jnp.sum(share, axis=0)
    grads = lax.all_to_all(
        jnp.broadcast_to(share[None], (parts, piece, width)), SCATTER, 0, 0, tiled=True
    ).reshape(4 * dim, width)
    target = target[: group * own].reshape(1, group, own, blocks)
    return target, grads[:dim], grads[dim:]


def solution(mesh):
    fine = Mesh(mesh.devices.reshape(8, 4, 4, 2, 2), ("y", "zl", "x", "zh", "c"))
    rows = P(("zh", "c"), CTX, "x", None)
    return jax.shard_map(
        body,
        mesh=fine,
        in_specs=(rows, rows, P(), P(), P(), P()),
        out_specs=(P(("zh", "c"), "x", CTX, None), P(), P()),
        check_vma=False,
    )
```

```python
import functools
import math

import jax
import jax.numpy as jnp
from jax import lax
from jax.experimental import pallas as pl
from jax.experimental.pallas import tpu as pltpu
from jax.sharding import Mesh
from jax.sharding import PartitionSpec as P

BLK = 64
LANES = 128
COUNT = 16
STEP = 8
MASKED = -1e30
EPS = 1e-06
HIGHEST = lax.Precision.HIGHEST

CTX = ("y", "zl")
SCATTER = ("x", "y")
REST = ("zh", "zl", "c")


def dot(a, b, dims):
    return lax.dot_general(
        a, b, (dims, ((), ())), precision=HIGHEST, preferred_element_type=jnp.float32
    )


def scores(k, q):
    return lax.dot_general(k, q, (((1,), (1,)), ((), ())), preferred_element_type=jnp.float32)


def lane_part(rows, toks):
    tok = lax.rem(lax.broadcasted_iota(jnp.int32, (1, rows), 1), toks)
    return tok // BLK, lax.rem(tok, BLK)


def lane_block(scal, part, own):
    block = jnp.zeros_like(part)
    for i in range(own):
        block = jnp.where(part == i, scal[1 + i], block)
    return block


def tile_sum(s, new, scale):
    e = jnp.exp2((s.reshape(s.shape[0] // 8, 8, s.shape[1]) - new) * scale)
    return jnp.sum(e, axis=0)


def spread(x, op):
    for shift in (4, 2, 1):
        x = op(x, pltpu.roll(x, shift, 0))
    return x


def fold8(parts, op):
    sub = lax.broadcasted_iota(jnp.int32, parts[0].shape, 0)
    low = sub < 4
    t = []
    for i in range(4):
        a, b = parts[i], parts[i + 4]
        t.append(op(jnp.where(low, a, b), pltpu.roll(jnp.where(low, b, a), 4, 0)))
    for shift in (2, 1):
        half = len(t) // 2
        low = lax.rem(sub, 2 * shift) < shift
        t = [
            jnp.where(
                low,
                op(t[i], pltpu.roll(t[i], 8 - shift, 0)),
                op(t[i + half], pltpu.roll(t[i + half], shift, 0)),
            )
            for i in range(half)
        ]
    return t[0]


def fold_keys(k, reduce, op):
    parts = [
        reduce(k[j * BLK : (j + 1) * BLK].reshape(BLK // 8, 8, k.shape[1]), axis=0)
        for j in range(STEP)
    ]
    return fold8(parts, op)


def first_kernel(group, q_ref, k_ref, wq, high_ref, total_ref, pq_ref, xq_ref):
    rows, dim = q_ref.shape
    toks = rows // group
    own = toks // BLK
    scale = math.log2(math.e) / math.sqrt(dim)
    part, pos = lane_part(rows, toks)
    q = q_ref[...]
    s = scores(k_ref[...], q)
    tile = s[0:BLK]
    for i in range(1, own):
        tile = jnp.where(part == i, s[i * BLK : (i + 1) * BLK], tile)
    tile = jnp.where(lax.broadcasted_iota(jnp.int32, (BLK, rows), 0) <= pos, tile, MASKED)
    high = jnp.max(tile, axis=0, keepdims=True)
    high_ref[...] = high
    total_ref[...] = tile_sum(tile, high, scale)
    pq = jnp.sum(q.astype(jnp.float32).reshape(group * own, BLK, dim), axis=1) * (1.0 / BLK)
    pq = jnp.concatenate([pq, jnp.zeros((COUNT - group * own, dim), jnp.float32)], axis=0)
    pq_ref[...] = pq
    xq_ref[...] = dot(pq, wq[...], ((1,), (0,)))


def scan_keys(own, scal, order, odd, q, k_ref, ordc, diag, high, total, m_ref, pk_ref, s0, s1):
    rows, dim = q.shape
    toks = own * BLK
    scale = math.log2(math.e) / math.sqrt(dim)
    width = STEP * BLK
    part, _ = lane_part(rows, toks)
    block8 = jnp.broadcast_to(lane_block(scal, part, own), (8, rows))
    diag = jnp.broadcast_to(diag, (8, rows))
    col = lax.broadcasted_iota(jnp.int32, (STEP, width), 1) // BLK
    mean = jnp.where(col == lax.broadcasted_iota(jnp.int32, (STEP, width), 0), 1.0 / BLK, 0.0)
    mean = mean.astype(k_ref.dtype)

    def fill(c, s_ref):
        k = k_ref[pl.ds(pl.multiple_of(c * width, width), width), :]
        s = scores(k, q)
        s_ref[...] = s
        tops = [
            jnp.max(s[j * BLK : (j + 1) * BLK].reshape(BLK // 8, 8, rows), axis=0)
            for j in range(STEP)
        ]
        top = fold8(tops, jnp.maximum)
        at = pl.ds(pl.multiple_of((2 * c + odd) * STEP, STEP), STEP)
        kb = jnp.tile(ordc[at, :], (1, rows // LANES))
        top = jnp.where(block8 > kb, top, jnp.where(block8 == kb, diag, MASKED))
        m_ref[at, :] = top
        kf = k.astype(jnp.float32)
        pk_ref[at, 0:dim] = fold_keys(kf, jnp.max, jnp.maximum)
        pk_ref[at, dim : 2 * dim] = fold_keys(kf, jnp.min, jnp.minimum)
        pk_ref[at, 2 * dim : 3 * dim] = lax.dot_general(
            mean, k, (((1,), (0,)), ((), ())), preferred_element_type=jnp.float32
        )
        return spread(top, jnp.maximum)

    def drain(c, s_ref, top, high, total):
        new = jnp.maximum(high, top)
        total = total * jnp.exp2((high - new) * scale)
        for j in range(STEP):
            fresh = tile_sum(s_ref[j * BLK : (j + 1) * BLK, :], new, scale)
            total = total + jnp.where(block8 > order[(2 * c + odd) * STEP + j], fresh, 0.0)
        return new, total

    chunks = k_ref.shape[0] // width
    bufs = (s0, s1)
    top = fill(0, s0)
    for c in range(chunks):
        ahead = fill(c + 1, bufs[(c + 1) % 2]) if c + 1 < chunks else None
        high, total = drain(c, bufs[c % 2], top, high, total)
        top = ahead
    return high, total


def half_kernel(
    own, scal, order, q_ref, k_ref, ordc, high_ref, total_ref,
    high_out, total_out, m_ref, pk_ref, s0, s1,
):
    diag = high_ref[...]
    high = jnp.broadcast_to(diag, high_out.shape)
    m_ref[...] = jnp.full(m_ref.shape, MASKED, jnp.float32)
    pk_ref[...] = jnp.zeros(pk_ref.shape, jnp.float32)
    high, total = scan_keys(
        own, scal, order, scal[1 + own], q_ref[...], k_ref, ordc, diag, high, total_ref[...],
        m_ref, pk_ref, s0, s1,
    )
    high_out[...] = high
    total_out[...] = total


def kernel(
    own, scal, order, q_ref, k_ref, ordv, ordc, diag_ref, high_ref, total_ref, m_in, pk_in,
    pq_ref, xq_ref, wk, t_ref, g_ref, m_ref, pk_ref, s0, s1,
):
    rows, dim = q_ref.shape
    toks = own * BLK
    group = rows // toks
    blocks = order.shape[0]
    length = scal[0]
    odd = scal[1 + own]
    scale = math.log2(math.e) / math.sqrt(dim)
    part, pos = lane_part(rows, toks)
    block = lane_block(scal, part, own)
    m_ref[...] = jnp.full(m_ref.shape, MASKED, jnp.float32)
    high, total = scan_keys(
        own, scal, order, 1 - odd, q_ref[...], k_ref, ordc, diag_ref[...], high_ref[...],
        total_ref[...], m_ref, pk_ref, s0, s1,
    )
    seen = lax.rem(lax.broadcasted_iota(jnp.int32, (blocks, 1), 0) // STEP, 2) == odd
    m_ref[0:blocks, :] = jnp.where(seen, m_in[...], m_ref[0:blocks, :])

    log_total = jnp.log2(jnp.sum(total, axis=0, keepdims=True))
    depth = jnp.where(pos + block * BLK < length, (m_ref[...] - high[0:1]) * scale - log_total, MASKED)
    depth = jnp.max(jnp.transpose(depth).reshape(group * own, BLK, LANES), axis=1)[:, :blocks]
    pad = COUNT - group * own
    depth = jnp.concatenate([depth, jnp.full((pad, blocks), MASKED, jnp.float32)], axis=0)
    pooled = jnp.exp2(depth)
    row = lax.broadcasted_iota(jnp.int32, (COUNT, 1), 0)
    qblock = lane_block(scal, lax.rem(row, own), own)
    good = (qblock * BLK < length) & (row < group * own)
    totals = jnp.sum(pooled, axis=1, keepdims=True)
    target = jnp.where(good, pooled / jnp.where(good, totals, 1.0), 0.0)
    t_ref[...] = target

    pq = pq_ref[...]
    xq = xq_ref[...]
    pk = jnp.where(seen, pk_in[...], pk_ref[...])
    xk = dot(pk, wk[...], ((1,), (0,)))
    rq = lax.rsqrt(jnp.mean(xq * xq, axis=1, keepdims=True) + EPS)
    rk = lax.rsqrt(jnp.mean(xk * xk, axis=1, keepdims=True) + EPS)
    uq = xq * rq
    uk = xk * rk
    gate_scale = 1.0 / math.sqrt(xq.shape[1])
    logits = dot(uq, uk, ((1,), (1,))) * gate_scale
    kblock = ordv[...]
    allowed = (kblock <= qblock) & (kblock * BLK < length)
    weights = jnp.where(allowed, jnp.exp(logits), 0.0)
    soft = weights / jnp.sum(weights, axis=1, keepdims=True)
    dl = (soft * jnp.sum(target, axis=1, keepdims=True) - target) * gate_scale
    duq = dot(dl, uk, ((1,), (0,)))
    duk = dot(dl, uq, ((0,), (0,)))
    dxq = rq * (duq - uq * jnp.mean(duq * uq, axis=1, keepdims=True))
    dxk = rk * (duk - uk * jnp.mean(duk * uk, axis=1, keepdims=True))
    g_ref[0:dim, :] = dot(pq, dxq, ((0,), (0,)))
    g_ref[dim : 4 * dim, :] = dot(pk, dxk, ((0,), (0,)))


def body(queries, key_rows, block_order, conv_len, gate_wq, gate_wk):
    toks = queries.shape[1]
    group = queries.shape[2]
    dim = queries.shape[3]
    own = toks // BLK
    rows = group * toks
    blocks = block_order.shape[0]
    width = gate_wq.shape[1]
    key_own = key_rows[0, :, 0, :]
    ny, nz = lax.axis_size("y"), lax.axis_size("zl")
    odd = lax.rem(lax.axis_index("y"), 2)
    peers = ny // 2 * nz
    same = [[y * nz + z for y in range(h, ny, 2) for z in range(nz)] for h in range(2)]
    near = lax.all_to_all(
        jnp.broadcast_to(key_own[None], (peers, toks, dim)),
        CTX, 0, 0, axis_index_groups=same, tiled=True,
    ).reshape(peers * toks, dim)
    pairs = []
    for y in range(ny):
        for c in range(2):
            other = y + 1 if y % 2 == c else y - 1
            pairs.append((2 * y + c, 2 * (other % ny) + c))
    far = lax.ppermute(near, ("y", "c"), pairs)
    length = lax.dynamic_index_in_dim(conv_len, lax.axis_index(("zh", "c")))
    mine = lax.dynamic_slice_in_dim(block_order, lax.axis_index(CTX) * own, own)
    scal = jnp.concatenate([length, mine, odd[None]])
    q = jnp.transpose(queries[0], (1, 0, 2)).reshape(rows, dim)
    ordc = jnp.broadcast_to(block_order[:, None], (blocks, LANES))
    smem = pl.BlockSpec(memory_space=pltpu.SMEM)
    vmem = pl.BlockSpec(memory_space=pltpu.VMEM)

    def f32(*shape):
        return jax.ShapeDtypeStruct(shape, jnp.float32)

    first = pl.pallas_call(
        functools.partial(first_kernel, group),
        out_shape=(f32(1, rows), f32(8, rows), f32(COUNT, dim), f32(COUNT, width)),
        in_specs=[vmem] * 3,
        out_specs=(vmem,) * 4,
        name="own_block",
    )(q, key_own, gate_wq)
    high, total, pq, xq = first
    buffers = [pltpu.VMEM((STEP * BLK, rows), jnp.float32)] * 2
    after, total, m_half, pk_half = pl.pallas_call(
        functools.partial(half_kernel, own),
        out_shape=(f32(8, rows), f32(8, rows), f32(blocks, rows), f32(blocks, 3 * dim)),
        in_specs=[smem, smem] + [vmem] * 5,
        out_specs=(vmem,) * 4,
        scratch_shapes=buffers,
        name="teacher_near",
    )(scal, block_order, q, pltpu.with_memory_space_constraint(near, pltpu.VMEM), ordc, high, total)
    target, grads = pl.pallas_call(
        functools.partial(kernel, own),
        out_shape=(f32(COUNT, blocks), f32(4 * dim, width)),
        in_specs=[smem, smem] + [vmem] * 12,
        out_specs=(vmem, vmem),
        scratch_shapes=[
            pltpu.VMEM((LANES, rows), jnp.float32),
            pltpu.VMEM((blocks, 3 * dim), jnp.float32),
            *buffers,
        ],
        name="teacher_gate",
    )(
        scal, block_order, q, pltpu.with_memory_space_constraint(far, pltpu.VMEM),
        block_order[None], ordc, high, after, total, m_half, pk_half,
        pq, xq, gate_wk,
    )

    parts = lax.axis_size(SCATTER)
    rest = lax.axis_size(REST)
    piece = 4 * dim // parts
    share = lax.all_to_all(grads.reshape(parts, piece, width), SCATTER, 0, 0, tiled=True)
    share = jnp.sum(share, axis=0)
    share = lax.all_to_all(
        jnp.broadcast_to(share[None], (rest, piece, width)), REST, 0, 0, tiled=True
    )
    share = jnp.sum(share, axis=0)
    grads = lax.all_to_all(
        jnp.broadcast_to(share[None], (parts, piece, width)), SCATTER, 0, 0, tiled=True
    ).reshape(4 * dim, width)
    target = target[: group * own].reshape(1, group, own, blocks)
    return target, grads[:dim], grads[dim:]


def solution(mesh):
    fine = Mesh(mesh.devices.reshape(8, 4, 4, 2, 2), ("y", "zl", "x", "zh", "c"))
    rows = P(("zh", "c"), CTX, "x", None)
    return jax.shard_map(
        body,
        mesh=fine,
        in_specs=(rows, rows, P(), P(), P(), P()),
        out_specs=(P(("zh", "c"), "x", CTX, None), P(), P()),
        check_vma=False,
    )
```

```python
import functools
import math

import jax
import jax.numpy as jnp
from jax import lax
from jax.experimental import pallas as pl
from jax.experimental.pallas import tpu as pltpu
from jax.sharding import Mesh
from jax.sharding import PartitionSpec as P

BLK = 64
LANES = 128
COUNT = 16
STEP = 8
MASKED = -1e30
EPS = 1e-06
HIGHEST = lax.Precision.HIGHEST

CTX = ("y", "zl")
SCATTER = ("x", "y")
REST = ("zh", "zl", "c")


def dot(a, b, dims):
    return lax.dot_general(
        a, b, (dims, ((), ())), precision=HIGHEST, preferred_element_type=jnp.float32
    )


def scores(k, q):
    return lax.dot_general(k, q, (((1,), (1,)), ((), ())), preferred_element_type=jnp.float32)


def lane_part(rows, toks):
    tok = lax.rem(lax.broadcasted_iota(jnp.int32, (1, rows), 1), toks)
    return tok // BLK, lax.rem(tok, BLK)


def lane_block(scal, part, own):
    block = jnp.zeros_like(part)
    for i in range(own):
        block = jnp.where(part == i, scal[1 + i], block)
    return block


def tile_sum(s, new, scale):
    e = jnp.exp2((s.reshape(s.shape[0] // 8, 8, s.shape[1]) - new) * scale)
    return jnp.sum(e, axis=0)


def spread(x, op):
    for shift in (4, 2, 1):
        x = op(x, pltpu.roll(x, shift, 0))
    return x


def fold8(parts, op):
    sub = lax.broadcasted_iota(jnp.int32, parts[0].shape, 0)
    low = sub < 4
    t = []
    for i in range(4):
        a, b = parts[i], parts[i + 4]
        t.append(op(jnp.where(low, a, b), pltpu.roll(jnp.where(low, b, a), 4, 0)))
    for shift in (2, 1):
        half = len(t) // 2
        low = lax.rem(sub, 2 * shift) < shift
        t = [
            jnp.where(
                low,
                op(t[i], pltpu.roll(t[i], 8 - shift, 0)),
                op(t[i + half], pltpu.roll(t[i + half], shift, 0)),
            )
            for i in range(half)
        ]
    return t[0]


def fold_keys(k, reduce, op):
    parts = [
        reduce(k[j * BLK : (j + 1) * BLK].reshape(BLK // 8, 8, k.shape[1]), axis=0)
        for j in range(STEP)
    ]
    return fold8(parts, op)


def first_kernel(group, q_ref, k_ref, wq, high_ref, total_ref, pq_ref, xq_ref):
    rows, dim = q_ref.shape
    toks = rows // group
    own = toks // BLK
    scale = math.log2(math.e) / math.sqrt(dim)
    part, pos = lane_part(rows, toks)
    q = q_ref[...]
    s = scores(k_ref[...], q)
    tile = s[0:BLK]
    for i in range(1, own):
        tile = jnp.where(part == i, s[i * BLK : (i + 1) * BLK], tile)
    tile = jnp.where(lax.broadcasted_iota(jnp.int32, (BLK, rows), 0) <= pos, tile, MASKED)
    high = jnp.max(tile, axis=0, keepdims=True)
    high_ref[...] = high
    total_ref[...] = tile_sum(tile, high, scale)
    pq = jnp.sum(q.astype(jnp.float32).reshape(group * own, BLK, dim), axis=1) * (1.0 / BLK)
    pq = jnp.concatenate([pq, jnp.zeros((COUNT - group * own, dim), jnp.float32)], axis=0)
    pq_ref[...] = pq
    xq_ref[...] = dot(pq, wq[...], ((1,), (0,)))


def scan_keys(own, scal, order, odd, q, k_ref, diag, high, total, m_ref, pk_ref, s0, s1):
    rows, dim = q.shape
    toks = own * BLK
    scale = math.log2(math.e) / math.sqrt(dim)
    width = STEP * BLK
    part, _ = lane_part(rows, toks)
    block8 = jnp.broadcast_to(lane_block(scal, part, own), (8, rows))
    diag = jnp.broadcast_to(diag, (8, rows))
    col = lax.broadcasted_iota(jnp.int32, (STEP, width), 1) // BLK
    mean = jnp.where(col == lax.broadcasted_iota(jnp.int32, (STEP, width), 0), 1.0 / BLK, 0.0)
    mean = mean.astype(k_ref.dtype)

    sub = lax.broadcasted_iota(jnp.int32, (STEP, LANES), 0)

    def fill(c, s_ref):
        k = k_ref[pl.ds(pl.multiple_of(c * width, width), width), :]
        s = scores(k, q)
        s_ref[...] = s
        tops = [
            jnp.max(s[j * BLK : (j + 1) * BLK].reshape(BLK // 8, 8, rows), axis=0)
            for j in range(STEP)
        ]
        top = fold8(tops, jnp.maximum)
        at = pl.ds(pl.multiple_of((2 * c + odd) * STEP, STEP), STEP)
        kb = jnp.zeros((STEP, LANES), jnp.int32)
        for j in range(STEP):
            kb = jnp.where(sub == j, order[(2 * c + odd) * STEP + j], kb)
        kb = jnp.tile(kb, (1, rows // LANES))
        top = jnp.where(block8 > kb, top, jnp.where(block8 == kb, diag, MASKED))
        m_ref[at, :] = top
        kf = k.astype(jnp.float32)
        pk_ref[at, 0:dim] = fold_keys(kf, jnp.max, jnp.maximum)
        pk_ref[at, dim : 2 * dim] = fold_keys(kf, jnp.min, jnp.minimum)
        pk_ref[at, 2 * dim : 3 * dim] = lax.dot_general(
            mean, k, (((1,), (0,)), ((), ())), preferred_element_type=jnp.float32
        )
        return spread(top, jnp.maximum)

    def drain(c, s_ref, top, high, total):
        new = jnp.maximum(high, top)
        total = total * jnp.exp2((high - new) * scale)
        for j in range(STEP):
            fresh = tile_sum(s_ref[j * BLK : (j + 1) * BLK, :], new, scale)
            total = total + jnp.where(block8 > order[(2 * c + odd) * STEP + j], fresh, 0.0)
        return new, total

    chunks = k_ref.shape[0] // width
    bufs = (s0, s1)
    top = fill(0, s0)
    for c in range(chunks):
        ahead = fill(c + 1, bufs[(c + 1) % 2]) if c + 1 < chunks else None
        high, total = drain(c, bufs[c % 2], top, high, total)
        top = ahead
    return high, total


def half_kernel(
    own, scal, order, q_ref, k_ref, high_ref, total_ref,
    high_out, total_out, m_ref, pk_ref, s0, s1,
):
    diag = high_ref[...]
    high = jnp.broadcast_to(diag, high_out.shape)
    m_ref[...] = jnp.full(m_ref.shape, MASKED, jnp.float32)
    pk_ref[...] = jnp.zeros(pk_ref.shape, jnp.float32)
    high, total = scan_keys(
        own, scal, order, scal[1 + own], q_ref[...], k_ref, diag, high, total_ref[...],
        m_ref, pk_ref, s0, s1,
    )
    high_out[...] = high
    total_out[...] = total


def kernel(
    own, scal, order, q_ref, k_ref, ordv, diag_ref, high_ref, total_ref, m_in, pk_in,
    pq_ref, xq_ref, wk, t_ref, g_ref, m_ref, pk_ref, s0, s1,
):
    rows, dim = q_ref.shape
    toks = own * BLK
    group = rows // toks
    blocks = order.shape[0]
    length = scal[0]
    odd = scal[1 + own]
    scale = math.log2(math.e) / math.sqrt(dim)
    part, pos = lane_part(rows, toks)
    block = lane_block(scal, part, own)
    m_ref[...] = jnp.full(m_ref.shape, MASKED, jnp.float32)
    high, total = scan_keys(
        own, scal, order, 1 - odd, q_ref[...], k_ref, diag_ref[...], high_ref[...],
        total_ref[...], m_ref, pk_ref, s0, s1,
    )
    seen = lax.rem(lax.broadcasted_iota(jnp.int32, (blocks, 1), 0) // STEP, 2) == odd
    m_ref[0:blocks, :] = jnp.where(seen, m_in[...], m_ref[0:blocks, :])

    log_total = jnp.log2(jnp.sum(total, axis=0, keepdims=True))
    depth = jnp.where(pos + block * BLK < length, (m_ref[...] - high[0:1]) * scale - log_total, MASKED)
    depth = jnp.max(jnp.transpose(depth).reshape(group * own, BLK, LANES), axis=1)[:, :blocks]
    pad = COUNT - group * own
    depth = jnp.concatenate([depth, jnp.full((pad, blocks), MASKED, jnp.float32)], axis=0)
    pooled = jnp.exp2(depth)
    row = lax.broadcasted_iota(jnp.int32, (COUNT, 1), 0)
    qblock = lane_block(scal, lax.rem(row, own), own)
    good = (qblock * BLK < length) & (row < group * own)
    totals = jnp.sum(pooled, axis=1, keepdims=True)
    target = jnp.where(good, pooled / jnp.where(good, totals, 1.0), 0.0)
    for h in range(group):
        t_ref[0, h] = target[own * h : own * (h + 1)]

    pq = pq_ref[...]
    xq = xq_ref[...]
    pk = jnp.where(seen, pk_in[...], pk_ref[...])
    xk = dot(pk, wk[...], ((1,), (0,)))
    rq = lax.rsqrt(jnp.mean(xq * xq, axis=1, keepdims=True) + EPS)
    rk = lax.rsqrt(jnp.mean(xk * xk, axis=1, keepdims=True) + EPS)
    uq = xq * rq
    uk = xk * rk
    gate_scale = 1.0 / math.sqrt(xq.shape[1])
    logits = dot(uq, uk, ((1,), (1,))) * gate_scale
    kblock = ordv[...]
    allowed = (kblock <= qblock) & (kblock * BLK < length)
    weights = jnp.where(allowed, jnp.exp(logits), 0.0)
    soft = weights / jnp.sum(weights, axis=1, keepdims=True)
    dl = (soft * jnp.sum(target, axis=1, keepdims=True) - target) * gate_scale
    duq = dot(dl, uk, ((1,), (0,)))
    duk = dot(dl, uq, ((0,), (0,)))
    dxq = rq * (duq - uq * jnp.mean(duq * uq, axis=1, keepdims=True))
    dxk = rk * (duk - uk * jnp.mean(duk * uk, axis=1, keepdims=True))
    g_ref[0:dim, :] = dot(pq, dxq, ((0,), (0,)))
    g_ref[dim : 4 * dim, :] = dot(pk, dxk, ((0,), (0,)))


def split_kernel(g_ref, q_ref, k_ref, sem):
    rows = q_ref.shape[0]
    copies = [
        pltpu.make_async_copy(g_ref.at[pl.ds(0, rows)], q_ref, sem.at[0]),
        pltpu.make_async_copy(g_ref.at[pl.ds(rows, k_ref.shape[0])], k_ref, sem.at[1]),
    ]
    for copy in copies:
        copy.start()
    for copy in copies:
        copy.wait()


def body(queries, key_rows, block_order, conv_len, gate_wq, gate_wk):
    toks = queries.shape[1]
    group = queries.shape[2]
    dim = queries.shape[3]
    own = toks // BLK
    rows = group * toks
    blocks = block_order.shape[0]
    width = gate_wq.shape[1]
    key_own = key_rows[0, :, 0, :]
    ny, nz = lax.axis_size("y"), lax.axis_size("zl")
    odd = lax.rem(lax.axis_index("y"), 2)
    peers = ny // 2 * nz
    same = [[y * nz + z for y in range(h, ny, 2) for z in range(nz)] for h in range(2)]
    near = lax.all_to_all(
        jnp.broadcast_to(key_own[None], (peers, toks, dim)),
        CTX, 0, 0, axis_index_groups=same, tiled=True,
    ).reshape(peers * toks, dim)
    length = lax.dynamic_index_in_dim(conv_len, lax.axis_index(("zh", "c")))
    mine = lax.dynamic_slice_in_dim(block_order, lax.axis_index(CTX) * own, own)
    scal = jnp.concatenate([length, mine, odd[None]])
    q = jnp.transpose(queries[0], (1, 0, 2)).reshape(rows, dim)
    smem = pl.BlockSpec(memory_space=pltpu.SMEM)
    vmem = pl.BlockSpec(memory_space=pltpu.VMEM)

    def f32(*shape):
        return jax.ShapeDtypeStruct(shape, jnp.float32)

    first = pl.pallas_call(
        functools.partial(first_kernel, group),
        out_shape=(f32(1, rows), f32(8, rows), f32(COUNT, dim), f32(COUNT, width)),
        in_specs=[vmem] * 3,
        out_specs=(vmem,) * 4,
        name="own_block",
    )(q, key_own, gate_wq)
    near, scal, first = lax.optimization_barrier((near, scal, first))
    high, total, pq, xq = first
    pairs = []
    for y in range(ny):
        for c in range(2):
            other = y + 1 if y % 2 == c else y - 1
            pairs.append((2 * y + c, 2 * (other % ny) + c))
    far = lax.ppermute(near, ("y", "c"), pairs)
    buffers = [pltpu.VMEM((STEP * BLK, rows), jnp.float32)] * 2
    after, total, m_half, pk_half = pl.pallas_call(
        functools.partial(half_kernel, own),
        out_shape=(f32(8, rows), f32(8, rows), f32(blocks, rows), f32(blocks, 3 * dim)),
        in_specs=[smem, smem] + [vmem] * 4,
        out_specs=(vmem,) * 4,
        scratch_shapes=buffers,
        name="teacher_near",
    )(scal, block_order, q, pltpu.with_memory_space_constraint(near, pltpu.VMEM), high, total)
    target, grads = pl.pallas_call(
        functools.partial(kernel, own),
        out_shape=(f32(1, group, own, blocks), f32(4 * dim, width)),
        in_specs=[smem, smem] + [vmem] * 11,
        out_specs=(vmem, vmem),
        scratch_shapes=[
            pltpu.VMEM((LANES, rows), jnp.float32),
            pltpu.VMEM((blocks, 3 * dim), jnp.float32),
            *buffers,
        ],
        name="teacher_gate",
    )(
        scal, block_order, q, pltpu.with_memory_space_constraint(far, pltpu.VMEM),
        block_order[None], high, after, total, m_half, pk_half,
        pq, xq, gate_wk,
    )

    parts = lax.axis_size(SCATTER)
    rest = lax.axis_size(REST)
    piece = 4 * dim // parts
    share = lax.all_to_all(grads.reshape(parts, piece, width), SCATTER, 0, 0, tiled=True)
    share = jnp.sum(share, axis=0)
    share = lax.all_to_all(
        jnp.broadcast_to(share[None], (rest, piece, width)), REST, 0, 0, tiled=True
    )
    share = jnp.sum(share, axis=0)
    grads = lax.all_to_all(
        jnp.broadcast_to(share[None], (parts, piece, width)), SCATTER, 0, 0, tiled=True
    ).reshape(4 * dim, width)
    anywhere = pl.BlockSpec(memory_space=pl.ANY)
    grad_wq, grad_wk = pl.pallas_call(
        split_kernel,
        out_shape=(f32(dim, width), f32(3 * dim, width)),
        in_specs=[vmem],
        out_specs=(anywhere, anywhere),
        scratch_shapes=[pltpu.SemaphoreType.DMA((2,))],
        name="split_grads",
    )(pltpu.with_memory_space_constraint(grads, pltpu.VMEM))
    return target, grad_wq, grad_wk


def solution(mesh):
    fine = Mesh(mesh.devices.reshape(8, 4, 4, 2, 2), ("y", "zl", "x", "zh", "c"))
    rows = P(("zh", "c"), CTX, "x", None)
    return jax.shard_map(
        body,
        mesh=fine,
        in_specs=(rows, rows, P(), P(), P(), P()),
        out_specs=(P(("zh", "c"), "x", CTX, None), P(), P()),
        check_vma=False,
    )
```

```python
import functools
import math

import jax
import jax.numpy as jnp
from jax import lax
from jax.experimental import pallas as pl
from jax.experimental.pallas import tpu as pltpu
from jax.sharding import Mesh
from jax.sharding import PartitionSpec as P

BLK = 64
LANES = 128
COUNT = 16
STEP = 8
MASKED = -1e30
EPS = 1e-06
HIGHEST = lax.Precision.HIGHEST

CTX = ("y", "zl")
SCATTER = ("x", "y")
REST = ("zh", "zl", "c")


def dot(a, b, dims):
    return lax.dot_general(
        a, b, (dims, ((), ())), precision=HIGHEST, preferred_element_type=jnp.float32
    )


def scores(k, q):
    return lax.dot_general(k, q, (((1,), (1,)), ((), ())), preferred_element_type=jnp.float32)


def lane_part(rows, toks):
    tok = lax.rem(lax.broadcasted_iota(jnp.int32, (1, rows), 1), toks)
    return tok // BLK, lax.rem(tok, BLK)


def lane_block(scal, part, own):
    block = jnp.zeros_like(part)
    for i in range(own):
        block = jnp.where(part == i, scal[1 + i], block)
    return block


def tile_sum(s, new, scale):
    e = jnp.exp2((s.reshape(s.shape[0] // 8, 8, s.shape[1]) - new) * scale)
    return jnp.sum(e, axis=0)


def spread(x, op):
    for shift in (4, 2, 1):
        x = op(x, pltpu.roll(x, shift, 0))
    return x


def fold8(parts, op):
    sub = lax.broadcasted_iota(jnp.int32, parts[0].shape, 0)
    low = sub < 4
    t = []
    for i in range(4):
        a, b = parts[i], parts[i + 4]
        t.append(op(jnp.where(low, a, b), pltpu.roll(jnp.where(low, b, a), 4, 0)))
    for shift in (2, 1):
        half = len(t) // 2
        low = lax.rem(sub, 2 * shift) < shift
        t = [
            jnp.where(
                low,
                op(t[i], pltpu.roll(t[i], 8 - shift, 0)),
                op(t[i + half], pltpu.roll(t[i + half], shift, 0)),
            )
            for i in range(half)
        ]
    return t[0]


def fold_keys(k, reduce, op):
    parts = [
        reduce(k[j * BLK : (j + 1) * BLK].reshape(BLK // 8, 8, k.shape[1]), axis=0)
        for j in range(STEP)
    ]
    return fold8(parts, op)


def first_kernel(group, q_ref, k_ref, ord_ref, wq, high_ref, total_ref, ord_out, pq_ref, xq_ref):
    rows, dim = q_ref.shape
    toks = rows // group
    own = toks // BLK
    scale = math.log2(math.e) / math.sqrt(dim)
    part, pos = lane_part(rows, toks)
    q = q_ref[...]
    s = scores(k_ref[...], q)
    tile = s[0:BLK]
    for i in range(1, own):
        tile = jnp.where(part == i, s[i * BLK : (i + 1) * BLK], tile)
    tile = jnp.where(lax.broadcasted_iota(jnp.int32, (BLK, rows), 0) <= pos, tile, MASKED)
    high = jnp.max(tile, axis=0, keepdims=True)
    high_ref[...] = high
    total_ref[...] = tile_sum(tile, high, scale)
    pq = jnp.sum(q.astype(jnp.float32).reshape(group * own, BLK, dim), axis=1) * (1.0 / BLK)
    pq = jnp.concatenate([pq, jnp.zeros((COUNT - group * own, dim), jnp.float32)], axis=0)
    pq_ref[...] = pq
    ord_out[...] = ord_ref[...]
    xq_ref[...] = dot(pq, wq[...], ((1,), (0,)))


def scan_keys(own, scal, order, odd, q, k_ref, diag, high, total, m_ref, pk_ref, s0, s1, before_last=None):
    rows, dim = q.shape
    toks = own * BLK
    scale = math.log2(math.e) / math.sqrt(dim)
    width = STEP * BLK
    part, _ = lane_part(rows, toks)
    block8 = jnp.broadcast_to(lane_block(scal, part, own), (8, rows))
    diag = jnp.broadcast_to(diag, (8, rows))
    col = lax.broadcasted_iota(jnp.int32, (STEP, width), 1) // BLK
    mean = jnp.where(col == lax.broadcasted_iota(jnp.int32, (STEP, width), 0), 1.0 / BLK, 0.0)
    mean = mean.astype(k_ref.dtype)

    sub = lax.broadcasted_iota(jnp.int32, (STEP, LANES), 0)

    def fill(c, s_ref):
        k = k_ref[pl.ds(pl.multiple_of(c * width, width), width), :]
        s = scores(k, q)
        s_ref[...] = s
        tops = [
            jnp.max(s[j * BLK : (j + 1) * BLK].reshape(BLK // 8, 8, rows), axis=0)
            for j in range(STEP)
        ]
        top = fold8(tops, jnp.maximum)
        at = pl.ds(pl.multiple_of((2 * c + odd) * STEP, STEP), STEP)
        kb = jnp.zeros((STEP, LANES), jnp.int32)
        for j in range(STEP):
            kb = jnp.where(sub == j, order[(2 * c + odd) * STEP + j], kb)
        kb = jnp.tile(kb, (1, rows // LANES))
        top = jnp.where(block8 > kb, top, jnp.where(block8 == kb, diag, MASKED))
        m_ref[at, :] = top
        kf = k.astype(jnp.float32)
        pk_ref[at, 0:dim] = fold_keys(kf, jnp.max, jnp.maximum)
        pk_ref[at, dim : 2 * dim] = fold_keys(kf, jnp.min, jnp.minimum)
        pk_ref[at, 2 * dim : 3 * dim] = lax.dot_general(
            mean, k, (((1,), (0,)), ((), ())), preferred_element_type=jnp.float32
        )
        return spread(top, jnp.maximum)

    def drain(c, s_ref, top, high, total):
        new = jnp.maximum(high, top)
        total = total * jnp.exp2((high - new) * scale)
        for j in range(STEP):
            fresh = tile_sum(s_ref[j * BLK : (j + 1) * BLK, :], new, scale)
            total = total + jnp.where(block8 > order[(2 * c + odd) * STEP + j], fresh, 0.0)
        return new, total

    chunks = k_ref.shape[0] // width
    bufs = (s0, s1)
    top = fill(0, s0)
    for c in range(chunks):
        ahead = fill(c + 1, bufs[(c + 1) % 2]) if c + 1 < chunks else None
        if c + 1 == chunks and before_last is not None:
            before_last()
        high, total = drain(c, bufs[c % 2], top, high, total)
        top = ahead
    return high, total


def half_kernel(
    own, scal, order, q_ref, k_ref, high_ref, total_ref,
    high_out, total_out, m_ref, pk_ref, s0, s1,
):
    diag = high_ref[...]
    high = jnp.broadcast_to(diag, high_out.shape)
    m_ref[...] = jnp.full(m_ref.shape, MASKED, jnp.float32)
    pk_ref[...] = jnp.zeros(pk_ref.shape, jnp.float32)
    high, total = scan_keys(
        own, scal, order, scal[1 + own], q_ref[...], k_ref, diag, high, total_ref[...],
        m_ref, pk_ref, s0, s1,
    )
    high_out[...] = high
    total_out[...] = total


def kernel(
    own, scal, order, q_ref, k_ref, ordv, diag_ref, high_ref, total_ref, m_in, pk_in,
    pq_ref, xq_ref, wk, t_ref, g_ref, m_ref, pk_ref, s0, s1,
):
    rows, dim = q_ref.shape
    toks = own * BLK
    group = rows // toks
    blocks = order.shape[0]
    length = scal[0]
    odd = scal[1 + own]
    scale = math.log2(math.e) / math.sqrt(dim)
    part, pos = lane_part(rows, toks)
    block = lane_block(scal, part, own)
    m_ref[...] = jnp.full(m_ref.shape, MASKED, jnp.float32)
    seen = lax.rem(lax.broadcasted_iota(jnp.int32, (blocks, 1), 0) // STEP, 2) == odd
    row = lax.broadcasted_iota(jnp.int32, (COUNT, 1), 0)
    qblock = lane_block(scal, lax.rem(row, own), own)
    gate = {}

    def gate_forward():
        pq = pq_ref[...]
        xq = xq_ref[...]
        pk = jnp.where(seen, pk_in[...], pk_ref[...])
        xk = dot(pk, wk[...], ((1,), (0,)))
        rq = lax.rsqrt(jnp.mean(xq * xq, axis=1, keepdims=True) + EPS)
        rk = lax.rsqrt(jnp.mean(xk * xk, axis=1, keepdims=True) + EPS)
        uq = xq * rq
        uk = xk * rk
        gate_scale = 1.0 / math.sqrt(xq.shape[1])
        logits = dot(uq, uk, ((1,), (1,))) * gate_scale
        kblock = ordv[...]
        allowed = (kblock <= qblock) & (kblock * BLK < length)
        weights = jnp.where(allowed, jnp.exp(logits), 0.0)
        soft = weights / jnp.sum(weights, axis=1, keepdims=True)
        gate.update(pq=pq, pkt=jnp.transpose(pk), uq=uq, uk=uk, rq=rq, rk=rk, soft=soft)
        gate.update(scale=gate_scale)

    high, total = scan_keys(
        own, scal, order, 1 - odd, q_ref[...], k_ref, diag_ref[...], high_ref[...],
        total_ref[...], m_ref, pk_ref, s0, s1, gate_forward,
    )
    m_ref[0:blocks, :] = jnp.where(seen, m_in[...], m_ref[0:blocks, :])

    log_total = jnp.log2(jnp.sum(total, axis=0, keepdims=True))
    depth = jnp.where(pos + block * BLK < length, (m_ref[...] - high[0:1]) * scale - log_total, MASKED)
    depth = jnp.max(jnp.transpose(depth).reshape(group * own, BLK, LANES), axis=1)[:, :blocks]
    pad = COUNT - group * own
    depth = jnp.concatenate([depth, jnp.full((pad, blocks), MASKED, jnp.float32)], axis=0)
    pooled = jnp.exp2(depth)
    good = (qblock * BLK < length) & (row < group * own)
    totals = jnp.sum(pooled, axis=1, keepdims=True)
    target = jnp.where(good, pooled / jnp.where(good, totals, 1.0), 0.0)
    for h in range(group):
        t_ref[0, h] = target[own * h : own * (h + 1)]

    dl = (gate["soft"] * jnp.sum(target, axis=1, keepdims=True) - target) * gate["scale"]
    uq, uk, rq, rk = gate["uq"], gate["uk"], gate["rq"], gate["rk"]
    duq = dot(dl, uk, ((1,), (0,)))
    duk = dot(dl, uq, ((0,), (0,)))
    dxq = rq * (duq - uq * jnp.mean(duq * uq, axis=1, keepdims=True))
    dxk = rk * (duk - uk * jnp.mean(duk * uk, axis=1, keepdims=True))
    g_ref[0:dim, :] = dot(gate["pq"], dxq, ((0,), (0,)))
    g_ref[dim : 4 * dim, :] = dot(gate["pkt"], dxk, ((1,), (0,)))


def split_kernel(g_ref, q_ref, k_ref, sem):
    rows = q_ref.shape[0]
    copies = [
        pltpu.make_async_copy(g_ref.at[pl.ds(0, rows)], q_ref, sem.at[0]),
        pltpu.make_async_copy(g_ref.at[pl.ds(rows, k_ref.shape[0])], k_ref, sem.at[1]),
    ]
    for copy in copies:
        copy.start()
    for copy in copies:
        copy.wait()


def repeat_kernel(x_ref, o_ref, sem):
    copies = [
        pltpu.make_async_copy(x_ref, o_ref.at[i], sem.at[i]) for i in range(o_ref.shape[0])
    ]
    for copy in copies:
        copy.start()
    for copy in copies:
        copy.wait()


def body(queries, key_rows, block_order, conv_len, gate_wq, gate_wk):
    toks = queries.shape[1]
    group = queries.shape[2]
    dim = queries.shape[3]
    own = toks // BLK
    rows = group * toks
    blocks = block_order.shape[0]
    width = gate_wq.shape[1]
    key_own = key_rows[0, :, 0, :]
    ny, nz = lax.axis_size("y"), lax.axis_size("zl")
    odd = lax.rem(lax.axis_index("y"), 2)
    peers = ny // 2 * nz
    same = [[y * nz + z for y in range(h, ny, 2) for z in range(nz)] for h in range(2)]
    anywhere = pl.BlockSpec(memory_space=pl.ANY)
    repeated = pl.pallas_call(
        repeat_kernel,
        out_shape=jax.ShapeDtypeStruct((peers, toks, dim), key_own.dtype),
        in_specs=[anywhere],
        out_specs=anywhere,
        scratch_shapes=[pltpu.SemaphoreType.DMA((peers,))],
        name="repeat_keys",
    )(key_own)
    near = lax.all_to_all(
        repeated, CTX, 0, 0, axis_index_groups=same, tiled=True,
    ).reshape(peers * toks, dim)
    length = lax.dynamic_index_in_dim(conv_len, lax.axis_index(("zh", "c")))
    mine = lax.dynamic_slice_in_dim(block_order, lax.axis_index(CTX) * own, own)
    scal = jnp.concatenate([length, mine, odd[None]])
    q = jnp.transpose(queries[0], (1, 0, 2)).reshape(rows, dim)
    smem = pl.BlockSpec(memory_space=pltpu.SMEM)
    vmem = pl.BlockSpec(memory_space=pltpu.VMEM)

    def f32(*shape):
        return jax.ShapeDtypeStruct(shape, jnp.float32)

    def near_core(*shape):
        return pltpu.VMEM(shape, jnp.float32)

    def pinned(*arrays):
        return [pltpu.with_memory_space_constraint(x, pltpu.VMEM) for x in arrays]

    first = pl.pallas_call(
        functools.partial(first_kernel, group),
        out_shape=(
            near_core(1, rows), near_core(8, rows), pltpu.VMEM((1, blocks), jnp.int32),
            near_core(COUNT, dim), near_core(COUNT, width),
        ),
        in_specs=[vmem] * 4,
        out_specs=(vmem,) * 5,
        name="own_block",
    )(q, key_own, block_order[None], gate_wq)
    near, scal, first = lax.optimization_barrier((near, scal, first))
    high, total, ordv, pq, xq = first
    pairs = []
    for y in range(ny):
        for c in range(2):
            other = y + 1 if y % 2 == c else y - 1
            pairs.append((2 * y + c, 2 * (other % ny) + c))
    far = lax.ppermute(near, ("y", "c"), pairs)
    buffers = [pltpu.VMEM((STEP * BLK, rows), jnp.float32)] * 2
    after, total, m_half, pk_half = pl.pallas_call(
        functools.partial(half_kernel, own),
        out_shape=(
            near_core(8, rows), near_core(8, rows), near_core(blocks, rows), near_core(blocks, 3 * dim)
        ),
        in_specs=[smem, smem] + [vmem] * 4,
        out_specs=(vmem,) * 4,
        scratch_shapes=buffers,
        name="teacher_near",
    )(scal, block_order, *pinned(q, near, high, total))
    target, grads = pl.pallas_call(
        functools.partial(kernel, own),
        out_shape=(f32(1, group, own, blocks), near_core(4 * dim, width)),
        in_specs=[smem, smem] + [vmem] * 11,
        out_specs=(vmem, vmem),
        scratch_shapes=[
            pltpu.VMEM((LANES, rows), jnp.float32),
            pltpu.VMEM((blocks, 3 * dim), jnp.float32),
            *buffers,
        ],
        name="teacher_gate",
    )(
        scal, block_order,
        *pinned(
            q, far, ordv, high, after, total, m_half, pk_half, pq, xq, gate_wk
        ),
    )

    parts = lax.axis_size(SCATTER)
    rest = lax.axis_size(REST)
    piece = 4 * dim // parts
    share = lax.all_to_all(grads.reshape(parts, piece, width), SCATTER, 0, 0, tiled=True)
    share = jnp.sum(share, axis=0)
    share = lax.all_to_all(
        jnp.broadcast_to(share[None], (rest, piece, width)), REST, 0, 0, tiled=True
    )
    share = jnp.sum(share, axis=0)
    grads = lax.all_to_all(
        jnp.broadcast_to(share[None], (parts, piece, width)), SCATTER, 0, 0, tiled=True
    ).reshape(4 * dim, width)
    grad_wq, grad_wk = pl.pallas_call(
        split_kernel,
        out_shape=(f32(dim, width), f32(3 * dim, width)),
        in_specs=[vmem],
        out_specs=(anywhere, anywhere),
        scratch_shapes=[pltpu.SemaphoreType.DMA((2,))],
        name="split_grads",
    )(*pinned(grads))
    return target, grad_wq, grad_wk


def solution(mesh):
    fine = Mesh(mesh.devices.reshape(8, 4, 4, 2, 2), ("y", "zl", "x", "zh", "c"))
    rows = P(("zh", "c"), CTX, "x", None)
    return jax.shard_map(
        body,
        mesh=fine,
        in_specs=(rows, rows, P(), P(), P(), P()),
        out_specs=(P(("zh", "c"), "x", CTX, None), P(), P()),
        check_vma=False,
    )
```

```python
import functools
import math

import jax
import jax.numpy as jnp
from jax import lax
from jax.experimental import pallas as pl
from jax.experimental.pallas import tpu as pltpu
from jax.sharding import Mesh
from jax.sharding import PartitionSpec as P

BLK = 64
LANES = 128
COUNT = 16
STEP = 8
MASKED = -1e30
EPS = 1e-06
HIGHEST = lax.Precision.HIGHEST

CTX = ("y", "zl")
SCATTER = ("x", "y")
REST = ("zh", "zl", "c")


def dot(a, b, dims):
    return lax.dot_general(
        a, b, (dims, ((), ())), precision=HIGHEST, preferred_element_type=jnp.float32
    )


def scores(k, q):
    return lax.dot_general(k, q, (((1,), (1,)), ((), ())), preferred_element_type=jnp.float32)


def lane_part(rows, toks):
    tok = lax.rem(lax.broadcasted_iota(jnp.int32, (1, rows), 1), toks)
    return tok // BLK, lax.rem(tok, BLK)


def lane_block(scal, part, own):
    block = jnp.zeros_like(part)
    for i in range(own):
        block = jnp.where(part == i, scal[1 + i], block)
    return block


def tile_sum(s, new, scale):
    e = jnp.exp2((s.reshape(s.shape[0] // 8, 8, s.shape[1]) - new) * scale)
    return jnp.sum(e, axis=0)


def spread(x, op):
    for shift in (4, 2, 1):
        x = op(x, pltpu.roll(x, shift, 0))
    return x


def fold8(parts, op):
    sub = lax.broadcasted_iota(jnp.int32, parts[0].shape, 0)
    low = sub < 4
    t = []
    for i in range(4):
        a, b = parts[i], parts[i + 4]
        t.append(op(jnp.where(low, a, b), pltpu.roll(jnp.where(low, b, a), 4, 0)))
    for shift in (2, 1):
        half = len(t) // 2
        low = lax.rem(sub, 2 * shift) < shift
        t = [
            jnp.where(
                low,
                op(t[i], pltpu.roll(t[i], 8 - shift, 0)),
                op(t[i + half], pltpu.roll(t[i + half], shift, 0)),
            )
            for i in range(half)
        ]
    return t[0]


def fold_keys(k, reduce, op):
    parts = [
        reduce(k[j * BLK : (j + 1) * BLK].reshape(BLK // 8, 8, k.shape[1]), axis=0)
        for j in range(STEP)
    ]
    return fold8(parts, op)


def first_kernel(group, q_ref, k_ref, ord_ref, wq, high_ref, total_ref, ord_out, pq_ref, xq_ref):
    rows, dim = q_ref.shape
    toks = rows // group
    own = toks // BLK
    scale = math.log2(math.e) / math.sqrt(dim)
    part, pos = lane_part(rows, toks)
    q = q_ref[...]
    s = scores(k_ref[...], q)
    tile = s[0:BLK]
    for i in range(1, own):
        tile = jnp.where(part == i, s[i * BLK : (i + 1) * BLK], tile)
    tile = jnp.where(lax.broadcasted_iota(jnp.int32, (BLK, rows), 0) <= pos, tile, MASKED)
    high = jnp.max(tile, axis=0, keepdims=True)
    high_ref[...] = high
    total_ref[...] = tile_sum(tile, high, scale)
    pq = jnp.sum(q.astype(jnp.float32).reshape(group * own, BLK, dim), axis=1) * (1.0 / BLK)
    pq = jnp.concatenate([pq, jnp.zeros((COUNT - group * own, dim), jnp.float32)], axis=0)
    pq_ref[...] = pq
    ord_out[...] = ord_ref[...]
    xq_ref[...] = dot(pq, wq[...], ((1,), (0,)))


def scan_keys(own, scal, order, odd, q, k_ref, diag, high, total, m_ref, pk_ref, s0, s1, before_last=None):
    rows, dim = q.shape
    toks = own * BLK
    scale = math.log2(math.e) / math.sqrt(dim)
    width = STEP * BLK
    part, _ = lane_part(rows, toks)
    block8 = jnp.broadcast_to(lane_block(scal, part, own), (8, rows))
    diag = jnp.broadcast_to(diag, (8, rows))
    col = lax.broadcasted_iota(jnp.int32, (STEP, width), 1) // BLK
    mean = jnp.where(col == lax.broadcasted_iota(jnp.int32, (STEP, width), 0), 1.0 / BLK, 0.0)
    mean = mean.astype(k_ref.dtype)

    sub = lax.broadcasted_iota(jnp.int32, (STEP, LANES), 0)

    def fill(c, s_ref):
        k = k_ref[pl.ds(pl.multiple_of(c * width, width), width), :]
        s = scores(k, q)
        s_ref[...] = s
        tops = [
            jnp.max(s[j * BLK : (j + 1) * BLK].reshape(BLK // 8, 8, rows), axis=0)
            for j in range(STEP)
        ]
        top = fold8(tops, jnp.maximum)
        at = pl.ds(pl.multiple_of((2 * c + odd) * STEP, STEP), STEP)
        kb = jnp.zeros((STEP, LANES), jnp.int32)
        for j in range(STEP):
            kb = jnp.where(sub == j, order[(2 * c + odd) * STEP + j], kb)
        kb = jnp.tile(kb, (1, rows // LANES))
        top = jnp.where(block8 > kb, top, jnp.where(block8 == kb, diag, MASKED))
        m_ref[at, :] = top
        kf = k.astype(jnp.float32)
        pk_ref[at, 0:dim] = fold_keys(kf, jnp.max, jnp.maximum)
        pk_ref[at, dim : 2 * dim] = fold_keys(kf, jnp.min, jnp.minimum)
        pk_ref[at, 2 * dim : 3 * dim] = lax.dot_general(
            mean, k, (((1,), (0,)), ((), ())), preferred_element_type=jnp.float32
        )
        return spread(top, jnp.maximum)

    def drain(c, s_ref, top, high, total):
        new = jnp.maximum(high, top)
        total = total * jnp.exp2((high - new) * scale)
        for j in range(STEP):
            fresh = tile_sum(s_ref[j * BLK : (j + 1) * BLK, :], new, scale)
            total = total + jnp.where(block8 > order[(2 * c + odd) * STEP + j], fresh, 0.0)
        return new, total

    chunks = k_ref.shape[0] // width
    bufs = (s0, s1)
    top = fill(0, s0)
    for c in range(chunks):
        ahead = fill(c + 1, bufs[(c + 1) % 2]) if c + 1 < chunks else None
        if c + 1 == chunks and before_last is not None:
            before_last()
        high, total = drain(c, bufs[c % 2], top, high, total)
        top = ahead
    return high, total


def half_kernel(
    own, scal, order, q_ref, k_ref, high_ref, total_ref,
    high_out, total_out, m_ref, pk_ref, s0, s1,
):
    diag = high_ref[...]
    high = jnp.broadcast_to(diag, high_out.shape)
    m_ref[...] = jnp.full(m_ref.shape, MASKED, jnp.float32)
    pk_ref[...] = jnp.zeros(pk_ref.shape, jnp.float32)
    high, total = scan_keys(
        own, scal, order, scal[1 + own], q_ref[...], k_ref, diag, high, total_ref[...],
        m_ref, pk_ref, s0, s1,
    )
    high_out[...] = high
    total_out[...] = total


def kernel(
    own, scal, order, q_ref, k_ref, ordv, diag_ref, high_ref, total_ref, m_in, pk_in,
    pq_ref, xq_ref, wk, t_ref, g_ref, m_ref, pk_ref, s0, s1,
):
    rows, dim = q_ref.shape
    toks = own * BLK
    group = rows // toks
    blocks = order.shape[0]
    length = scal[0]
    odd = scal[1 + own]
    scale = math.log2(math.e) / math.sqrt(dim)
    part, pos = lane_part(rows, toks)
    block = lane_block(scal, part, own)
    m_ref[...] = jnp.full(m_ref.shape, MASKED, jnp.float32)
    seen = lax.rem(lax.broadcasted_iota(jnp.int32, (blocks, 1), 0) // STEP, 2) == odd
    row = lax.broadcasted_iota(jnp.int32, (COUNT, 1), 0)
    qblock = lane_block(scal, lax.rem(row, own), own)
    gate = {}

    def gate_forward():
        pq = pq_ref[...]
        xq = xq_ref[...]
        pk = jnp.where(seen, pk_in[...], pk_ref[...])
        xk = dot(pk, wk[...], ((1,), (0,)))
        rq = lax.rsqrt(jnp.mean(xq * xq, axis=1, keepdims=True) + EPS)
        rk = lax.rsqrt(jnp.mean(xk * xk, axis=1, keepdims=True) + EPS)
        uq = xq * rq
        uk = xk * rk
        gate_scale = 1.0 / math.sqrt(xq.shape[1])
        logits = dot(uq, uk, ((1,), (1,))) * gate_scale
        kblock = ordv[...]
        allowed = (kblock <= qblock) & (kblock * BLK < length)
        weights = jnp.where(allowed, jnp.exp(logits), 0.0)
        soft = weights / jnp.sum(weights, axis=1, keepdims=True)
        gate.update(pq=pq, pkt=jnp.transpose(pk), uq=uq, uk=uk, rq=rq, rk=rk, soft=soft)
        gate.update(scale=gate_scale)

    high, total = scan_keys(
        own, scal, order, 1 - odd, q_ref[...], k_ref, diag_ref[...], high_ref[...],
        total_ref[...], m_ref, pk_ref, s0, s1, gate_forward,
    )
    m_ref[0:blocks, :] = jnp.where(seen, m_in[...], m_ref[0:blocks, :])

    log_total = jnp.log2(jnp.sum(total, axis=0, keepdims=True))
    depth = jnp.where(pos + block * BLK < length, (m_ref[...] - high[0:1]) * scale - log_total, MASKED)
    depth = jnp.max(jnp.transpose(depth).reshape(group * own, BLK, LANES), axis=1)[:, :blocks]
    pad = COUNT - group * own
    depth = jnp.concatenate([depth, jnp.full((pad, blocks), MASKED, jnp.float32)], axis=0)
    pooled = jnp.exp2(depth)
    good = (qblock * BLK < length) & (row < group * own)
    totals = jnp.sum(pooled, axis=1, keepdims=True)
    target = jnp.where(good, pooled / jnp.where(good, totals, 1.0), 0.0)
    for h in range(group):
        t_ref[0, h] = target[own * h : own * (h + 1)]

    dl = (gate["soft"] * jnp.sum(target, axis=1, keepdims=True) - target) * gate["scale"]
    uq, uk, rq, rk = gate["uq"], gate["uk"], gate["rq"], gate["rk"]
    duq = dot(dl, uk, ((1,), (0,)))
    duk = dot(dl, uq, ((0,), (0,)))
    dxq = rq * (duq - uq * jnp.mean(duq * uq, axis=1, keepdims=True))
    dxk = rk * (duk - uk * jnp.mean(duk * uk, axis=1, keepdims=True))
    g_ref[0:dim, :] = dot(gate["pq"], dxq, ((0,), (0,)))
    g_ref[dim : 4 * dim, :] = dot(gate["pkt"], dxk, ((1,), (0,)))


def split_kernel(g_ref, q_ref, k_ref, sem):
    rows = q_ref.shape[0]
    copies = [
        pltpu.make_async_copy(g_ref.at[pl.ds(0, rows)], q_ref, sem.at[0]),
        pltpu.make_async_copy(g_ref.at[pl.ds(rows, k_ref.shape[0])], k_ref, sem.at[1]),
    ]
    for copy in copies:
        copy.start()
    for copy in copies:
        copy.wait()


def repeat_kernel(x_ref, o_ref):
    o_ref[...] = jnp.broadcast_to(x_ref[...][None], o_ref.shape)


def body(queries, key_rows, block_order, conv_len, gate_wq, gate_wk):
    toks = queries.shape[1]
    group = queries.shape[2]
    dim = queries.shape[3]
    own = toks // BLK
    rows = group * toks
    blocks = block_order.shape[0]
    width = gate_wq.shape[1]
    key_own = key_rows[0, :, 0, :]
    ny, nz = lax.axis_size("y"), lax.axis_size("zl")
    odd = lax.rem(lax.axis_index("y"), 2)
    peers = ny // 2 * nz
    same = [[y * nz + z for y in range(h, ny, 2) for z in range(nz)] for h in range(2)]
    smem = pl.BlockSpec(memory_space=pltpu.SMEM)
    vmem = pl.BlockSpec(memory_space=pltpu.VMEM)
    anywhere = pl.BlockSpec(memory_space=pl.ANY)
    repeated = pl.pallas_call(
        repeat_kernel,
        out_shape=pltpu.VMEM((peers, toks, dim), key_own.dtype),
        in_specs=[vmem],
        out_specs=vmem,
        name="repeat_keys",
    )(key_own)
    near = lax.all_to_all(
        repeated, CTX, 0, 0, axis_index_groups=same, tiled=True,
    ).reshape(peers * toks, dim)
    length = lax.dynamic_index_in_dim(conv_len, lax.axis_index(("zh", "c")))
    mine = lax.dynamic_slice_in_dim(block_order, lax.axis_index(CTX) * own, own)
    scal = jnp.concatenate([length, mine, odd[None]])
    q = jnp.transpose(queries[0], (1, 0, 2)).reshape(rows, dim)

    def f32(*shape):
        return jax.ShapeDtypeStruct(shape, jnp.float32)

    def near_core(*shape):
        return pltpu.VMEM(shape, jnp.float32)

    def pinned(*arrays):
        return [pltpu.with_memory_space_constraint(x, pltpu.VMEM) for x in arrays]

    first = pl.pallas_call(
        functools.partial(first_kernel, group),
        out_shape=(
            near_core(1, rows), near_core(8, rows), pltpu.VMEM((1, blocks), jnp.int32),
            near_core(COUNT, dim), near_core(COUNT, width),
        ),
        in_specs=[vmem] * 4,
        out_specs=(vmem,) * 5,
        name="own_block",
    )(q, key_own, block_order[None], gate_wq)
    near, scal, first = lax.optimization_barrier((near, scal, first))
    high, total, ordv, pq, xq = first
    pairs = []
    for y in range(ny):
        for c in range(2):
            other = y + 1 if y % 2 == c else y - 1
            pairs.append((2 * y + c, 2 * (other % ny) + c))
    far = lax.ppermute(near, ("y", "c"), pairs)
    buffers = [pltpu.VMEM((STEP * BLK, rows), jnp.float32)] * 2
    after, total, m_half, pk_half = pl.pallas_call(
        functools.partial(half_kernel, own),
        out_shape=(
            near_core(8, rows), near_core(8, rows), near_core(blocks, rows), near_core(blocks, 3 * dim)
        ),
        in_specs=[smem, smem] + [vmem] * 4,
        out_specs=(vmem,) * 4,
        scratch_shapes=buffers,
        name="teacher_near",
    )(scal, block_order, *pinned(q, near, high, total))
    target, grads = pl.pallas_call(
        functools.partial(kernel, own),
        out_shape=(f32(1, group, own, blocks), near_core(4 * dim, width)),
        in_specs=[smem, smem] + [vmem] * 11,
        out_specs=(vmem, vmem),
        scratch_shapes=[
            pltpu.VMEM((LANES, rows), jnp.float32),
            pltpu.VMEM((blocks, 3 * dim), jnp.float32),
            *buffers,
        ],
        name="teacher_gate",
    )(
        scal, block_order,
        *pinned(
            q, far, ordv, high, after, total, m_half, pk_half, pq, xq, gate_wk
        ),
    )

    parts = lax.axis_size(SCATTER)
    rest = lax.axis_size(REST)
    piece = 4 * dim // parts
    share = lax.all_to_all(grads.reshape(parts, piece, width), SCATTER, 0, 0, tiled=True)
    share = jnp.sum(share, axis=0)
    share = lax.all_to_all(
        jnp.broadcast_to(share[None], (rest, piece, width)), REST, 0, 0, tiled=True
    )
    share = jnp.sum(share, axis=0)
    grads = lax.all_to_all(
        jnp.broadcast_to(share[None], (parts, piece, width)), SCATTER, 0, 0, tiled=True
    ).reshape(4 * dim, width)
    grad_wq, grad_wk = pl.pallas_call(
        split_kernel,
        out_shape=(f32(dim, width), f32(3 * dim, width)),
        in_specs=[vmem],
        out_specs=(anywhere, anywhere),
        scratch_shapes=[pltpu.SemaphoreType.DMA((2,))],
        name="split_grads",
    )(*pinned(grads))
    return target, grad_wq, grad_wk


def solution(mesh):
    fine = Mesh(mesh.devices.reshape(8, 4, 4, 2, 2), ("y", "zl", "x", "zh", "c"))
    rows = P(("zh", "c"), CTX, "x", None)
    return jax.shard_map(
        body,
        mesh=fine,
        in_specs=(rows, rows, P(), P(), P(), P()),
        out_specs=(P(("zh", "c"), "x", CTX, None), P(), P()),
        check_vma=False,
    )
```

```python
import functools
import math

import jax
import jax.numpy as jnp
from jax import lax
from jax.experimental import pallas as pl
from jax.experimental.pallas import tpu as pltpu
from jax.sharding import Mesh
from jax.sharding import PartitionSpec as P

BLK = 64
LANES = 128
COUNT = 16
STEP = 8
MASKED = -1e30
EPS = 1e-06
HIGHEST = lax.Precision.HIGHEST


CTX = ("y", "zl")
SCATTER = ("x", "y")
REST = ("zh", "zl", "c")


def dot(a, b, dims):
    return lax.dot_general(
        a, b, (dims, ((), ())), precision=HIGHEST, preferred_element_type=jnp.float32
    )


def scores(k, q):
    return lax.dot_general(k, q, (((1,), (1,)), ((), ())), preferred_element_type=jnp.float32)


def lane_part(rows, toks):
    tok = lax.rem(lax.broadcasted_iota(jnp.int32, (1, rows), 1), toks)
    return tok // BLK, lax.rem(tok, BLK)


def lane_block(scal, part, own):
    block = jnp.zeros_like(part)
    for i in range(own):
        block = jnp.where(part == i, scal[1 + i], block)
    return block


def tile_sum(s, new, scale):
    e = jnp.exp2((s.reshape(s.shape[0] // 8, 8, s.shape[1]) - new) * scale)
    return jnp.sum(e, axis=0)


def spread(x, op):
    for shift in (4, 2, 1):
        x = op(x, pltpu.roll(x, shift, 0))
    return x


def fold8(parts, op):
    sub = lax.broadcasted_iota(jnp.int32, parts[0].shape, 0)
    low = sub < 4
    t = []
    for i in range(4):
        a, b = parts[i], parts[i + 4]
        t.append(op(jnp.where(low, a, b), pltpu.roll(jnp.where(low, b, a), 4, 0)))
    for shift in (2, 1):
        half = len(t) // 2
        low = lax.rem(sub, 2 * shift) < shift
        t = [
            jnp.where(
                low,
                op(t[i], pltpu.roll(t[i], 8 - shift, 0)),
                op(t[i + half], pltpu.roll(t[i + half], shift, 0)),
            )
            for i in range(half)
        ]
    return t[0]


def fold_keys(k, reduce, op):
    parts = [
        reduce(k[j * BLK : (j + 1) * BLK].reshape(BLK // 8, 8, k.shape[1]), axis=0)
        for j in range(STEP)
    ]
    return fold8(parts, op)


def first_kernel(group, q_ref, k_ref, ord_ref, wq, high_ref, total_ref, ord_out, pq_ref, xq_ref):
    rows, dim = q_ref.shape
    toks = rows // group
    own = toks // BLK
    scale = math.log2(math.e) / math.sqrt(dim)
    part, pos = lane_part(rows, toks)
    q = q_ref[...]
    s = scores(k_ref[...], q)
    tile = s[0:BLK]
    for i in range(1, own):
        tile = jnp.where(part == i, s[i * BLK : (i + 1) * BLK], tile)
    tile = jnp.where(lax.broadcasted_iota(jnp.int32, (BLK, rows), 0) <= pos, tile, MASKED)
    high = jnp.max(tile, axis=0, keepdims=True)
    high_ref[...] = high
    total_ref[...] = tile_sum(tile, high, scale)
    pq = jnp.sum(q.astype(jnp.float32).reshape(group * own, BLK, dim), axis=1) * (1.0 / BLK)
    pq = jnp.concatenate([pq, jnp.zeros((COUNT - group * own, dim), jnp.float32)], axis=0)
    pq_ref[...] = pq
    ord_out[...] = ord_ref[...]
    xq_ref[...] = dot(pq, wq[...], ((1,), (0,)))


def scan_keys(own, scal, order, odd, base, q, k_ref, diag, high, total, m_ref, pk_ref, s0, s1, before_last=None):
    rows, dim = q.shape
    toks = own * BLK
    scale = math.log2(math.e) / math.sqrt(dim)
    width = STEP * BLK
    part, _ = lane_part(rows, toks)
    block8 = jnp.broadcast_to(lane_block(scal, part, own), (8, rows))
    diag = jnp.broadcast_to(diag, (8, rows))
    col = lax.broadcasted_iota(jnp.int32, (STEP, width), 1) // BLK
    mean = jnp.where(col == lax.broadcasted_iota(jnp.int32, (STEP, width), 0), 1.0 / BLK, 0.0)
    mean = mean.astype(k_ref.dtype)

    sub = lax.broadcasted_iota(jnp.int32, (STEP, LANES), 0)

    def fill(c, s_ref):
        k = k_ref[pl.ds(pl.multiple_of(c * width, width), width), :]
        s = scores(k, q)
        s_ref[...] = s
        tops = [
            jnp.max(s[j * BLK : (j + 1) * BLK].reshape(BLK // 8, 8, rows), axis=0)
            for j in range(STEP)
        ]
        top = fold8(tops, jnp.maximum)
        at = pl.ds(pl.multiple_of((2 * (base + c) + odd) * STEP, STEP), STEP)
        kb = jnp.zeros((STEP, LANES), jnp.int32)
        for j in range(STEP):
            kb = jnp.where(sub == j, order[(2 * (base + c) + odd) * STEP + j], kb)
        kb = jnp.tile(kb, (1, rows // LANES))
        top = jnp.where(block8 > kb, top, jnp.where(block8 == kb, diag, MASKED))
        m_ref[at, :] = top
        kf = k.astype(jnp.float32)
        pk_ref[at, 0:dim] = fold_keys(kf, jnp.max, jnp.maximum)
        pk_ref[at, dim : 2 * dim] = fold_keys(kf, jnp.min, jnp.minimum)
        pk_ref[at, 2 * dim : 3 * dim] = lax.dot_general(
            mean, k, (((1,), (0,)), ((), ())), preferred_element_type=jnp.float32
        )
        return spread(top, jnp.maximum)

    def drain(c, s_ref, top, high, total):
        new = jnp.maximum(high, top)
        total = total * jnp.exp2((high - new) * scale)
        for j in range(STEP):
            fresh = tile_sum(s_ref[j * BLK : (j + 1) * BLK, :], new, scale)
            total = total + jnp.where(block8 > order[(2 * (base + c) + odd) * STEP + j], fresh, 0.0)
        return new, total

    chunks = k_ref.shape[0] // width
    bufs = (s0, s1)
    top = fill(0, s0)
    for c in range(chunks):
        ahead = fill(c + 1, bufs[(c + 1) % 2]) if c + 1 < chunks else None
        if c + 1 == chunks and before_last is not None:
            before_last()
        high, total = drain(c, bufs[c % 2], top, high, total)
        top = ahead
    return high, total


def near_kernel(
    own, scal, order, q_ref, k_ref, diag_ref, total_ref,
    high_out, total_out, m_ref, pk_ref, s0, s1,
):
    diag = diag_ref[...]
    m_ref[...] = jnp.full(m_ref.shape, MASKED, jnp.float32)
    pk_ref[...] = jnp.zeros(pk_ref.shape, jnp.float32)
    high_out[...], total_out[...] = scan_keys(
        own, scal, order, scal[1 + own], 0, q_ref[...], k_ref, diag,
        jnp.broadcast_to(diag, high_out.shape), total_ref[...], m_ref, pk_ref, s0, s1,
    )


def far_kernel(
    own, scal, order, q_ref, k_ref, diag_ref, high_ref, total_ref, m_in, pk_in,
    high_out, total_out, m_ref, pk_ref, s0, s1,
):
    m_ref[...] = m_in[...]
    pk_ref[...] = pk_in[...]
    high_out[...], total_out[...] = scan_keys(
        own, scal, order, 1 - scal[1 + own], 0, q_ref[...], k_ref, diag_ref[...],
        high_ref[...], total_ref[...], m_ref, pk_ref, s0, s1,
    )


def kernel(
    own, base, scal, order, q_ref, k_ref, ordv, diag_ref, high_ref, total_ref, m_in, pk_in,
    pq_ref, xq_ref, wk, t_ref, g_ref, m_ref, pk_ref, s0, s1,
):
    rows, dim = q_ref.shape
    toks = own * BLK
    group = rows // toks
    blocks = order.shape[0]
    length = scal[0]
    odd = scal[1 + own]
    scale = math.log2(math.e) / math.sqrt(dim)
    part, pos = lane_part(rows, toks)
    block = lane_block(scal, part, own)
    m_ref[0:blocks, :] = m_in[...]
    m_ref[blocks:, :] = jnp.full((m_ref.shape[0] - blocks, rows), MASKED, jnp.float32)
    pk_ref[...] = pk_in[...]
    row = lax.broadcasted_iota(jnp.int32, (COUNT, 1), 0)
    qblock = lane_block(scal, lax.rem(row, own), own)
    gate = {}

    def gate_forward():
        pq = pq_ref[...]
        xq = xq_ref[...]
        pk = pk_ref[...]
        xk = dot(pk, wk[...], ((1,), (0,)))
        rq = lax.rsqrt(jnp.mean(xq * xq, axis=1, keepdims=True) + EPS)
        rk = lax.rsqrt(jnp.mean(xk * xk, axis=1, keepdims=True) + EPS)
        uq = xq * rq
        uk = xk * rk
        gate_scale = 1.0 / math.sqrt(xq.shape[1])
        logits = dot(uq, uk, ((1,), (1,))) * gate_scale
        kblock = ordv[...]
        allowed = (kblock <= qblock) & (kblock * BLK < length)
        weights = jnp.where(allowed, jnp.exp(logits), 0.0)
        soft = weights / jnp.sum(weights, axis=1, keepdims=True)
        gate.update(pq=pq, pkt=jnp.transpose(pk), uq=uq, uk=uk, rq=rq, rk=rk, soft=soft)
        gate.update(scale=gate_scale)

    high, total = scan_keys(
        own, scal, order, 1 - odd, base, q_ref[...], k_ref, diag_ref[...], high_ref[...],
        total_ref[...], m_ref, pk_ref, s0, s1, gate_forward,
    )

    log_total = jnp.log2(jnp.sum(total, axis=0, keepdims=True))
    depth = jnp.where(pos + block * BLK < length, (m_ref[...] - high[0:1]) * scale - log_total, MASKED)
    depth = jnp.max(jnp.transpose(depth).reshape(group * own, BLK, LANES), axis=1)[:, :blocks]
    pad = COUNT - group * own
    depth = jnp.concatenate([depth, jnp.full((pad, blocks), MASKED, jnp.float32)], axis=0)
    pooled = jnp.exp2(depth)
    good = (qblock * BLK < length) & (row < group * own)
    totals = jnp.sum(pooled, axis=1, keepdims=True)
    target = jnp.where(good, pooled / jnp.where(good, totals, 1.0), 0.0)
    for h in range(group):
        t_ref[0, h] = target[own * h : own * (h + 1)]

    dl = (gate["soft"] * jnp.sum(target, axis=1, keepdims=True) - target) * gate["scale"]
    uq, uk, rq, rk = gate["uq"], gate["uk"], gate["rq"], gate["rk"]
    duq = dot(dl, uk, ((1,), (0,)))
    duk = dot(dl, uq, ((0,), (0,)))
    dxq = rq * (duq - uq * jnp.mean(duq * uq, axis=1, keepdims=True))
    dxk = rk * (duk - uk * jnp.mean(duk * uk, axis=1, keepdims=True))
    g_ref[0:dim, :] = dot(gate["pq"], dxq, ((0,), (0,)))
    g_ref[dim : 4 * dim, :] = dot(gate["pkt"], dxk, ((1,), (0,)))


def split_kernel(g_ref, q_ref, k_ref, sem):
    rows = q_ref.shape[0]
    copies = [
        pltpu.make_async_copy(g_ref.at[pl.ds(0, rows)], q_ref, sem.at[0]),
        pltpu.make_async_copy(g_ref.at[pl.ds(rows, k_ref.shape[0])], k_ref, sem.at[1]),
    ]
    for copy in copies:
        copy.start()
    for copy in copies:
        copy.wait()


def repeat_kernel(x_ref, o_ref, sem):
    copies = [
        pltpu.make_async_copy(x_ref, o_ref.at[i], sem.at[i]) for i in range(o_ref.shape[0])
    ]
    for copy in copies:
        copy.start()
    for copy in copies:
        copy.wait()


def body(queries, key_rows, block_order, conv_len, gate_wq, gate_wk):
    toks = queries.shape[1]
    group = queries.shape[2]
    dim = queries.shape[3]
    own = toks // BLK
    rows = group * toks
    blocks = block_order.shape[0]
    width = gate_wq.shape[1]
    key_own = key_rows[0, :, 0, :]
    ny, nz = lax.axis_size("y"), lax.axis_size("zl")
    odd = lax.rem(lax.axis_index("y"), 2)
    peers = ny // 2 * nz
    same = [[y * nz + z for y in range(h, ny, 2) for z in range(nz)] for h in range(2)]
    smem = pl.BlockSpec(memory_space=pltpu.SMEM)
    vmem = pl.BlockSpec(memory_space=pltpu.VMEM)
    anywhere = pl.BlockSpec(memory_space=pl.ANY)
    repeated = pl.pallas_call(
        repeat_kernel,
        out_shape=jax.ShapeDtypeStruct((peers, toks, dim), key_own.dtype),
        in_specs=[vmem],
        out_specs=anywhere,
        scratch_shapes=[pltpu.SemaphoreType.DMA((peers,))],
        name="repeat_keys",
    )(key_own)
    near = lax.all_to_all(
        repeated, CTX, 0, 0, axis_index_groups=same, tiled=True,
    ).reshape(peers * toks, dim)
    length = lax.dynamic_index_in_dim(conv_len, lax.axis_index(("zh", "c")))
    mine = lax.dynamic_slice_in_dim(block_order, lax.axis_index(CTX) * own, own)
    scal = jnp.concatenate([length, mine, odd[None]])
    q = jnp.transpose(queries[0], (1, 0, 2)).reshape(rows, dim)

    def f32(*shape):
        return jax.ShapeDtypeStruct(shape, jnp.float32)

    def near_core(*shape):
        return pltpu.VMEM(shape, jnp.float32)

    def pinned(*arrays):
        return [pltpu.with_memory_space_constraint(x, pltpu.VMEM) for x in arrays]

    first = pl.pallas_call(
        functools.partial(first_kernel, group),
        out_shape=(
            near_core(1, rows), near_core(8, rows), pltpu.VMEM((1, blocks), jnp.int32),
            near_core(COUNT, dim), near_core(COUNT, width),
        ),
        in_specs=[vmem] * 4,
        out_specs=(vmem,) * 5,
        name="own_block",
    )(q, key_own, block_order[None], gate_wq)
    near, scal, first = lax.optimization_barrier((near, scal, first))
    high, total, ordv, pq, xq = first
    pairs = []
    for y in range(ny):
        for c in range(2):
            other = y + 1 if y % 2 == c else y - 1
            pairs.append((2 * y + c, 2 * (other % ny) + c))
    cut = near.shape[0] // 2
    far = [lax.ppermute(part, ("y", "c"), pairs) for part in (near[:cut], near[cut:])]
    buffers = [pltpu.VMEM((STEP * BLK, rows), jnp.float32)] * 2
    state = (
        near_core(8, rows), near_core(8, rows), near_core(blocks, rows), near_core(blocks, 3 * dim)
    )
    seen = pl.pallas_call(
        functools.partial(near_kernel, own),
        out_shape=state,
        in_specs=[smem, smem] + [vmem] * 4,
        out_specs=(vmem,) * 4,
        scratch_shapes=buffers,
        name="teacher_near",
    )(scal, block_order, *pinned(q, near, high, total))
    seen = pl.pallas_call(
        functools.partial(far_kernel, own),
        out_shape=state,
        in_specs=[smem, smem] + [vmem] * 7,
        out_specs=(vmem,) * 4,
        scratch_shapes=buffers,
        name="teacher_far",
    )(scal, block_order, *pinned(q, far[0], high, *seen))
    target, grads = pl.pallas_call(
        functools.partial(kernel, own, cut // (STEP * BLK)),
        out_shape=(f32(1, group, own, blocks), near_core(4 * dim, width)),
        in_specs=[smem, smem] + [vmem] * 11,
        out_specs=(vmem, vmem),
        scratch_shapes=[
            pltpu.VMEM((LANES, rows), jnp.float32),
            pltpu.VMEM((blocks, 3 * dim), jnp.float32),
            *buffers,
        ],
        name="teacher_gate",
    )(scal, block_order, *pinned(q, far[1], ordv, high, *seen, pq, xq, gate_wk))

    parts = lax.axis_size(SCATTER)
    rest = lax.axis_size(REST)
    piece = 4 * dim // parts
    share = lax.all_to_all(grads.reshape(parts, piece, width), SCATTER, 0, 0, tiled=True)
    share = jnp.sum(share, axis=0)
    share = lax.all_to_all(
        jnp.broadcast_to(share[None], (rest, piece, width)), REST, 0, 0, tiled=True
    )
    share = jnp.sum(share, axis=0)
    grads = lax.all_to_all(
        jnp.broadcast_to(share[None], (parts, piece, width)), SCATTER, 0, 0, tiled=True
    ).reshape(4 * dim, width)
    grad_wq, grad_wk = pl.pallas_call(
        split_kernel,
        out_shape=(f32(dim, width), f32(3 * dim, width)),
        in_specs=[vmem],
        out_specs=(anywhere, anywhere),
        scratch_shapes=[pltpu.SemaphoreType.DMA((2,))],
        name="split_grads",
    )(*pinned(grads))
    return target, grad_wq, grad_wk


def solution(mesh):
    fine = Mesh(mesh.devices.reshape(8, 4, 4, 2, 2), ("y", "zl", "x", "zh", "c"))
    rows = P(("zh", "c"), CTX, "x", None)
    return jax.shard_map(
        body,
        mesh=fine,
        in_specs=(rows, rows, P(), P(), P(), P()),
        out_specs=(P(("zh", "c"), "x", CTX, None), P(), P()),
        check_vma=False,
    )
```

```python
import functools
import math

import jax
import jax.numpy as jnp
from jax import lax
from jax.experimental import pallas as pl
from jax.experimental.pallas import tpu as pltpu
from jax.sharding import Mesh
from jax.sharding import PartitionSpec as P

BLK = 64
LANES = 128
COUNT = 16
STEP = 8
MASKED = -1e30
EPS = 1e-06
HIGHEST = lax.Precision.HIGHEST


Y = ("yh", "yl")
Z = ("zm", "zn")
CTX = Y + Z
BATCH = ("zh", "c")
SCATTER = ("x", "yl", "zn", "c")
REST = ("yh", "zh", "zm")


def dot(a, b, dims):
    return lax.dot_general(
        a, b, (dims, ((), ())), precision=HIGHEST, preferred_element_type=jnp.float32
    )


def scores(k, q):
    return lax.dot_general(k, q, (((1,), (1,)), ((), ())), preferred_element_type=jnp.float32)


def lane_part(rows, toks):
    tok = lax.rem(lax.broadcasted_iota(jnp.int32, (1, rows), 1), toks)
    return tok // BLK, lax.rem(tok, BLK)


def lane_block(scal, part, own):
    block = jnp.zeros_like(part)
    for i in range(own):
        block = jnp.where(part == i, scal[1 + i], block)
    return block


def tile_sum(s, new, scale):
    e = jnp.exp2((s.reshape(s.shape[0] // 8, 8, s.shape[1]) - new) * scale)
    return jnp.sum(e, axis=0)


def spread(x, op):
    for shift in (4, 2, 1):
        x = op(x, pltpu.roll(x, shift, 0))
    return x


def fold8(parts, op):
    sub = lax.broadcasted_iota(jnp.int32, parts[0].shape, 0)
    low = sub < 4
    t = []
    for i in range(4):
        a, b = parts[i], parts[i + 4]
        t.append(op(jnp.where(low, a, b), pltpu.roll(jnp.where(low, b, a), 4, 0)))
    for shift in (2, 1):
        half = len(t) // 2
        low = lax.rem(sub, 2 * shift) < shift
        t = [
            jnp.where(
                low,
                op(t[i], pltpu.roll(t[i], 8 - shift, 0)),
                op(t[i + half], pltpu.roll(t[i + half], shift, 0)),
            )
            for i in range(half)
        ]
    return t[0]


def fold_keys(k, reduce, op):
    parts = [
        reduce(k[j * BLK : (j + 1) * BLK].reshape(BLK // 8, 8, k.shape[1]), axis=0)
        for j in range(STEP)
    ]
    return fold8(parts, op)


def first_kernel(group, q_ref, k_ref, ord_ref, wq, high_ref, total_ref, ord_out, pq_ref, xq_ref):
    rows, dim = q_ref.shape
    toks = rows // group
    own = toks // BLK
    scale = math.log2(math.e) / math.sqrt(dim)
    part, pos = lane_part(rows, toks)
    q = q_ref[...]
    s = scores(k_ref[...], q)
    tile = s[0:BLK]
    for i in range(1, own):
        tile = jnp.where(part == i, s[i * BLK : (i + 1) * BLK], tile)
    tile = jnp.where(lax.broadcasted_iota(jnp.int32, (BLK, rows), 0) <= pos, tile, MASKED)
    high = jnp.max(tile, axis=0, keepdims=True)
    high_ref[...] = high
    total_ref[...] = tile_sum(tile, high, scale)
    pq = jnp.sum(q.astype(jnp.float32).reshape(group * own, BLK, dim), axis=1) * (1.0 / BLK)
    pq = jnp.concatenate([pq, jnp.zeros((COUNT - group * own, dim), jnp.float32)], axis=0)
    pq_ref[...] = pq
    ord_out[...] = ord_ref[...]
    xq_ref[...] = dot(pq, wq[...], ((1,), (0,)))


def scan_keys(own, scal, order, odd, base, q, k_ref, diag, high, total, m_ref, pk_ref, s0, s1, before_last=None):
    rows, dim = q.shape
    toks = own * BLK
    scale = math.log2(math.e) / math.sqrt(dim)
    width = STEP * BLK
    part, _ = lane_part(rows, toks)
    block8 = jnp.broadcast_to(lane_block(scal, part, own), (8, rows))
    diag = jnp.broadcast_to(diag, (8, rows))
    col = lax.broadcasted_iota(jnp.int32, (STEP, width), 1) // BLK
    mean = jnp.where(col == lax.broadcasted_iota(jnp.int32, (STEP, width), 0), 1.0 / BLK, 0.0)
    mean = mean.astype(k_ref.dtype)

    sub = lax.broadcasted_iota(jnp.int32, (STEP, LANES), 0)

    def fill(c, s_ref):
        k = k_ref[pl.ds(pl.multiple_of(c * width, width), width), :]
        s = scores(k, q)
        s_ref[...] = s
        tops = [
            jnp.max(s[j * BLK : (j + 1) * BLK].reshape(BLK // 8, 8, rows), axis=0)
            for j in range(STEP)
        ]
        top = fold8(tops, jnp.maximum)
        at = pl.ds(pl.multiple_of((2 * (base + c) + odd) * STEP, STEP), STEP)
        kb = jnp.zeros((STEP, LANES), jnp.int32)
        for j in range(STEP):
            kb = jnp.where(sub == j, order[(2 * (base + c) + odd) * STEP + j], kb)
        kb = jnp.tile(kb, (1, rows // LANES))
        top = jnp.where(block8 > kb, top, jnp.where(block8 == kb, diag, MASKED))
        m_ref[at, :] = top
        kf = k.astype(jnp.float32)
        pk_ref[at, 0:dim] = fold_keys(kf, jnp.max, jnp.maximum)
        pk_ref[at, dim : 2 * dim] = fold_keys(kf, jnp.min, jnp.minimum)
        pk_ref[at, 2 * dim : 3 * dim] = lax.dot_general(
            mean, k, (((1,), (0,)), ((), ())), preferred_element_type=jnp.float32
        )
        return spread(top, jnp.maximum)

    def drain(c, s_ref, top, high, total):
        new = jnp.maximum(high, top)
        total = total * jnp.exp2((high - new) * scale)
        for j in range(STEP):
            fresh = tile_sum(s_ref[j * BLK : (j + 1) * BLK, :], new, scale)
            total = total + jnp.where(block8 > order[(2 * (base + c) + odd) * STEP + j], fresh, 0.0)
        return new, total

    chunks = k_ref.shape[0] // width
    bufs = (s0, s1)
    top = fill(0, s0)
    for c in range(chunks):
        ahead = fill(c + 1, bufs[(c + 1) % 2]) if c + 1 < chunks else None
        if c + 1 == chunks and before_last is not None:
            before_last()
        high, total = drain(c, bufs[c % 2], top, high, total)
        top = ahead
    return high, total


def near_kernel(
    own, scal, order, q_ref, k_ref, diag_ref, total_ref,
    high_out, total_out, m_ref, pk_ref, s0, s1,
):
    diag = diag_ref[...]
    m_ref[...] = jnp.full(m_ref.shape, MASKED, jnp.float32)
    pk_ref[...] = jnp.zeros(pk_ref.shape, jnp.float32)
    high_out[...], total_out[...] = scan_keys(
        own, scal, order, scal[1 + own], 0, q_ref[...], k_ref, diag,
        jnp.broadcast_to(diag, high_out.shape), total_ref[...], m_ref, pk_ref, s0, s1,
    )


def far_kernel(
    own, scal, order, q_ref, k_ref, diag_ref, high_ref, total_ref, m_in, pk_in,
    high_out, total_out, m_ref, pk_ref, s0, s1,
):
    m_ref[...] = m_in[...]
    pk_ref[...] = pk_in[...]
    high_out[...], total_out[...] = scan_keys(
        own, scal, order, 1 - scal[1 + own], 0, q_ref[...], k_ref, diag_ref[...],
        high_ref[...], total_ref[...], m_ref, pk_ref, s0, s1,
    )


def kernel(
    own, base, scal, order, q_ref, k_ref, ordv, diag_ref, high_ref, total_ref, m_in, pk_in,
    pq_ref, xq_ref, wk, t_ref, g_ref, m_ref, pk_ref, s0, s1,
):
    rows, dim = q_ref.shape
    toks = own * BLK
    group = rows // toks
    blocks = order.shape[0]
    length = scal[0]
    odd = scal[1 + own]
    scale = math.log2(math.e) / math.sqrt(dim)
    part, pos = lane_part(rows, toks)
    block = lane_block(scal, part, own)
    m_ref[0:blocks, :] = m_in[...]
    m_ref[blocks:, :] = jnp.full((m_ref.shape[0] - blocks, rows), MASKED, jnp.float32)
    pk_ref[...] = pk_in[...]
    row = lax.broadcasted_iota(jnp.int32, (COUNT, 1), 0)
    qblock = lane_block(scal, lax.rem(row, own), own)
    gate = {}

    def gate_forward():
        pq = pq_ref[...]
        xq = xq_ref[...]
        pk = pk_ref[...]
        xk = dot(pk, wk[...], ((1,), (0,)))
        rq = lax.rsqrt(jnp.mean(xq * xq, axis=1, keepdims=True) + EPS)
        rk = lax.rsqrt(jnp.mean(xk * xk, axis=1, keepdims=True) + EPS)
        uq = xq * rq
        uk = xk * rk
        gate_scale = 1.0 / math.sqrt(xq.shape[1])
        logits = dot(uq, uk, ((1,), (1,))) * gate_scale
        kblock = ordv[...]
        allowed = (kblock <= qblock) & (kblock * BLK < length)
        weights = jnp.where(allowed, jnp.exp(logits), 0.0)
        soft = weights / jnp.sum(weights, axis=1, keepdims=True)
        gate.update(pq=pq, pkt=jnp.transpose(pk), uq=uq, uk=uk, rq=rq, rk=rk, soft=soft)
        gate.update(scale=gate_scale)

    high, total = scan_keys(
        own, scal, order, 1 - odd, base, q_ref[...], k_ref, diag_ref[...], high_ref[...],
        total_ref[...], m_ref, pk_ref, s0, s1, gate_forward,
    )

    log_total = jnp.log2(jnp.sum(total, axis=0, keepdims=True))
    depth = jnp.where(pos + block * BLK < length, (m_ref[...] - high[0:1]) * scale - log_total, MASKED)
    depth = jnp.max(jnp.transpose(depth).reshape(group * own, BLK, LANES), axis=1)[:, :blocks]
    pad = COUNT - group * own
    depth = jnp.concatenate([depth, jnp.full((pad, blocks), MASKED, jnp.float32)], axis=0)
    pooled = jnp.exp2(depth)
    good = (qblock * BLK < length) & (row < group * own)
    totals = jnp.sum(pooled, axis=1, keepdims=True)
    target = jnp.where(good, pooled / jnp.where(good, totals, 1.0), 0.0)
    for h in range(group):
        t_ref[0, h] = target[own * h : own * (h + 1)]

    dl = (gate["soft"] * jnp.sum(target, axis=1, keepdims=True) - target) * gate["scale"]
    uq, uk, rq, rk = gate["uq"], gate["uk"], gate["rq"], gate["rk"]
    duq = dot(dl, uk, ((1,), (0,)))
    duk = dot(dl, uq, ((0,), (0,)))
    dxq = rq * (duq - uq * jnp.mean(duq * uq, axis=1, keepdims=True))
    dxk = rk * (duk - uk * jnp.mean(duk * uk, axis=1, keepdims=True))
    g_ref[0:dim, :] = dot(gate["pq"], dxq, ((0,), (0,)))
    g_ref[dim : 4 * dim, :] = dot(gate["pkt"], dxk, ((1,), (0,)))


def split_kernel(g_ref, q_ref, k_ref, sem):
    rows = q_ref.shape[0]
    copies = [
        pltpu.make_async_copy(g_ref.at[pl.ds(0, rows)], q_ref, sem.at[0]),
        pltpu.make_async_copy(g_ref.at[pl.ds(rows, k_ref.shape[0])], k_ref, sem.at[1]),
    ]
    for copy in copies:
        copy.start()
    for copy in copies:
        copy.wait()


def repeat_kernel(x_ref, o_ref, sem):
    copies = [
        pltpu.make_async_copy(x_ref, o_ref.at[i], sem.at[i]) for i in range(o_ref.shape[0])
    ]
    for copy in copies:
        copy.start()
    for copy in copies:
        copy.wait()


def body(queries, key_rows, block_order, conv_len, gate_wq, gate_wk):
    toks = queries.shape[1]
    group = queries.shape[2]
    dim = queries.shape[3]
    own = toks // BLK
    rows = group * toks
    blocks = block_order.shape[0]
    width = gate_wq.shape[1]
    key_own = key_rows[0, :, 0, :]
    ny, nz = lax.axis_size(Y), lax.axis_size(Z)
    odd = lax.rem(lax.axis_index(Y), 2)
    peers = ny // 2 * nz
    same = [[y * nz + z for y in range(h, ny, 2) for z in range(nz)] for h in range(2)]
    smem = pl.BlockSpec(memory_space=pltpu.SMEM)
    vmem = pl.BlockSpec(memory_space=pltpu.VMEM)
    anywhere = pl.BlockSpec(memory_space=pl.ANY)
    repeated = pl.pallas_call(
        repeat_kernel,
        out_shape=jax.ShapeDtypeStruct((peers, toks, dim), key_own.dtype),
        in_specs=[vmem],
        out_specs=anywhere,
        scratch_shapes=[pltpu.SemaphoreType.DMA((peers,))],
        name="repeat_keys",
    )(key_own)
    near = lax.all_to_all(
        repeated, CTX, 0, 0, axis_index_groups=same, tiled=True,
    ).reshape(peers * toks, dim)
    length = lax.dynamic_index_in_dim(conv_len, lax.axis_index(BATCH))
    mine = lax.dynamic_slice_in_dim(block_order, lax.axis_index(CTX) * own, own)
    scal = jnp.concatenate([length, mine, odd[None]])
    q = jnp.transpose(queries[0], (1, 0, 2)).reshape(rows, dim)

    def f32(*shape):
        return jax.ShapeDtypeStruct(shape, jnp.float32)

    def near_core(*shape):
        return pltpu.VMEM(shape, jnp.float32)

    def pinned(*arrays):
        return [pltpu.with_memory_space_constraint(x, pltpu.VMEM) for x in arrays]

    first = pl.pallas_call(
        functools.partial(first_kernel, group),
        out_shape=(
            near_core(1, rows), near_core(8, rows), pltpu.VMEM((1, blocks), jnp.int32),
            near_core(COUNT, dim), near_core(COUNT, width),
        ),
        in_specs=[vmem] * 4,
        out_specs=(vmem,) * 5,
        name="own_block",
    )(q, key_own, block_order[None], gate_wq)
    near, scal, first = lax.optimization_barrier((near, scal, first))
    high, total, ordv, pq, xq = first
    pairs = []
    for y in range(ny):
        for c in range(2):
            other = y + 1 if y % 2 == c else y - 1
            pairs.append((2 * y + c, 2 * (other % ny) + c))
    cut = near.shape[0] // 2
    far = [lax.ppermute(part, Y + ("c",), pairs) for part in (near[:cut], near[cut:])]
    buffers = [pltpu.VMEM((STEP * BLK, rows), jnp.float32)] * 2
    state = (
        near_core(8, rows), near_core(8, rows), near_core(blocks, rows), near_core(blocks, 3 * dim)
    )
    seen = pl.pallas_call(
        functools.partial(near_kernel, own),
        out_shape=state,
        in_specs=[smem, smem] + [vmem] * 4,
        out_specs=(vmem,) * 4,
        scratch_shapes=buffers,
        name="teacher_near",
    )(scal, block_order, *pinned(q, near, high, total))
    seen = pl.pallas_call(
        functools.partial(far_kernel, own),
        out_shape=state,
        in_specs=[smem, smem] + [vmem] * 7,
        out_specs=(vmem,) * 4,
        scratch_shapes=buffers,
        name="teacher_far",
    )(scal, block_order, *pinned(q, far[0], high, *seen))
    target, grads = pl.pallas_call(
        functools.partial(kernel, own, cut // (STEP * BLK)),
        out_shape=(f32(1, group, own, blocks), near_core(4 * dim, width)),
        in_specs=[smem, smem] + [vmem] * 11,
        out_specs=(vmem, vmem),
        scratch_shapes=[
            pltpu.VMEM((LANES, rows), jnp.float32),
            pltpu.VMEM((blocks, 3 * dim), jnp.float32),
            *buffers,
        ],
        name="teacher_gate",
    )(scal, block_order, *pinned(q, far[1], ordv, high, *seen, pq, xq, gate_wk))

    parts = lax.axis_size(SCATTER)
    rest = lax.axis_size(REST)
    piece = 4 * dim // parts
    share = lax.all_to_all(grads.reshape(parts, piece, width), SCATTER, 0, 0, tiled=True)
    share = jnp.sum(share, axis=0)
    share = lax.all_to_all(
        jnp.broadcast_to(share[None], (rest, piece, width)), REST, 0, 0, tiled=True
    )
    share = jnp.sum(share, axis=0)
    grads = lax.all_to_all(
        jnp.broadcast_to(share[None], (parts, piece, width)), SCATTER, 0, 0, tiled=True
    ).reshape(4 * dim, width)
    grad_wq, grad_wk = pl.pallas_call(
        split_kernel,
        out_shape=(f32(dim, width), f32(3 * dim, width)),
        in_specs=[vmem],
        out_specs=(anywhere, anywhere),
        scratch_shapes=[pltpu.SemaphoreType.DMA((2,))],
        name="split_grads",
    )(*pinned(grads))
    return target, grad_wq, grad_wk


def solution(mesh):
    names = Y + Z + ("x",) + BATCH
    fine = Mesh(mesh.devices.reshape(4, 2, 2, 2, 4, 2, 2), names)
    rows = P(BATCH, CTX, "x", None)
    return jax.shard_map(
        body,
        mesh=fine,
        in_specs=(rows, rows, P(), P(), P(), P()),
        out_specs=(P(BATCH, "x", CTX, None), P(), P()),
        check_vma=False,
    )
```

```python
import functools
import math

import jax
import jax.numpy as jnp
from jax import lax
from jax.experimental import pallas as pl
from jax.experimental.pallas import tpu as pltpu
from jax.sharding import Mesh
from jax.sharding import PartitionSpec as P

BLK = 64
LANES = 128
COUNT = 16
STEP = 8
MASKED = -1e30
EPS = 1e-06
HIGHEST = lax.Precision.HIGHEST


Y = ("yh", "yl")
Z = ("zm", "zn")
CTX = Y + Z
BATCH = ("zh", "c")
SCATTER = ("x", "yl", "zn", "c")
REST = ("yh", "zh", "zm")


def dot(a, b, dims):
    return lax.dot_general(
        a, b, (dims, ((), ())), precision=HIGHEST, preferred_element_type=jnp.float32
    )


def scores(k, q):
    return lax.dot_general(k, q, (((1,), (1,)), ((), ())), preferred_element_type=jnp.float32)


def lane_part(rows, toks):
    tok = lax.rem(lax.broadcasted_iota(jnp.int32, (1, rows), 1), toks)
    return tok // BLK, lax.rem(tok, BLK)


def lane_block(scal, part, own):
    block = jnp.zeros_like(part)
    for i in range(own):
        block = jnp.where(part == i, scal[1 + i], block)
    return block


def tile_sum(s, new, scale):
    e = jnp.exp2((s.reshape(s.shape[0] // 8, 8, s.shape[1]) - new) * scale)
    return jnp.sum(e, axis=0)


def spread(x, op):
    for shift in (4, 2, 1):
        x = op(x, pltpu.roll(x, shift, 0))
    return x


def fold8(parts, op):
    sub = lax.broadcasted_iota(jnp.int32, parts[0].shape, 0)
    low = sub < 4
    t = []
    for i in range(4):
        a, b = parts[i], parts[i + 4]
        t.append(op(jnp.where(low, a, b), pltpu.roll(jnp.where(low, b, a), 4, 0)))
    for shift in (2, 1):
        half = len(t) // 2
        low = lax.rem(sub, 2 * shift) < shift
        t = [
            jnp.where(
                low,
                op(t[i], pltpu.roll(t[i], 8 - shift, 0)),
                op(t[i + half], pltpu.roll(t[i + half], shift, 0)),
            )
            for i in range(half)
        ]
    return t[0]


def fold_keys(k, reduce, op):
    parts = [
        reduce(k[j * BLK : (j + 1) * BLK].reshape(BLK // 8, 8, k.shape[1]), axis=0)
        for j in range(STEP)
    ]
    return fold8(parts, op)


def first_kernel(group, q_ref, k_ref, ord_ref, wq, high_ref, total_ref, ord_out, pq_ref, xq_ref):
    rows, dim = q_ref.shape
    toks = rows // group
    own = toks // BLK
    scale = math.log2(math.e) / math.sqrt(dim)
    part, pos = lane_part(rows, toks)
    q = q_ref[...]
    s = scores(k_ref[...], q)
    tile = s[0:BLK]
    for i in range(1, own):
        tile = jnp.where(part == i, s[i * BLK : (i + 1) * BLK], tile)
    tile = jnp.where(lax.broadcasted_iota(jnp.int32, (BLK, rows), 0) <= pos, tile, MASKED)
    high = jnp.max(tile, axis=0, keepdims=True)
    high_ref[...] = high
    total_ref[...] = tile_sum(tile, high, scale)
    pq = jnp.sum(q.astype(jnp.float32).reshape(group * own, BLK, dim), axis=1) * (1.0 / BLK)
    pq = jnp.concatenate([pq, jnp.zeros((COUNT - group * own, dim), jnp.float32)], axis=0)
    pq_ref[...] = pq
    ord_out[...] = ord_ref[...]
    xq_ref[...] = dot(pq, wq[...], ((1,), (0,)))


def scan_keys(own, scal, order, odd, base, q, k_ref, diag, high, total, m_ref, pk_ref, s0, s1, before_last=None):
    rows, dim = q.shape
    toks = own * BLK
    scale = math.log2(math.e) / math.sqrt(dim)
    width = STEP * BLK
    part, _ = lane_part(rows, toks)
    block8 = jnp.broadcast_to(lane_block(scal, part, own), (8, rows))
    diag = jnp.broadcast_to(diag, (8, rows))
    col = lax.broadcasted_iota(jnp.int32, (STEP, width), 1) // BLK
    mean = jnp.where(col == lax.broadcasted_iota(jnp.int32, (STEP, width), 0), 1.0 / BLK, 0.0)
    mean = mean.astype(k_ref.dtype)

    sub = lax.broadcasted_iota(jnp.int32, (STEP, LANES), 0)

    def fill(c, s_ref):
        k = k_ref[pl.ds(pl.multiple_of(c * width, width), width), :]
        s = scores(k, q)
        s_ref[...] = s
        tops = [
            jnp.max(s[j * BLK : (j + 1) * BLK].reshape(BLK // 8, 8, rows), axis=0)
            for j in range(STEP)
        ]
        top = fold8(tops, jnp.maximum)
        at = pl.ds(pl.multiple_of((2 * (base + c) + odd) * STEP, STEP), STEP)
        kb = jnp.zeros((STEP, LANES), jnp.int32)
        for j in range(STEP):
            kb = jnp.where(sub == j, order[(2 * (base + c) + odd) * STEP + j], kb)
        kb = jnp.tile(kb, (1, rows // LANES))
        top = jnp.where(block8 > kb, top, jnp.where(block8 == kb, diag, MASKED))
        m_ref[at, :] = top
        kf = k.astype(jnp.float32)
        pk_ref[at, 0:dim] = fold_keys(kf, jnp.max, jnp.maximum)
        pk_ref[at, dim : 2 * dim] = fold_keys(kf, jnp.min, jnp.minimum)
        pk_ref[at, 2 * dim : 3 * dim] = lax.dot_general(
            mean, k, (((1,), (0,)), ((), ())), preferred_element_type=jnp.float32
        )
        return spread(top, jnp.maximum)

    def drain(c, s_ref, top, high, total):
        new = jnp.maximum(high, top)
        total = total * jnp.exp2((high - new) * scale)
        for j in range(STEP):
            fresh = tile_sum(s_ref[j * BLK : (j + 1) * BLK, :], new, scale)
            total = total + jnp.where(block8 > order[(2 * (base + c) + odd) * STEP + j], fresh, 0.0)
        return new, total

    chunks = k_ref.shape[0] // width
    bufs = (s0, s1)
    top = fill(0, s0)
    for c in range(chunks):
        ahead = fill(c + 1, bufs[(c + 1) % 2]) if c + 1 < chunks else None
        if c + 1 == chunks and before_last is not None:
            before_last()
        high, total = drain(c, bufs[c % 2], top, high, total)
        top = ahead
    return high, total


def near_kernel(
    own, scal, order, q_ref, k_ref, diag_ref, total_ref,
    high_out, total_out, m_ref, pk_ref, s0, s1,
):
    diag = diag_ref[...]
    m_ref[...] = jnp.full(m_ref.shape, MASKED, jnp.float32)
    pk_ref[...] = jnp.zeros(pk_ref.shape, jnp.float32)
    high_out[...], total_out[...] = scan_keys(
        own, scal, order, scal[1 + own], 0, q_ref[...], k_ref, diag,
        jnp.broadcast_to(diag, high_out.shape), total_ref[...], m_ref, pk_ref, s0, s1,
    )


def far_kernel(
    own, scal, order, q_ref, k_ref, diag_ref, high_ref, total_ref, m_in, pk_in,
    high_out, total_out, m_ref, pk_ref, s0, s1,
):
    m_ref[...] = m_in[...]
    pk_ref[...] = pk_in[...]
    high_out[...], total_out[...] = scan_keys(
        own, scal, order, 1 - scal[1 + own], 0, q_ref[...], k_ref, diag_ref[...],
        high_ref[...], total_ref[...], m_ref, pk_ref, s0, s1,
    )


def kernel(
    own, base, scal, order, q_ref, k_ref, ordv, diag_ref, high_ref, total_ref, m_in, pk_in,
    pq_ref, xq_ref, wk, t_ref, g_ref, m_ref, pk_ref, s0, s1,
):
    rows, dim = q_ref.shape
    toks = own * BLK
    group = rows // toks
    blocks = order.shape[0]
    length = scal[0]
    odd = scal[1 + own]
    scale = math.log2(math.e) / math.sqrt(dim)
    part, pos = lane_part(rows, toks)
    block = lane_block(scal, part, own)
    m_ref[...] = m_in[...]
    pk_ref[...] = pk_in[...]
    row = lax.broadcasted_iota(jnp.int32, (COUNT, 1), 0)
    qblock = lane_block(scal, lax.rem(row, own), own)
    gate = {}

    def gate_forward():
        pq = pq_ref[...]
        xq = xq_ref[...]
        pk = pk_ref[...]
        xk = dot(pk, wk[...], ((1,), (0,)))
        rq = lax.rsqrt(jnp.mean(xq * xq, axis=1, keepdims=True) + EPS)
        rk = lax.rsqrt(jnp.mean(xk * xk, axis=1, keepdims=True) + EPS)
        uq = xq * rq
        uk = xk * rk
        gate_scale = 1.0 / math.sqrt(xq.shape[1])
        logits = dot(uq, uk, ((1,), (1,))) * gate_scale
        kblock = ordv[...]
        allowed = (kblock <= qblock) & (kblock * BLK < length)
        weights = jnp.where(allowed, jnp.exp(logits), 0.0)
        soft = weights / jnp.sum(weights, axis=1, keepdims=True)
        gate.update(pq=pq, pkt=jnp.transpose(pk), uq=uq, uk=uk, rq=rq, rk=rk, soft=soft)
        gate.update(scale=gate_scale)

    high, total = scan_keys(
        own, scal, order, 1 - odd, base, q_ref[...], k_ref, diag_ref[...], high_ref[...],
        total_ref[...], m_ref, pk_ref, s0, s1, gate_forward,
    )

    log_total = jnp.log2(jnp.sum(total, axis=0, keepdims=True))
    depth = jnp.where(pos + block * BLK < length, (m_ref[...] - high[0:1]) * scale - log_total, MASKED)
    depth = jnp.max(jnp.transpose(depth).reshape(group * own, BLK, blocks), axis=1)
    pad = COUNT - group * own
    depth = jnp.concatenate([depth, jnp.full((pad, blocks), MASKED, jnp.float32)], axis=0)
    pooled = jnp.exp2(depth)
    good = (qblock * BLK < length) & (row < group * own)
    totals = jnp.sum(pooled, axis=1, keepdims=True)
    target = jnp.where(good, pooled / jnp.where(good, totals, 1.0), 0.0)
    for h in range(group):
        t_ref[0, h] = target[own * h : own * (h + 1)]

    dl = (jnp.where(good, gate["soft"], 0.0) - target) * gate["scale"]
    uq, uk, rq, rk = gate["uq"], gate["uk"], gate["rq"], gate["rk"]
    duq = dot(dl, uk, ((1,), (0,)))
    duk = dot(dl, uq, ((0,), (0,)))
    dxq = rq * (duq - uq * jnp.mean(duq * uq, axis=1, keepdims=True))
    dxk = rk * (duk - uk * jnp.mean(duk * uk, axis=1, keepdims=True))
    g_ref[0:dim, :] = dot(gate["pq"], dxq, ((0,), (0,)))
    g_ref[dim : 4 * dim, :] = dot(gate["pkt"], dxk, ((1,), (0,)))


def split_kernel(g_ref, q_ref, k_ref, sem):
    rows = q_ref.shape[0]
    copies = [
        pltpu.make_async_copy(g_ref.at[pl.ds(0, rows)], q_ref, sem.at[0]),
        pltpu.make_async_copy(g_ref.at[pl.ds(rows, k_ref.shape[0])], k_ref, sem.at[1]),
    ]
    for copy in copies:
        copy.start()
    for copy in copies:
        copy.wait()


def repeat_kernel(x_ref, o_ref, sem):
    copies = [
        pltpu.make_async_copy(x_ref, o_ref.at[i], sem.at[i]) for i in range(o_ref.shape[0])
    ]
    for copy in copies:
        copy.start()
    for copy in copies:
        copy.wait()


def body(queries, key_rows, block_order, conv_len, gate_wq, gate_wk):
    toks = queries.shape[1]
    group = queries.shape[2]
    dim = queries.shape[3]
    own = toks // BLK
    rows = group * toks
    blocks = block_order.shape[0]
    width = gate_wq.shape[1]
    key_own = key_rows[0, :, 0, :]
    ny, nz = lax.axis_size(Y), lax.axis_size(Z)
    odd = lax.rem(lax.axis_index(Y), 2)
    peers = ny // 2 * nz
    same = [[y * nz + z for y in range(h, ny, 2) for z in range(nz)] for h in range(2)]
    smem = pl.BlockSpec(memory_space=pltpu.SMEM)
    vmem = pl.BlockSpec(memory_space=pltpu.VMEM)
    anywhere = pl.BlockSpec(memory_space=pl.ANY)
    repeated = pl.pallas_call(
        repeat_kernel,
        out_shape=jax.ShapeDtypeStruct((peers, toks, dim), key_own.dtype),
        in_specs=[vmem],
        out_specs=anywhere,
        scratch_shapes=[pltpu.SemaphoreType.DMA((peers,))],
        name="repeat_keys",
    )(key_own)
    near = lax.all_to_all(
        repeated, CTX, 0, 0, axis_index_groups=same, tiled=True,
    ).reshape(peers * toks, dim)
    length = lax.dynamic_index_in_dim(conv_len, lax.axis_index(BATCH))
    mine = lax.dynamic_slice_in_dim(block_order, lax.axis_index(CTX) * own, own)
    scal = jnp.concatenate([length, mine, odd[None]])
    q = jnp.transpose(queries[0], (1, 0, 2)).reshape(rows, dim)

    def f32(*shape):
        return jax.ShapeDtypeStruct(shape, jnp.float32)

    def near_core(*shape):
        return pltpu.VMEM(shape, jnp.float32)

    def pinned(*arrays):
        return [pltpu.with_memory_space_constraint(x, pltpu.VMEM) for x in arrays]

    first = pl.pallas_call(
        functools.partial(first_kernel, group),
        out_shape=(
            near_core(1, rows), near_core(8, rows), pltpu.VMEM((1, blocks), jnp.int32),
            near_core(COUNT, dim), near_core(COUNT, width),
        ),
        in_specs=[vmem] * 4,
        out_specs=(vmem,) * 5,
        name="own_block",
    )(q, key_own, block_order[None], gate_wq)
    near, scal, first = lax.optimization_barrier((near, scal, first))
    high, total, ordv, pq, xq = first
    pairs = []
    for y in range(ny):
        for c in range(2):
            other = y + 1 if y % 2 == c else y - 1
            pairs.append((2 * y + c, 2 * (other % ny) + c))
    cut = near.shape[0] // 4 * 3
    far = [lax.ppermute(part, Y + ("c",), pairs) for part in (near[:cut], near[cut:])]
    buffers = [pltpu.VMEM((STEP * BLK, rows), jnp.float32)] * 2
    state = (
        near_core(8, rows), near_core(8, rows), near_core(blocks, rows), near_core(blocks, 3 * dim)
    )
    seen = pl.pallas_call(
        functools.partial(near_kernel, own),
        out_shape=state,
        in_specs=[smem, smem] + [vmem] * 4,
        out_specs=(vmem,) * 4,
        scratch_shapes=buffers,
        name="teacher_near",
    )(scal, block_order, *pinned(q, near, high, total))
    seen = pl.pallas_call(
        functools.partial(far_kernel, own),
        out_shape=state,
        in_specs=[smem, smem] + [vmem] * 7,
        out_specs=(vmem,) * 4,
        scratch_shapes=buffers,
        name="teacher_far",
    )(scal, block_order, *pinned(q, far[0], high, *seen))
    target, grads = pl.pallas_call(
        functools.partial(kernel, own, cut // (STEP * BLK)),
        out_shape=(f32(1, group, own, blocks), near_core(4 * dim, width)),
        in_specs=[smem, smem] + [vmem] * 11,
        out_specs=(vmem, vmem),
        scratch_shapes=[
            pltpu.VMEM((blocks, rows), jnp.float32),
            pltpu.VMEM((blocks, 3 * dim), jnp.float32),
            *buffers,
        ],
        name="teacher_gate",
    )(scal, block_order, *pinned(q, far[1], ordv, high, *seen, pq, xq, gate_wk))

    parts = lax.axis_size(SCATTER)
    rest = lax.axis_size(REST)
    piece = 4 * dim // parts
    share = lax.all_to_all(grads.reshape(parts, piece, width), SCATTER, 0, 0, tiled=True)
    share = jnp.sum(share, axis=0)
    share = lax.all_to_all(
        jnp.broadcast_to(share[None], (rest, piece, width)), REST, 0, 0, tiled=True
    )
    share = jnp.sum(share, axis=0)
    grads = lax.all_to_all(
        jnp.broadcast_to(share[None], (parts, piece, width)), SCATTER, 0, 0, tiled=True
    ).reshape(4 * dim, width)
    grad_wq, grad_wk = pl.pallas_call(
        split_kernel,
        out_shape=(f32(dim, width), f32(3 * dim, width)),
        in_specs=[vmem],
        out_specs=(anywhere, anywhere),
        scratch_shapes=[pltpu.SemaphoreType.DMA((2,))],
        name="split_grads",
    )(*pinned(grads))
    return target, grad_wq, grad_wk


def solution(mesh):
    names = Y + Z + ("x",) + BATCH
    fine = Mesh(mesh.devices.reshape(4, 2, 2, 2, 4, 2, 2), names)
    rows = P(BATCH, CTX, "x", None)
    return jax.shard_map(
        body,
        mesh=fine,
        in_specs=(rows, rows, P(), P(), P(), P()),
        out_specs=(P(BATCH, "x", CTX, None), P(), P()),
        check_vma=False,
    )
```

```python
import functools
import math

import jax
import jax.numpy as jnp
from jax import lax
from jax.experimental import pallas as pl
from jax.experimental.pallas import tpu as pltpu
from jax.sharding import Mesh
from jax.sharding import PartitionSpec as P

BLK = 64
LANES = 128
COUNT = 16
STEP = 8
MASKED = -1e30
EPS = 1e-06
HIGHEST = lax.Precision.HIGHEST


Y = ("yh", "yl")
Z = ("zm", "zn")
CTX = Y + Z
FAR = ("yh", "zm")
BATCH = ("zh", "c")
SETS = ((0, 0), (0, 1), (1, 0), (1, 1))
SCATTER = ("x", "yl", "zn", "c")
REST = ("yh", "zh", "zm")


def dot(a, b, dims):
    return lax.dot_general(
        a, b, (dims, ((), ())), precision=HIGHEST, preferred_element_type=jnp.float32
    )


def scores(k, q):
    return lax.dot_general(k, q, (((1,), (1,)), ((), ())), preferred_element_type=jnp.float32)


def lane_part(rows, toks):
    tok = lax.rem(lax.broadcasted_iota(jnp.int32, (1, rows), 1), toks)
    return tok // BLK, lax.rem(tok, BLK)


def lane_block(scal, part, own):
    block = jnp.zeros_like(part)
    for i in range(own):
        block = jnp.where(part == i, scal[1 + i], block)
    return block


def tile_sum(s, new, scale):
    e = jnp.exp2((s.reshape(s.shape[0] // 8, 8, s.shape[1]) - new) * scale)
    return jnp.sum(e, axis=0)


def spread(x, op):
    for shift in (4, 2, 1):
        x = op(x, pltpu.roll(x, shift, 0))
    return x


def fold8(parts, op):
    sub = lax.broadcasted_iota(jnp.int32, parts[0].shape, 0)
    low = sub < 4
    t = []
    for i in range(4):
        a, b = parts[i], parts[i + 4]
        t.append(op(jnp.where(low, a, b), pltpu.roll(jnp.where(low, b, a), 4, 0)))
    for shift in (2, 1):
        half = len(t) // 2
        low = lax.rem(sub, 2 * shift) < shift
        t = [
            jnp.where(
                low,
                op(t[i], pltpu.roll(t[i], 8 - shift, 0)),
                op(t[i + half], pltpu.roll(t[i + half], shift, 0)),
            )
            for i in range(half)
        ]
    return t[0]


def fold_keys(k, reduce, op):
    parts = [
        reduce(k[j * BLK : (j + 1) * BLK].reshape(BLK // 8, 8, k.shape[1]), axis=0)
        for j in range(STEP)
    ]
    return fold8(parts, op)


def first_kernel(group, scal, order, q_ref, k_ref, wq, high_ref, total_ref, ord_out, pq_ref, xq_ref):
    rows, dim = q_ref.shape
    toks = rows // group
    own = toks // BLK
    scale = math.log2(math.e) / math.sqrt(dim)
    part, pos = lane_part(rows, toks)
    q = q_ref[...]
    s = scores(k_ref[...], q)
    tile = s[0:BLK]
    for i in range(1, own):
        tile = jnp.where(part == i, s[i * BLK : (i + 1) * BLK], tile)
    tile = jnp.where(lax.broadcasted_iota(jnp.int32, (BLK, rows), 0) <= pos, tile, MASKED)
    high = jnp.max(tile, axis=0, keepdims=True)
    high_ref[...] = high
    total_ref[...] = tile_sum(tile, high, scale)
    pq = jnp.sum(q.astype(jnp.float32).reshape(group * own, BLK, dim), axis=1) * (1.0 / BLK)
    pq = jnp.concatenate([pq, jnp.zeros((COUNT - group * own, dim), jnp.float32)], axis=0)
    pq_ref[...] = pq
    lane = lax.broadcasted_iota(jnp.int32, ord_out.shape, 1)
    ids = jnp.zeros(ord_out.shape, jnp.int32)
    share = ord_out.shape[1] // len(SETS)
    for i in range(ord_out.shape[1]):
        at = slot(scal, own, i // share, i % share // STEP, i % STEP)
        ids = jnp.where(lane == i, order[at], ids)
    ord_out[...] = ids
    xq_ref[...] = dot(pq, wq[...], ((1,), (0,)))


def slot(scal, own, which, c, j):
    dy, dz = SETS[which]
    fy = scal[1 + own] if dy == 0 else 1 - scal[1 + own]
    fz = scal[2 + own] if dz == 0 else 1 - scal[2 + own]
    y = 2 * (2 * c + j // (2 * own)) + fy
    z = 2 * (j // own % 2) + fz
    return (y * 4 + z) * own + j % own


def scan_keys(own, scal, order, which, q, k_ref, diag, high, total, m_ref, pk_ref, s0, s1, before_last=None):
    rows, dim = q.shape
    toks = own * BLK
    scale = math.log2(math.e) / math.sqrt(dim)
    width = STEP * BLK
    chunks = k_ref.shape[0] // width
    part, _ = lane_part(rows, toks)
    block8 = jnp.broadcast_to(lane_block(scal, part, own), (8, rows))
    diag = jnp.broadcast_to(diag, (8, rows))
    col = lax.broadcasted_iota(jnp.int32, (STEP, width), 1) // BLK
    mean = jnp.where(col == lax.broadcasted_iota(jnp.int32, (STEP, width), 0), 1.0 / BLK, 0.0)
    mean = mean.astype(k_ref.dtype)

    sub = lax.broadcasted_iota(jnp.int32, (STEP, LANES), 0)

    def fill(c, s_ref):
        k = k_ref[pl.ds(c * width, width), :]
        s = scores(k, q)
        s_ref[...] = s
        tops = [
            jnp.max(s[j * BLK : (j + 1) * BLK].reshape(BLK // 8, 8, rows), axis=0)
            for j in range(STEP)
        ]
        top = fold8(tops, jnp.maximum)
        at = pl.ds((which * chunks + c) * STEP, STEP)
        kb = jnp.zeros((STEP, LANES), jnp.int32)
        for j in range(STEP):
            kb = jnp.where(sub == j, order[slot(scal, own, which, c, j)], kb)
        kb = jnp.tile(kb, (1, rows // LANES))
        top = jnp.where(block8 > kb, top, jnp.where(block8 == kb, diag, MASKED))
        m_ref[at, :] = top
        kf = k.astype(jnp.float32)
        pk_ref[at, 0:dim] = fold_keys(kf, jnp.max, jnp.maximum)
        pk_ref[at, dim : 2 * dim] = fold_keys(kf, jnp.min, jnp.minimum)
        pk_ref[at, 2 * dim : 3 * dim] = lax.dot_general(
            mean, k, (((1,), (0,)), ((), ())), preferred_element_type=jnp.float32
        )
        return spread(top, jnp.maximum)

    def drain(c, s_ref, top, high, total):
        new = jnp.maximum(high, top)
        total = total * jnp.exp2((high - new) * scale)
        for j in range(STEP):
            fresh = tile_sum(s_ref[j * BLK : (j + 1) * BLK, :], new, scale)
            total = total + jnp.where(block8 > order[slot(scal, own, which, c, j)], fresh, 0.0)
        return new, total

    bufs = (s0, s1)
    top = fill(0, s0)
    for c in range(chunks):
        ahead = fill(c + 1, bufs[(c + 1) % 2]) if c + 1 < chunks else None
        if c + 1 == chunks and before_last is not None:
            before_last()
        high, total = drain(c, bufs[c % 2], top, high, total)
        top = ahead
    return high, total


def near_kernel(
    own, scal, order, q_ref, k_ref, diag_ref, total_ref,
    high_out, total_out, m_ref, pk_ref, s0, s1,
):
    diag = diag_ref[...]
    m_ref[...] = jnp.full(m_ref.shape, MASKED, jnp.float32)
    pk_ref[...] = jnp.zeros(pk_ref.shape, jnp.float32)
    high_out[...], total_out[...] = scan_keys(
        own, scal, order, 0, q_ref[...], k_ref, diag,
        jnp.broadcast_to(diag, high_out.shape), total_ref[...], m_ref, pk_ref, s0, s1,
    )


def far_kernel(
    own, which, scal, order, q_ref, k_ref, diag_ref, high_ref, total_ref, m_in, pk_in,
    high_out, total_out, m_ref, pk_ref, s0, s1,
):
    m_ref[...] = m_in[...]
    pk_ref[...] = pk_in[...]
    high_out[...], total_out[...] = scan_keys(
        own, scal, order, which, q_ref[...], k_ref, diag_ref[...],
        high_ref[...], total_ref[...], m_ref, pk_ref, s0, s1,
    )


def kernel(
    own, which, scal, order, q_ref, k_ref, ordv, diag_ref, high_ref, total_ref, m_in, pk_in,
    pq_ref, xq_ref, wk, t_ref, g_ref, m_ref, pk_ref, s0, s1,
):
    rows, dim = q_ref.shape
    toks = own * BLK
    group = rows // toks
    blocks = order.shape[0]
    length = scal[0]
    scale = math.log2(math.e) / math.sqrt(dim)
    part, pos = lane_part(rows, toks)
    block = lane_block(scal, part, own)
    m_ref[...] = m_in[...]
    pk_ref[...] = pk_in[...]
    row = lax.broadcasted_iota(jnp.int32, (COUNT, 1), 0)
    qblock = lane_block(scal, lax.rem(row, own), own)
    gate = {}

    def gate_forward():
        pq = pq_ref[...]
        xq = xq_ref[...]
        pk = pk_ref[...]
        xk = dot(pk, wk[...], ((1,), (0,)))
        rq = lax.rsqrt(jnp.mean(xq * xq, axis=1, keepdims=True) + EPS)
        rk = lax.rsqrt(jnp.mean(xk * xk, axis=1, keepdims=True) + EPS)
        uq = xq * rq
        uk = xk * rk
        gate_scale = 1.0 / math.sqrt(xq.shape[1])
        logits = dot(uq, uk, ((1,), (1,))) * gate_scale
        kblock = ordv[...]
        allowed = (kblock <= qblock) & (kblock * BLK < length)
        weights = jnp.where(allowed, jnp.exp(logits), 0.0)
        soft = weights / jnp.sum(weights, axis=1, keepdims=True)
        gate.update(pq=pq, pkt=jnp.transpose(pk), uq=uq, uk=uk, rq=rq, rk=rk, soft=soft)
        gate.update(scale=gate_scale)

    high, total = scan_keys(
        own, scal, order, which, q_ref[...], k_ref, diag_ref[...], high_ref[...],
        total_ref[...], m_ref, pk_ref, s0, s1, gate_forward,
    )

    log_total = jnp.log2(jnp.sum(total, axis=0, keepdims=True))
    depth = jnp.where(pos + block * BLK < length, (m_ref[...] - high[0:1]) * scale - log_total, MASKED)
    depth = jnp.max(jnp.transpose(depth).reshape(group * own, BLK, blocks), axis=1)
    pad = COUNT - group * own
    depth = jnp.concatenate([depth, jnp.full((pad, blocks), MASKED, jnp.float32)], axis=0)
    pooled = jnp.exp2(depth)
    good = (qblock * BLK < length) & (row < group * own)
    totals = jnp.sum(pooled, axis=1, keepdims=True)
    target = jnp.where(good, pooled / jnp.where(good, totals, 1.0), 0.0)
    place = lax.broadcasted_iota(jnp.int32, (blocks, blocks), 1)
    y, z = place // (4 * own), place // own % 4
    fy, fz = y % 2 != scal[1 + own], z % 2 != scal[2 + own]
    at = jnp.where(fy, 2, 0) + jnp.where(fz, 1, 0)
    at = ((at * 4 + y // 2) * 2 + z // 2) * own + place % own
    pick = jnp.where(lax.broadcasted_iota(jnp.int32, (blocks, blocks), 0) == at, 1.0, 0.0)
    laid = dot(target, pick, ((1,), (0,)))
    for h in range(group):
        t_ref[0, h] = laid[own * h : own * (h + 1)]

    dl = (jnp.where(good, gate["soft"], 0.0) - target) * gate["scale"]
    uq, uk, rq, rk = gate["uq"], gate["uk"], gate["rq"], gate["rk"]
    duq = dot(dl, uk, ((1,), (0,)))
    duk = dot(dl, uq, ((0,), (0,)))
    dxq = rq * (duq - uq * jnp.mean(duq * uq, axis=1, keepdims=True))
    dxk = rk * (duk - uk * jnp.mean(duk * uk, axis=1, keepdims=True))
    g_ref[0:dim, :] = dot(gate["pq"], dxq, ((0,), (0,)))
    g_ref[dim : 4 * dim, :] = dot(gate["pkt"], dxk, ((1,), (0,)))


def split_kernel(g_ref, q_ref, k_ref, sem):
    rows = q_ref.shape[0]
    copies = [
        pltpu.make_async_copy(g_ref.at[pl.ds(0, rows)], q_ref, sem.at[0]),
        pltpu.make_async_copy(g_ref.at[pl.ds(rows, k_ref.shape[0])], k_ref, sem.at[1]),
    ]
    for copy in copies:
        copy.start()
    for copy in copies:
        copy.wait()


def repeat_kernel(x_ref, o_ref, sem):
    copies = [
        pltpu.make_async_copy(x_ref, o_ref.at[i], sem.at[i]) for i in range(o_ref.shape[0])
    ]
    for copy in copies:
        copy.start()
    for copy in copies:
        copy.wait()


def body(queries, key_rows, block_order, conv_len, gate_wq, gate_wk):
    toks = queries.shape[1]
    group = queries.shape[2]
    dim = queries.shape[3]
    own = toks // BLK
    rows = group * toks
    blocks = block_order.shape[0]
    width = gate_wq.shape[1]
    key_own = key_rows[0, :, 0, :]
    ny, nz = lax.axis_size(Y), lax.axis_size(Z)
    spots = jnp.stack([lax.axis_index("yl"), lax.axis_index("zn")])
    peers = ny * nz // len(SETS)
    smem = pl.BlockSpec(memory_space=pltpu.SMEM)
    vmem = pl.BlockSpec(memory_space=pltpu.VMEM)
    anywhere = pl.BlockSpec(memory_space=pl.ANY)
    repeated = pl.pallas_call(
        repeat_kernel,
        out_shape=jax.ShapeDtypeStruct((peers, toks, dim), key_own.dtype),
        in_specs=[vmem],
        out_specs=anywhere,
        scratch_shapes=[pltpu.SemaphoreType.DMA((peers,))],
        name="repeat_keys",
    )(key_own)
    near = lax.all_to_all(repeated, FAR, 0, 0, tiled=True).reshape(peers * toks, dim)
    length = lax.dynamic_index_in_dim(conv_len, lax.axis_index(BATCH))
    mine = lax.dynamic_slice_in_dim(block_order, lax.axis_index(CTX) * own, own)
    scal = jnp.concatenate([length, mine, spots])
    q = jnp.transpose(queries[0], (1, 0, 2)).reshape(rows, dim)

    def f32(*shape):
        return jax.ShapeDtypeStruct(shape, jnp.float32)

    def near_core(*shape):
        return pltpu.VMEM(shape, jnp.float32)

    def pinned(*arrays):
        return [pltpu.with_memory_space_constraint(x, pltpu.VMEM) for x in arrays]

    first = pl.pallas_call(
        functools.partial(first_kernel, group),
        out_shape=(
            near_core(1, rows), near_core(8, rows), pltpu.VMEM((1, blocks), jnp.int32),
            near_core(COUNT, dim), near_core(COUNT, width),
        ),
        in_specs=[smem, smem] + [vmem] * 3,
        out_specs=(vmem,) * 5,
        name="own_block",
    )(scal, block_order, q, key_own, gate_wq)
    near, scal, first = lax.optimization_barrier((near, scal, first))
    high, total, ordv, pq, xq = first
    pairs = []
    for y in range(ny):
        for c in range(2):
            other = y + 1 if y % 2 == c else y - 1
            pairs.append((2 * y + c, 2 * (other % ny) + c))
    turn = [(z, z ^ 1) for z in range(nz)]
    by_z = lax.ppermute(near, Z, turn)
    by_y = lax.ppermute(near, Y + ("c",), pairs)
    by_yz = lax.ppermute(by_z, Y + ("c",), pairs)
    buffers = [pltpu.VMEM((STEP * BLK, rows), jnp.float32)] * 2
    state = (
        near_core(8, rows), near_core(8, rows), near_core(blocks, rows), near_core(blocks, 3 * dim)
    )
    seen = pl.pallas_call(
        functools.partial(near_kernel, own),
        out_shape=state,
        in_specs=[smem, smem] + [vmem] * 4,
        out_specs=(vmem,) * 4,
        scratch_shapes=buffers,
        name="teacher_near",
    )(scal, block_order, *pinned(q, near, high, total))
    for which, keys in ((1, by_z), (2, by_y)):
        seen = pl.pallas_call(
            functools.partial(far_kernel, own, which),
            out_shape=state,
            in_specs=[smem, smem] + [vmem] * 7,
            out_specs=(vmem,) * 4,
            scratch_shapes=buffers,
            name="teacher_far",
        )(scal, block_order, *pinned(q, keys, high, *seen))
    target, grads = pl.pallas_call(
        functools.partial(kernel, own, 3),
        out_shape=(f32(1, group, own, blocks), near_core(4 * dim, width)),
        in_specs=[smem, smem] + [vmem] * 11,
        out_specs=(vmem, vmem),
        scratch_shapes=[
            pltpu.VMEM((blocks, rows), jnp.float32),
            pltpu.VMEM((blocks, 3 * dim), jnp.float32),
            *buffers,
        ],
        name="teacher_gate",
    )(scal, block_order, *pinned(q, by_yz, ordv, high, *seen, pq, xq, gate_wk))

    parts = lax.axis_size(SCATTER)
    rest = lax.axis_size(REST)
    piece = 4 * dim // parts
    share = lax.all_to_all(grads.reshape(parts, piece, width), SCATTER, 0, 0, tiled=True)
    share = jnp.sum(share, axis=0)
    share = lax.all_to_all(
        jnp.broadcast_to(share[None], (rest, piece, width)), REST, 0, 0, tiled=True
    )
    share = jnp.sum(share, axis=0)
    grads = lax.all_to_all(
        jnp.broadcast_to(share[None], (parts, piece, width)), SCATTER, 0, 0, tiled=True
    ).reshape(4 * dim, width)
    grad_wq, grad_wk = pl.pallas_call(
        split_kernel,
        out_shape=(f32(dim, width), f32(3 * dim, width)),
        in_specs=[vmem],
        out_specs=(anywhere, anywhere),
        scratch_shapes=[pltpu.SemaphoreType.DMA((2,))],
        name="split_grads",
    )(*pinned(grads))
    return target, grad_wq, grad_wk


def solution(mesh):
    names = Y + Z + ("x",) + BATCH
    fine = Mesh(mesh.devices.reshape(4, 2, 2, 2, 4, 2, 2), names)
    rows = P(BATCH, CTX, "x", None)
    return jax.shard_map(
        body,
        mesh=fine,
        in_specs=(rows, rows, P(), P(), P(), P()),
        out_specs=(P(BATCH, "x", CTX, None), P(), P()),
        check_vma=False,
    )
```

```python
import functools
import math

import jax
import jax.numpy as jnp
from jax import lax
from jax.experimental import pallas as pl
from jax.experimental.pallas import tpu as pltpu
from jax.sharding import Mesh
from jax.sharding import PartitionSpec as P

BLK = 64
LANES = 128
COUNT = 16
STEP = 8
MASKED = -1e30
EPS = 1e-06
HIGHEST = lax.Precision.HIGHEST


Y = ("yh", "yl")
Z = ("zm", "zn")
CTX = Y + Z
FAR = ("yh", "zm")
BATCH = ("zh", "c")
SETS = ((0, 0), (0, 1), (1, 0), (1, 1))
SHARE = 2
SCATTER = ("x", "yl", "zn", "c")
REST = ("yh", "zh", "zm")


def dot(a, b, dims):
    return lax.dot_general(
        a, b, (dims, ((), ())), precision=HIGHEST, preferred_element_type=jnp.float32
    )


def scores(k, q):
    return lax.dot_general(k, q, (((1,), (1,)), ((), ())), preferred_element_type=jnp.float32)


def lane_part(rows, toks):
    tok = lax.rem(lax.broadcasted_iota(jnp.int32, (1, rows), 1), toks)
    return tok // BLK, lax.rem(tok, BLK)


def lane_block(scal, part, own):
    block = jnp.zeros_like(part)
    for i in range(own):
        block = jnp.where(part == i, scal[1 + i], block)
    return block


def tile_sum(s, new, scale):
    e = jnp.exp2((s.reshape(s.shape[0] // 8, 8, s.shape[1]) - new) * scale)
    return jnp.sum(e, axis=0)


def spread(x, op):
    for shift in (4, 2, 1):
        x = op(x, pltpu.roll(x, shift, 0))
    return x


def fold8(parts, op):
    sub = lax.broadcasted_iota(jnp.int32, parts[0].shape, 0)
    low = sub < 4
    t = []
    for i in range(4):
        a, b = parts[i], parts[i + 4]
        t.append(op(jnp.where(low, a, b), pltpu.roll(jnp.where(low, b, a), 4, 0)))
    for shift in (2, 1):
        half = len(t) // 2
        low = lax.rem(sub, 2 * shift) < shift
        t = [
            jnp.where(
                low,
                op(t[i], pltpu.roll(t[i], 8 - shift, 0)),
                op(t[i + half], pltpu.roll(t[i + half], shift, 0)),
            )
            for i in range(half)
        ]
    return t[0]


def fold_keys(k, reduce, op):
    parts = [
        reduce(k[j * BLK : (j + 1) * BLK].reshape(BLK // 8, 8, k.shape[1]), axis=0)
        for j in range(STEP)
    ]
    return fold8(parts, op)


def first_kernel(group, scal, order, q_ref, k_ref, wq, high_ref, total_ref, ord_out, pq_ref, xq_ref):
    rows, dim = q_ref.shape
    toks = rows // group
    own = toks // BLK
    scale = math.log2(math.e) / math.sqrt(dim)
    part, pos = lane_part(rows, toks)
    q = q_ref[...]
    s = scores(k_ref[...], q)
    tile = s[0:BLK]
    for i in range(1, own):
        tile = jnp.where(part == i, s[i * BLK : (i + 1) * BLK], tile)
    tile = jnp.where(lax.broadcasted_iota(jnp.int32, (BLK, rows), 0) <= pos, tile, MASKED)
    high = jnp.max(tile, axis=0, keepdims=True)
    high_ref[...] = high
    total_ref[...] = tile_sum(tile, high, scale)
    pq = jnp.sum(q.astype(jnp.float32).reshape(group * own, BLK, dim), axis=1) * (1.0 / BLK)
    pq = jnp.concatenate([pq, jnp.zeros((COUNT - group * own, dim), jnp.float32)], axis=0)
    pq_ref[...] = pq
    lane = lax.broadcasted_iota(jnp.int32, ord_out.shape, 1)
    ids = jnp.zeros(ord_out.shape, jnp.int32)
    share = ord_out.shape[1] // len(SETS)
    for i in range(ord_out.shape[1]):
        at = slot(scal, own, i // share, i % share // STEP, i % STEP)
        ids = jnp.where(lane == i, order[at], ids)
    ord_out[...] = ids
    xq_ref[...] = dot(pq, wq[...], ((1,), (0,)))


def slot(scal, own, which, c, j):
    dy, dz = SETS[which]
    fy = scal[1 + own] if dy == 0 else 1 - scal[1 + own]
    fz = scal[2 + own] if dz == 0 else 1 - scal[2 + own]
    y = 2 * (2 * c + j // (2 * own)) + fy
    z = 2 * (j // own % 2) + fz
    return (y * 4 + z) * own + j % own


def scan_keys(own, scal, order, parts, q, diag, high, total, m_ref, pk_ref, s0, s1, before_last=None):
    rows, dim = q.shape
    toks = own * BLK
    scale = math.log2(math.e) / math.sqrt(dim)
    width = STEP * BLK
    chunks = [
        (which, first + c, k_ref, c * width)
        for which, first, k_ref in parts
        for c in range(k_ref.shape[0] // width)
    ]
    part, _ = lane_part(rows, toks)
    block8 = jnp.broadcast_to(lane_block(scal, part, own), (8, rows))
    diag = jnp.broadcast_to(diag, (8, rows))
    col = lax.broadcasted_iota(jnp.int32, (STEP, width), 1) // BLK
    mean = jnp.where(col == lax.broadcasted_iota(jnp.int32, (STEP, width), 0), 1.0 / BLK, 0.0)
    mean = mean.astype(q.dtype)

    sub = lax.broadcasted_iota(jnp.int32, (STEP, LANES), 0)

    def fill(i, s_ref):
        which, c, k_ref, row = chunks[i]
        k = k_ref[row : row + width, :]
        s = scores(k, q)
        s_ref[...] = s
        tops = [
            jnp.max(s[j * BLK : (j + 1) * BLK].reshape(BLK // 8, 8, rows), axis=0)
            for j in range(STEP)
        ]
        top = fold8(tops, jnp.maximum)
        at = pl.ds((which * SHARE + c) * STEP, STEP)
        kb = jnp.zeros((STEP, LANES), jnp.int32)
        for j in range(STEP):
            kb = jnp.where(sub == j, order[slot(scal, own, which, c, j)], kb)
        kb = jnp.tile(kb, (1, rows // LANES))
        top = jnp.where(block8 > kb, top, jnp.where(block8 == kb, diag, MASKED))
        m_ref[at, :] = top
        kf = k.astype(jnp.float32)
        pk_ref[at, 0:dim] = fold_keys(kf, jnp.max, jnp.maximum)
        pk_ref[at, dim : 2 * dim] = fold_keys(kf, jnp.min, jnp.minimum)
        pk_ref[at, 2 * dim : 3 * dim] = lax.dot_general(
            mean, k, (((1,), (0,)), ((), ())), preferred_element_type=jnp.float32
        )
        return spread(top, jnp.maximum)

    def drain(i, s_ref, top, high, total):
        which, c = chunks[i][:2]
        new = jnp.maximum(high, top)
        total = total * jnp.exp2((high - new) * scale)
        for j in range(STEP):
            fresh = tile_sum(s_ref[j * BLK : (j + 1) * BLK, :], new, scale)
            total = total + jnp.where(block8 > order[slot(scal, own, which, c, j)], fresh, 0.0)
        return new, total

    bufs = (s0, s1)
    top = fill(0, s0)
    for i in range(len(chunks)):
        ahead = fill(i + 1, bufs[(i + 1) % 2]) if i + 1 < len(chunks) else None
        if i + 1 == len(chunks) and before_last is not None:
            before_last()
        high, total = drain(i, bufs[i % 2], top, high, total)
        top = ahead
    return high, total


def near_kernel(
    own, scal, order, q_ref, k_ref, diag_ref, total_ref,
    high_out, total_out, m_ref, pk_ref, s0, s1,
):
    diag = diag_ref[...]
    m_ref[...] = jnp.full(m_ref.shape, MASKED, jnp.float32)
    pk_ref[...] = jnp.zeros(pk_ref.shape, jnp.float32)
    high_out[...], total_out[...] = scan_keys(
        own, scal, order, [(0, 0, k_ref)], q_ref[...], diag,
        jnp.broadcast_to(diag, high_out.shape), total_ref[...], m_ref, pk_ref, s0, s1,
    )


def far_kernel(
    own, scal, order, q_ref, z_ref, y_ref, diag_ref, high_ref, total_ref, m_in, pk_in,
    high_out, total_out, m_ref, pk_ref, s0, s1,
):
    m_ref[...] = m_in[...]
    pk_ref[...] = pk_in[...]
    high_out[...], total_out[...] = scan_keys(
        own, scal, order, [(1, 0, z_ref), (2, 0, y_ref)], q_ref[...], diag_ref[...],
        high_ref[...], total_ref[...], m_ref, pk_ref, s0, s1,
    )


def kernel(
    own, scal, order, q_ref, a_ref, b_ref, ordv, diag_ref, high_ref, total_ref, m_in, pk_in,
    pq_ref, xq_ref, wk, t_ref, g_ref, m_ref, pk_ref, s0, s1,
):
    rows, dim = q_ref.shape
    toks = own * BLK
    group = rows // toks
    blocks = order.shape[0]
    length = scal[0]
    scale = math.log2(math.e) / math.sqrt(dim)
    part, pos = lane_part(rows, toks)
    block = lane_block(scal, part, own)
    m_ref[...] = m_in[...]
    pk_ref[...] = pk_in[...]
    row = lax.broadcasted_iota(jnp.int32, (COUNT, 1), 0)
    qblock = lane_block(scal, lax.rem(row, own), own)
    gate = {}

    def gate_forward():
        pq = pq_ref[...]
        xq = xq_ref[...]
        pk = pk_ref[...]
        xk = dot(pk, wk[...], ((1,), (0,)))
        rq = lax.rsqrt(jnp.mean(xq * xq, axis=1, keepdims=True) + EPS)
        rk = lax.rsqrt(jnp.mean(xk * xk, axis=1, keepdims=True) + EPS)
        uq = xq * rq
        uk = xk * rk
        gate_scale = 1.0 / math.sqrt(xq.shape[1])
        logits = dot(uq, uk, ((1,), (1,))) * gate_scale
        kblock = ordv[...]
        allowed = (kblock <= qblock) & (kblock * BLK < length)
        weights = jnp.where(allowed, jnp.exp(logits), 0.0)
        soft = weights / jnp.sum(weights, axis=1, keepdims=True)
        gate.update(pq=pq, pkt=jnp.transpose(pk), uq=uq, uk=uk, rq=rq, rk=rk, soft=soft)
        gate.update(scale=gate_scale)

    high, total = scan_keys(
        own, scal, order, [(3, 0, a_ref), (3, 1, b_ref)], q_ref[...], diag_ref[...], high_ref[...],
        total_ref[...], m_ref, pk_ref, s0, s1, gate_forward,
    )

    log_total = jnp.log2(jnp.sum(total, axis=0, keepdims=True))
    depth = jnp.where(pos + block * BLK < length, (m_ref[...] - high[0:1]) * scale - log_total, MASKED)
    depth = jnp.max(jnp.transpose(depth).reshape(group * own, BLK, blocks), axis=1)
    pad = COUNT - group * own
    depth = jnp.concatenate([depth, jnp.full((pad, blocks), MASKED, jnp.float32)], axis=0)
    pooled = jnp.exp2(depth)
    good = (qblock * BLK < length) & (row < group * own)
    totals = jnp.sum(pooled, axis=1, keepdims=True)
    target = jnp.where(good, pooled / jnp.where(good, totals, 1.0), 0.0)
    place = lax.broadcasted_iota(jnp.int32, (blocks, blocks), 1)
    y, z = place // (4 * own), place // own % 4
    fy, fz = y % 2 != scal[1 + own], z % 2 != scal[2 + own]
    at = jnp.where(fy, 2, 0) + jnp.where(fz, 1, 0)
    at = ((at * 4 + y // 2) * 2 + z // 2) * own + place % own
    pick = jnp.where(lax.broadcasted_iota(jnp.int32, (blocks, blocks), 0) == at, 1.0, 0.0)
    laid = dot(target, pick, ((1,), (0,)))
    for h in range(group):
        t_ref[0, h] = laid[own * h : own * (h + 1)]

    dl = (jnp.where(good, gate["soft"], 0.0) - target) * gate["scale"]
    uq, uk, rq, rk = gate["uq"], gate["uk"], gate["rq"], gate["rk"]
    duq = dot(dl, uk, ((1,), (0,)))
    duk = dot(dl, uq, ((0,), (0,)))
    dxq = rq * (duq - uq * jnp.mean(duq * uq, axis=1, keepdims=True))
    dxk = rk * (duk - uk * jnp.mean(duk * uk, axis=1, keepdims=True))
    g_ref[0:dim, :] = dot(gate["pq"], dxq, ((0,), (0,)))
    g_ref[dim : 4 * dim, :] = dot(gate["pkt"], dxk, ((1,), (0,)))


def split_kernel(g_ref, q_ref, k_ref, sem):
    rows = q_ref.shape[0]
    copies = [
        pltpu.make_async_copy(g_ref.at[pl.ds(0, rows)], q_ref, sem.at[0]),
        pltpu.make_async_copy(g_ref.at[pl.ds(rows, k_ref.shape[0])], k_ref, sem.at[1]),
    ]
    for copy in copies:
        copy.start()
    for copy in copies:
        copy.wait()


def repeat_kernel(x_ref, o_ref, sem):
    copies = [
        pltpu.make_async_copy(x_ref, o_ref.at[i], sem.at[i]) for i in range(o_ref.shape[0])
    ]
    for copy in copies:
        copy.start()
    for copy in copies:
        copy.wait()


def body(queries, key_rows, block_order, conv_len, gate_wq, gate_wk):
    toks = queries.shape[1]
    group = queries.shape[2]
    dim = queries.shape[3]
    own = toks // BLK
    rows = group * toks
    blocks = block_order.shape[0]
    width = gate_wq.shape[1]
    key_own = key_rows[0, :, 0, :]
    ny, nz = lax.axis_size(Y), lax.axis_size(Z)
    spots = jnp.stack([lax.axis_index("yl"), lax.axis_index("zn")])
    peers = ny * nz // len(SETS)
    smem = pl.BlockSpec(memory_space=pltpu.SMEM)
    vmem = pl.BlockSpec(memory_space=pltpu.VMEM)
    anywhere = pl.BlockSpec(memory_space=pl.ANY)
    repeated = pl.pallas_call(
        repeat_kernel,
        out_shape=jax.ShapeDtypeStruct((peers, toks, dim), key_own.dtype),
        in_specs=[vmem],
        out_specs=anywhere,
        scratch_shapes=[pltpu.SemaphoreType.DMA((peers,))],
        name="repeat_keys",
    )(key_own)
    near = lax.all_to_all(repeated, FAR, 0, 0, tiled=True).reshape(peers * toks, dim)
    length = lax.dynamic_index_in_dim(conv_len, lax.axis_index(BATCH))
    mine = lax.dynamic_slice_in_dim(block_order, lax.axis_index(CTX) * own, own)
    scal = jnp.concatenate([length, mine, spots])
    q = jnp.transpose(queries[0], (1, 0, 2)).reshape(rows, dim)

    def f32(*shape):
        return jax.ShapeDtypeStruct(shape, jnp.float32)

    def near_core(*shape):
        return pltpu.VMEM(shape, jnp.float32)

    def pinned(*arrays):
        return [pltpu.with_memory_space_constraint(x, pltpu.VMEM) for x in arrays]

    first = pl.pallas_call(
        functools.partial(first_kernel, group),
        out_shape=(
            near_core(1, rows), near_core(8, rows), pltpu.VMEM((1, blocks), jnp.int32),
            near_core(COUNT, dim), near_core(COUNT, width),
        ),
        in_specs=[smem, smem] + [vmem] * 3,
        out_specs=(vmem,) * 5,
        name="own_block",
    )(scal, block_order, q, key_own, gate_wq)
    near, scal, first = lax.optimization_barrier((near, scal, first))
    high, total, ordv, pq, xq = first
    pairs = []
    for y in range(ny):
        for c in range(2):
            other = y + 1 if y % 2 == c else y - 1
            pairs.append((2 * y + c, 2 * (other % ny) + c))
    turn = [(z, z ^ 1) for z in range(nz)]
    by_z = lax.ppermute(near, Z, turn)
    by_y = lax.ppermute(near, Y + ("c",), pairs)
    buffers = [pltpu.VMEM((STEP * BLK, rows), jnp.float32)] * 2
    state = (
        near_core(8, rows), near_core(8, rows), near_core(blocks, rows), near_core(blocks, 3 * dim)
    )
    seen = pl.pallas_call(
        functools.partial(near_kernel, own),
        out_shape=state,
        in_specs=[smem, smem] + [vmem] * 4,
        out_specs=(vmem,) * 4,
        scratch_shapes=buffers,
        name="teacher_near",
    )(scal, block_order, *pinned(q, near, high, total))
    seen, by_z = lax.optimization_barrier((seen, by_z))
    cut = near.shape[0] // 2
    low = lax.ppermute(by_z[:cut], Y + ("c",), pairs)
    top = lax.ppermute(by_y[cut:], Z, turn)
    seen = pl.pallas_call(
        functools.partial(far_kernel, own),
        out_shape=state,
        in_specs=[smem, smem] + [vmem] * 8,
        out_specs=(vmem,) * 4,
        scratch_shapes=buffers,
        name="teacher_far",
    )(scal, block_order, *pinned(q, by_z, by_y, high, *seen))
    target, grads = pl.pallas_call(
        functools.partial(kernel, own),
        out_shape=(f32(1, group, own, blocks), near_core(4 * dim, width)),
        in_specs=[smem, smem] + [vmem] * 12,
        out_specs=(vmem, vmem),
        scratch_shapes=[
            pltpu.VMEM((blocks, rows), jnp.float32),
            pltpu.VMEM((blocks, 3 * dim), jnp.float32),
            *buffers,
        ],
        name="teacher_gate",
    )(scal, block_order, *pinned(q, low, top, ordv, high, *seen, pq, xq, gate_wk))

    parts = lax.axis_size(SCATTER)
    rest = lax.axis_size(REST)
    piece = 4 * dim // parts
    share = lax.all_to_all(grads.reshape(parts, piece, width), SCATTER, 0, 0, tiled=True)
    share = jnp.sum(share, axis=0)
    share = lax.all_to_all(
        jnp.broadcast_to(share[None], (rest, piece, width)), REST, 0, 0, tiled=True
    )
    share = jnp.sum(share, axis=0)
    grads = lax.all_to_all(
        jnp.broadcast_to(share[None], (parts, piece, width)), SCATTER, 0, 0, tiled=True
    ).reshape(4 * dim, width)
    grad_wq, grad_wk = pl.pallas_call(
        split_kernel,
        out_shape=(f32(dim, width), f32(3 * dim, width)),
        in_specs=[vmem],
        out_specs=(anywhere, anywhere),
        scratch_shapes=[pltpu.SemaphoreType.DMA((2,))],
        name="split_grads",
    )(*pinned(grads))
    return target, grad_wq, grad_wk


def solution(mesh):
    names = Y + Z + ("x",) + BATCH
    fine = Mesh(mesh.devices.reshape(4, 2, 2, 2, 4, 2, 2), names)
    rows = P(BATCH, CTX, "x", None)
    return jax.shard_map(
        body,
        mesh=fine,
        in_specs=(rows, rows, P(), P(), P(), P()),
        out_specs=(P(BATCH, "x", CTX, None), P(), P()),
        check_vma=False,
    )
```

```python
import functools
import math

import jax
import jax.numpy as jnp
from jax import lax
from jax.experimental import pallas as pl
from jax.experimental.pallas import tpu as pltpu
from jax.sharding import Mesh
from jax.sharding import PartitionSpec as P

BLK = 64
LANES = 128
COUNT = 16
STEP = 8
MASKED = -1e30
EPS = 1e-06
HIGHEST = lax.Precision.HIGHEST


Y = ("yh", "yl")
Z = ("zm", "zn")
CTX = Y + Z
FAR = ("yh", "zm")
BATCH = ("zh", "c")
SETS = ((0, 0), (0, 1), (1, 0), (1, 1))
SHARE = 2
SCATTER = ("x", "yl", "zn", "c")
REST = ("yh", "zh", "zm")


def dot(a, b, dims):
    return lax.dot_general(
        a, b, (dims, ((), ())), precision=HIGHEST, preferred_element_type=jnp.float32
    )


def scores(k, q):
    return lax.dot_general(k, q, (((1,), (1,)), ((), ())), preferred_element_type=jnp.float32)


def lane_part(rows, toks):
    tok = lax.rem(lax.broadcasted_iota(jnp.int32, (1, rows), 1), toks)
    return tok // BLK, lax.rem(tok, BLK)


def lane_block(scal, part, own):
    block = jnp.zeros_like(part)
    for i in range(own):
        block = jnp.where(part == i, scal[1 + i], block)
    return block


def tile_sum(s, new, scale):
    e = jnp.exp2((s.reshape(s.shape[0] // 8, 8, s.shape[1]) - new) * scale)
    return jnp.sum(e, axis=0)


def spread(x, op):
    for shift in (4, 2, 1):
        x = op(x, pltpu.roll(x, shift, 0))
    return x


def fold8(parts, op):
    sub = lax.broadcasted_iota(jnp.int32, parts[0].shape, 0)
    low = sub < 4
    t = []
    for i in range(4):
        a, b = parts[i], parts[i + 4]
        t.append(op(jnp.where(low, a, b), pltpu.roll(jnp.where(low, b, a), 4, 0)))
    for shift in (2, 1):
        half = len(t) // 2
        low = lax.rem(sub, 2 * shift) < shift
        t = [
            jnp.where(
                low,
                op(t[i], pltpu.roll(t[i], 8 - shift, 0)),
                op(t[i + half], pltpu.roll(t[i + half], shift, 0)),
            )
            for i in range(half)
        ]
    return t[0]


def fold_keys(k, reduce, op):
    parts = [
        reduce(k[j * BLK : (j + 1) * BLK].reshape(BLK // 8, 8, k.shape[1]), axis=0)
        for j in range(STEP)
    ]
    return fold8(parts, op)


def first_kernel(group, scal, order, q_ref, k_ref, wq, high_ref, total_ref, ord_out, pq_ref, xq_ref):
    rows, dim = q_ref.shape
    toks = rows // group
    own = toks // BLK
    scale = math.log2(math.e) / math.sqrt(dim)
    part, pos = lane_part(rows, toks)
    q = q_ref[...]
    s = scores(k_ref[...], q)
    tile = s[0:BLK]
    for i in range(1, own):
        tile = jnp.where(part == i, s[i * BLK : (i + 1) * BLK], tile)
    tile = jnp.where(lax.broadcasted_iota(jnp.int32, (BLK, rows), 0) <= pos, tile, MASKED)
    high = jnp.max(tile, axis=0, keepdims=True)
    high_ref[...] = high
    total_ref[...] = tile_sum(tile, high, scale)
    pq = jnp.sum(q.astype(jnp.float32).reshape(group * own, BLK, dim), axis=1) * (1.0 / BLK)
    pq = jnp.concatenate([pq, jnp.zeros((COUNT - group * own, dim), jnp.float32)], axis=0)
    pq_ref[...] = pq
    lane = lax.broadcasted_iota(jnp.int32, ord_out.shape, 1)
    ids = jnp.zeros(ord_out.shape, jnp.int32)
    share = ord_out.shape[1] // len(SETS)
    for i in range(ord_out.shape[1]):
        at = slot(scal, own, i // share, i % share // STEP, i % STEP)
        ids = jnp.where(lane == i, order[at], ids)
    ord_out[...] = ids
    xq_ref[...] = dot(pq, wq[...], ((1,), (0,)))


def slot(scal, own, which, c, j):
    dy, dz = SETS[which]
    fy = scal[1 + own] if dy == 0 else 1 - scal[1 + own]
    fz = scal[2 + own] if dz == 0 else 1 - scal[2 + own]
    y = 2 * (2 * c + j // (2 * own)) + fy
    z = 2 * (j // own % 2) + fz
    return (y * 4 + z) * own + j % own


def scan_keys(own, scal, order, parts, q, diag, high, total, m_ref, pk_ref, s0, s1, before_last=None):
    rows, dim = q.shape
    toks = own * BLK
    scale = math.log2(math.e) / math.sqrt(dim)
    width = STEP * BLK
    chunks = [
        (which, first + c, k_ref, c * width)
        for which, first, k_ref in parts
        for c in range(k_ref.shape[0] // width)
    ]
    part, _ = lane_part(rows, toks)
    block8 = jnp.broadcast_to(lane_block(scal, part, own), (8, rows))
    diag = jnp.broadcast_to(diag, (8, rows))
    col = lax.broadcasted_iota(jnp.int32, (STEP, width), 1) // BLK
    mean = jnp.where(col == lax.broadcasted_iota(jnp.int32, (STEP, width), 0), 1.0 / BLK, 0.0)
    mean = mean.astype(q.dtype)

    sub = lax.broadcasted_iota(jnp.int32, (STEP, LANES), 0)

    def fill(i, s_ref):
        which, c, k_ref, row = chunks[i]
        k = k_ref[row : row + width, :]
        s = scores(k, q)
        s_ref[...] = s
        tops = [
            jnp.max(s[j * BLK : (j + 1) * BLK].reshape(BLK // 8, 8, rows), axis=0)
            for j in range(STEP)
        ]
        top = fold8(tops, jnp.maximum)
        at = pl.ds((which * SHARE + c) * STEP, STEP)
        kb = jnp.zeros((STEP, LANES), jnp.int32)
        for j in range(STEP):
            kb = jnp.where(sub == j, order[slot(scal, own, which, c, j)], kb)
        kb = jnp.tile(kb, (1, rows // LANES))
        top = jnp.where(block8 > kb, top, jnp.where(block8 == kb, diag, MASKED))
        m_ref[at, :] = top
        kf = k.astype(jnp.float32)
        pk_ref[at, 0:dim] = fold_keys(kf, jnp.max, jnp.maximum)
        pk_ref[at, dim : 2 * dim] = fold_keys(kf, jnp.min, jnp.minimum)
        pk_ref[at, 2 * dim : 3 * dim] = lax.dot_general(
            mean, k, (((1,), (0,)), ((), ())), preferred_element_type=jnp.float32
        )
        return spread(top, jnp.maximum)

    def drain(i, s_ref, top, high, total):
        which, c = chunks[i][:2]
        new = jnp.maximum(high, top)
        total = total * jnp.exp2((high - new) * scale)
        for j in range(STEP):
            fresh = tile_sum(s_ref[j * BLK : (j + 1) * BLK, :], new, scale)
            total = total + jnp.where(block8 > order[slot(scal, own, which, c, j)], fresh, 0.0)
        return new, total

    bufs = (s0, s1)
    top = fill(0, s0)
    for i in range(len(chunks)):
        ahead = fill(i + 1, bufs[(i + 1) % 2]) if i + 1 < len(chunks) else None
        if i + 1 == len(chunks) and before_last is not None:
            before_last()
        high, total = drain(i, bufs[i % 2], top, high, total)
        top = ahead
    return high, total


def near_kernel(
    own, scal, order, q_ref, k_ref, diag_ref, total_ref,
    high_out, total_out, m_ref, pk_ref, s0, s1,
):
    diag = diag_ref[...]
    m_ref[...] = jnp.full(m_ref.shape, MASKED, jnp.float32)
    pk_ref[...] = jnp.zeros(pk_ref.shape, jnp.float32)
    high_out[...], total_out[...] = scan_keys(
        own, scal, order, [(0, 0, k_ref)], q_ref[...], diag,
        jnp.broadcast_to(diag, high_out.shape), total_ref[...], m_ref, pk_ref, s0, s1,
    )


def far_kernel(
    own, scal, order, q_ref, z_ref, y_ref, diag_ref, high_ref, total_ref, m_in, pk_in,
    high_out, total_out, m_ref, pk_ref, s0, s1,
):
    m_ref[...] = m_in[...]
    pk_ref[...] = pk_in[...]
    high_out[...], total_out[...] = scan_keys(
        own, scal, order, [(1, 0, z_ref), (2, 0, y_ref)], q_ref[...], diag_ref[...],
        high_ref[...], total_ref[...], m_ref, pk_ref, s0, s1,
    )


def kernel(
    own, scal, order, q_ref, k_ref, ordv, diag_ref, high_ref, total_ref, m_in, pk_in,
    pq_ref, xq_ref, wk, t_ref, g_ref, m_ref, pk_ref, s0, s1,
):
    rows, dim = q_ref.shape
    toks = own * BLK
    group = rows // toks
    blocks = order.shape[0]
    length = scal[0]
    scale = math.log2(math.e) / math.sqrt(dim)
    part, pos = lane_part(rows, toks)
    block = lane_block(scal, part, own)
    m_ref[...] = m_in[...]
    pk_ref[...] = pk_in[...]
    row = lax.broadcasted_iota(jnp.int32, (COUNT, 1), 0)
    qblock = lane_block(scal, lax.rem(row, own), own)
    gate = {}

    def gate_forward():
        pq = pq_ref[...]
        xq = xq_ref[...]
        pk = pk_ref[...]
        xk = dot(pk, wk[...], ((1,), (0,)))
        rq = lax.rsqrt(jnp.mean(xq * xq, axis=1, keepdims=True) + EPS)
        rk = lax.rsqrt(jnp.mean(xk * xk, axis=1, keepdims=True) + EPS)
        uq = xq * rq
        uk = xk * rk
        gate_scale = 1.0 / math.sqrt(xq.shape[1])
        logits = dot(uq, uk, ((1,), (1,))) * gate_scale
        kblock = ordv[...]
        allowed = (kblock <= qblock) & (kblock * BLK < length)
        weights = jnp.where(allowed, jnp.exp(logits), 0.0)
        soft = weights / jnp.sum(weights, axis=1, keepdims=True)
        gate.update(pq=pq, pkt=jnp.transpose(pk), uq=uq, uk=uk, rq=rq, rk=rk, soft=soft)
        gate.update(scale=gate_scale)

    high, total = scan_keys(
        own, scal, order, [(3, 0, k_ref)], q_ref[...], diag_ref[...], high_ref[...],
        total_ref[...], m_ref, pk_ref, s0, s1, gate_forward,
    )

    log_total = jnp.log2(jnp.sum(total, axis=0, keepdims=True))
    depth = jnp.where(pos + block * BLK < length, (m_ref[...] - high[0:1]) * scale - log_total, MASKED)
    depth = jnp.max(jnp.transpose(depth).reshape(group * own, BLK, blocks), axis=1)
    pad = COUNT - group * own
    depth = jnp.concatenate([depth, jnp.full((pad, blocks), MASKED, jnp.float32)], axis=0)
    pooled = jnp.exp2(depth)
    good = (qblock * BLK < length) & (row < group * own)
    totals = jnp.sum(pooled, axis=1, keepdims=True)
    target = jnp.where(good, pooled / jnp.where(good, totals, 1.0), 0.0)
    place = lax.broadcasted_iota(jnp.int32, (blocks, blocks), 1)
    y, z = place // (4 * own), place // own % 4
    fy, fz = y % 2 != scal[1 + own], z % 2 != scal[2 + own]
    at = jnp.where(fy, 2, 0) + jnp.where(fz, 1, 0)
    at = ((at * 4 + y // 2) * 2 + z // 2) * own + place % own
    pick = jnp.where(lax.broadcasted_iota(jnp.int32, (blocks, blocks), 0) == at, 1.0, 0.0)
    laid = dot(target, pick, ((1,), (0,)))
    for h in range(group):
        t_ref[0, h] = laid[own * h : own * (h + 1)]

    dl = (jnp.where(good, gate["soft"], 0.0) - target) * gate["scale"]
    uq, uk, rq, rk = gate["uq"], gate["uk"], gate["rq"], gate["rk"]
    duq = dot(dl, uk, ((1,), (0,)))
    duk = dot(dl, uq, ((0,), (0,)))
    dxq = rq * (duq - uq * jnp.mean(duq * uq, axis=1, keepdims=True))
    dxk = rk * (duk - uk * jnp.mean(duk * uk, axis=1, keepdims=True))
    g_ref[0:dim, :] = dot(gate["pq"], dxq, ((0,), (0,)))
    g_ref[dim : 4 * dim, :] = dot(gate["pkt"], dxk, ((1,), (0,)))


def split_kernel(g_ref, q_ref, k_ref, sem):
    rows = q_ref.shape[0]
    copies = [
        pltpu.make_async_copy(g_ref.at[pl.ds(0, rows)], q_ref, sem.at[0]),
        pltpu.make_async_copy(g_ref.at[pl.ds(rows, k_ref.shape[0])], k_ref, sem.at[1]),
    ]
    for copy in copies:
        copy.start()
    for copy in copies:
        copy.wait()


def repeat_kernel(x_ref, o_ref, sem):
    copies = [
        pltpu.make_async_copy(x_ref, o_ref.at[i], sem.at[i]) for i in range(o_ref.shape[0])
    ]
    for copy in copies:
        copy.start()
    for copy in copies:
        copy.wait()


def body(queries, key_rows, block_order, conv_len, gate_wq, gate_wk):
    toks = queries.shape[1]
    group = queries.shape[2]
    dim = queries.shape[3]
    own = toks // BLK
    rows = group * toks
    blocks = block_order.shape[0]
    width = gate_wq.shape[1]
    key_own = key_rows[0, :, 0, :]
    ny, nz = lax.axis_size(Y), lax.axis_size(Z)
    spots = jnp.stack([lax.axis_index("yl"), lax.axis_index("zn")])
    peers = ny * nz // len(SETS)
    smem = pl.BlockSpec(memory_space=pltpu.SMEM)
    vmem = pl.BlockSpec(memory_space=pltpu.VMEM)
    anywhere = pl.BlockSpec(memory_space=pl.ANY)
    repeated = pl.pallas_call(
        repeat_kernel,
        out_shape=jax.ShapeDtypeStruct((peers, toks, dim), key_own.dtype),
        in_specs=[vmem],
        out_specs=anywhere,
        scratch_shapes=[pltpu.SemaphoreType.DMA((peers,))],
        name="repeat_keys",
    )(key_own)
    near = lax.all_to_all(repeated, FAR, 0, 0, tiled=True).reshape(peers * toks, dim)
    length = lax.dynamic_index_in_dim(conv_len, lax.axis_index(BATCH))
    mine = lax.dynamic_slice_in_dim(block_order, lax.axis_index(CTX) * own, own)
    scal = jnp.concatenate([length, mine, spots])
    q = jnp.transpose(queries[0], (1, 0, 2)).reshape(rows, dim)

    def f32(*shape):
        return jax.ShapeDtypeStruct(shape, jnp.float32)

    def near_core(*shape):
        return pltpu.VMEM(shape, jnp.float32)

    def pinned(*arrays):
        return [pltpu.with_memory_space_constraint(x, pltpu.VMEM) for x in arrays]

    first = pl.pallas_call(
        functools.partial(first_kernel, group),
        out_shape=(
            near_core(1, rows), near_core(8, rows), pltpu.VMEM((1, blocks), jnp.int32),
            near_core(COUNT, dim), near_core(COUNT, width),
        ),
        in_specs=[smem, smem] + [vmem] * 3,
        out_specs=(vmem,) * 5,
        name="own_block",
    )(scal, block_order, q, key_own, gate_wq)
    near, scal, first = lax.optimization_barrier((near, scal, first))
    high, total, ordv, pq, xq = first
    pairs = []
    for y in range(ny):
        for c in range(2):
            other = y + 1 if y % 2 == c else y - 1
            pairs.append((2 * y + c, 2 * (other % ny) + c))
    turn = [(z, z ^ 1) for z in range(nz)]
    by_z = lax.ppermute(near, Z, turn)
    by_y = lax.ppermute(near, Y + ("c",), pairs)
    buffers = [pltpu.VMEM((STEP * BLK, rows), jnp.float32)] * 2
    state = (
        near_core(8, rows), near_core(8, rows), near_core(blocks, rows), near_core(blocks, 3 * dim)
    )
    seen = pl.pallas_call(
        functools.partial(near_kernel, own),
        out_shape=state,
        in_specs=[smem, smem] + [vmem] * 4,
        out_specs=(vmem,) * 4,
        scratch_shapes=buffers,
        name="teacher_near",
    )(scal, block_order, *pinned(q, near, high, total))
    seen, by_z = lax.optimization_barrier((seen, by_z))
    by_yz = lax.ppermute(by_z, Y + ("c",), pairs)
    seen = pl.pallas_call(
        functools.partial(far_kernel, own),
        out_shape=state,
        in_specs=[smem, smem] + [vmem] * 8,
        out_specs=(vmem,) * 4,
        scratch_shapes=buffers,
        name="teacher_far",
    )(scal, block_order, *pinned(q, by_z, by_y, high, *seen))
    target, grads = pl.pallas_call(
        functools.partial(kernel, own),
        out_shape=(f32(1, group, own, blocks), near_core(4 * dim, width)),
        in_specs=[smem, smem] + [vmem] * 11,
        out_specs=(vmem, vmem),
        scratch_shapes=[
            pltpu.VMEM((blocks, rows), jnp.float32),
            pltpu.VMEM((blocks, 3 * dim), jnp.float32),
            *buffers,
        ],
        name="teacher_gate",
    )(scal, block_order, *pinned(q, by_yz, ordv, high, *seen, pq, xq, gate_wk))

    parts = lax.axis_size(SCATTER)
    rest = lax.axis_size(REST)
    piece = 4 * dim // parts
    share = lax.all_to_all(grads.reshape(parts, piece, width), SCATTER, 0, 0, tiled=True)
    share = jnp.sum(share, axis=0)
    share = lax.all_to_all(
        jnp.broadcast_to(share[None], (rest, piece, width)), REST, 0, 0, tiled=True
    )
    share = jnp.sum(share, axis=0)
    grads = lax.all_to_all(
        jnp.broadcast_to(share[None], (parts, piece, width)), SCATTER, 0, 0, tiled=True
    ).reshape(4 * dim, width)
    grad_wq, grad_wk = pl.pallas_call(
        split_kernel,
        out_shape=(f32(dim, width), f32(3 * dim, width)),
        in_specs=[vmem],
        out_specs=(anywhere, anywhere),
        scratch_shapes=[pltpu.SemaphoreType.DMA((2,))],
        name="split_grads",
    )(*pinned(grads))
    return target, grad_wq, grad_wk


def solution(mesh):
    names = Y + Z + ("x",) + BATCH
    fine = Mesh(mesh.devices.reshape(4, 2, 2, 2, 4, 2, 2), names)
    rows = P(BATCH, CTX, "x", None)
    return jax.shard_map(
        body,
        mesh=fine,
        in_specs=(rows, rows, P(), P(), P(), P()),
        out_specs=(P(BATCH, "x", CTX, None), P(), P()),
        check_vma=False,
    )
```

```python
import functools
import math

import jax
import jax.numpy as jnp
from jax import lax
from jax.experimental import pallas as pl
from jax.experimental.pallas import tpu as pltpu
from jax.sharding import Mesh
from jax.sharding import PartitionSpec as P

BLK = 64
LANES = 128
COUNT = 16
STEP = 8
MASKED = -1e30
EPS = 1e-06
HIGHEST = lax.Precision.HIGHEST


Y = ("yh", "yl")
Z = ("zm", "zn")
CTX = Y + Z
FAR = ("yh", "zm")
BATCH = ("zh", "c")
SETS = ((0, 0), (0, 1), (1, 0), (1, 1))
SHARE = 2
SCATTER = ("x", "yl", "zn", "c")
REST = ("yh", "zh", "zm")


def dot(a, b, dims):
    return lax.dot_general(
        a, b, (dims, ((), ())), precision=HIGHEST, preferred_element_type=jnp.float32
    )


def scores(k, q):
    return lax.dot_general(k, q, (((1,), (1,)), ((), ())), preferred_element_type=jnp.float32)


def lane_part(rows, toks):
    tok = lax.rem(lax.broadcasted_iota(jnp.int32, (1, rows), 1), toks)
    return tok // BLK, lax.rem(tok, BLK)


def lane_block(scal, part, own):
    block = jnp.zeros_like(part)
    for i in range(own):
        block = jnp.where(part == i, scal[1 + i], block)
    return block


def tile_sum(s, new, scale):
    e = jnp.exp2((s.reshape(s.shape[0] // 8, 8, s.shape[1]) - new) * scale)
    return jnp.sum(e, axis=0)


def spread(x, op):
    for shift in (4, 2, 1):
        x = op(x, pltpu.roll(x, shift, 0))
    return x


def fold8(parts, op):
    sub = lax.broadcasted_iota(jnp.int32, parts[0].shape, 0)
    low = sub < 4
    t = []
    for i in range(4):
        a, b = parts[i], parts[i + 4]
        t.append(op(jnp.where(low, a, b), pltpu.roll(jnp.where(low, b, a), 4, 0)))
    for shift in (2, 1):
        half = len(t) // 2
        low = lax.rem(sub, 2 * shift) < shift
        t = [
            jnp.where(
                low,
                op(t[i], pltpu.roll(t[i], 8 - shift, 0)),
                op(t[i + half], pltpu.roll(t[i + half], shift, 0)),
            )
            for i in range(half)
        ]
    return t[0]


def fold_keys(k, reduce, op):
    parts = [
        reduce(k[j * BLK : (j + 1) * BLK].reshape(BLK // 8, 8, k.shape[1]), axis=0)
        for j in range(STEP)
    ]
    return fold8(parts, op)


def first_kernel(group, scal, order, q_ref, k_ref, wq, high_ref, total_ref, ord_out, pq_ref, xq_ref):
    rows, dim = q_ref.shape
    toks = rows // group
    own = toks // BLK
    scale = math.log2(math.e) / math.sqrt(dim)
    part, pos = lane_part(rows, toks)
    q = q_ref[...]
    s = scores(k_ref[...], q)
    tile = s[0:BLK]
    for i in range(1, own):
        tile = jnp.where(part == i, s[i * BLK : (i + 1) * BLK], tile)
    tile = jnp.where(lax.broadcasted_iota(jnp.int32, (BLK, rows), 0) <= pos, tile, MASKED)
    high = jnp.max(tile, axis=0, keepdims=True)
    high_ref[...] = high
    total_ref[...] = tile_sum(tile, high, scale)
    pq = jnp.sum(q.astype(jnp.float32).reshape(group * own, BLK, dim), axis=1) * (1.0 / BLK)
    pq = jnp.concatenate([pq, jnp.zeros((COUNT - group * own, dim), jnp.float32)], axis=0)
    pq_ref[...] = pq
    lane = lax.broadcasted_iota(jnp.int32, ord_out.shape, 1)
    ids = jnp.zeros(ord_out.shape, jnp.int32)
    share = ord_out.shape[1] // len(SETS)
    for i in range(ord_out.shape[1]):
        at = slot(scal, own, i // share, i % share // STEP, i % STEP)
        ids = jnp.where(lane == i, order[at], ids)
    ord_out[...] = ids
    xq_ref[...] = dot(pq, wq[...], ((1,), (0,)))


def slot(scal, own, which, c, j):
    dy, dz = SETS[which]
    fy = scal[1 + own] if dy == 0 else 1 - scal[1 + own]
    fz = scal[2 + own] if dz == 0 else 1 - scal[2 + own]
    y = 2 * (2 * c + j // (2 * own)) + fy
    z = 2 * (j // own % 2) + fz
    return (y * 4 + z) * own + j % own


def scan_keys(own, scal, order, parts, q, diag, high, total, m_ref, pk_ref, s0, s1, before_last=None):
    rows, dim = q.shape
    toks = own * BLK
    scale = math.log2(math.e) / math.sqrt(dim)
    width = STEP * BLK
    chunks = [
        (which, first + c, k_ref, c * width)
        for which, first, k_ref in parts
        for c in range(k_ref.shape[0] // width)
    ]
    part, _ = lane_part(rows, toks)
    block8 = jnp.broadcast_to(lane_block(scal, part, own), (8, rows))
    diag = jnp.broadcast_to(diag, (8, rows))
    col = lax.broadcasted_iota(jnp.int32, (STEP, width), 1) // BLK
    mean = jnp.where(col == lax.broadcasted_iota(jnp.int32, (STEP, width), 0), 1.0 / BLK, 0.0)
    mean = mean.astype(q.dtype)

    sub = lax.broadcasted_iota(jnp.int32, (STEP, LANES), 0)

    def fill(i, s_ref):
        which, c, k_ref, row = chunks[i]
        k = k_ref[row : row + width, :]
        s = scores(k, q)
        s_ref[...] = s
        tops = [
            jnp.max(s[j * BLK : (j + 1) * BLK].reshape(BLK // 8, 8, rows), axis=0)
            for j in range(STEP)
        ]
        top = fold8(tops, jnp.maximum)
        at = pl.ds((which * SHARE + c) * STEP, STEP)
        kb = jnp.zeros((STEP, LANES), jnp.int32)
        for j in range(STEP):
            kb = jnp.where(sub == j, order[slot(scal, own, which, c, j)], kb)
        kb = jnp.tile(kb, (1, rows // LANES))
        top = jnp.where(block8 > kb, top, jnp.where(block8 == kb, diag, MASKED))
        m_ref[at, :] = top
        kf = k.astype(jnp.float32)
        pk_ref[at, 0:dim] = fold_keys(kf, jnp.max, jnp.maximum)
        pk_ref[at, dim : 2 * dim] = fold_keys(kf, jnp.min, jnp.minimum)
        pk_ref[at, 2 * dim : 3 * dim] = lax.dot_general(
            mean, k, (((1,), (0,)), ((), ())), preferred_element_type=jnp.float32
        )
        return spread(top, jnp.maximum)

    def drain(i, s_ref, top, high, total):
        which, c = chunks[i][:2]
        new = jnp.maximum(high, top)
        total = total * jnp.exp2((high - new) * scale)
        for j in range(STEP):
            fresh = tile_sum(s_ref[j * BLK : (j + 1) * BLK, :], new, scale)
            total = total + jnp.where(block8 > order[slot(scal, own, which, c, j)], fresh, 0.0)
        return new, total

    bufs = (s0, s1)
    top = fill(0, s0)
    for i in range(len(chunks)):
        ahead = fill(i + 1, bufs[(i + 1) % 2]) if i + 1 < len(chunks) else None
        if i + 1 == len(chunks) and before_last is not None:
            before_last()
        high, total = drain(i, bufs[i % 2], top, high, total)
        top = ahead
    return high, total


def near_kernel(
    own, scal, order, q_ref, k_ref, diag_ref, total_ref,
    high_out, total_out, m_ref, pk_ref, s0, s1,
):
    diag = diag_ref[...]
    m_ref[...] = jnp.full(m_ref.shape, MASKED, jnp.float32)
    pk_ref[...] = jnp.zeros(pk_ref.shape, jnp.float32)
    high_out[...], total_out[...] = scan_keys(
        own, scal, order, [(0, 0, k_ref)], q_ref[...], diag,
        jnp.broadcast_to(diag, high_out.shape), total_ref[...], m_ref, pk_ref, s0, s1,
    )


def far_kernel(
    own, scal, order, q_ref, z_ref, y_ref, diag_ref, high_ref, total_ref, m_in, pk_in,
    high_out, total_out, m_ref, pk_ref, s0, s1,
):
    m_ref[...] = m_in[...]
    pk_ref[...] = pk_in[...]
    high_out[...], total_out[...] = scan_keys(
        own, scal, order, [(1, 0, z_ref), (2, 0, y_ref)], q_ref[...], diag_ref[...],
        high_ref[...], total_ref[...], m_ref, pk_ref, s0, s1,
    )


def kernel(
    own, scal, order, q_ref, k_ref, ordv, diag_ref, high_ref, total_ref, m_in, pk_in,
    pq_ref, xq_ref, wk, t_ref, g_ref, m_ref, pk_ref, s0, s1,
):
    rows, dim = q_ref.shape
    toks = own * BLK
    group = rows // toks
    blocks = order.shape[0]
    length = scal[0]
    scale = math.log2(math.e) / math.sqrt(dim)
    part, pos = lane_part(rows, toks)
    block = lane_block(scal, part, own)
    m_ref[...] = m_in[...]
    pk_ref[...] = pk_in[...]
    row = lax.broadcasted_iota(jnp.int32, (COUNT, 1), 0)
    qblock = lane_block(scal, lax.rem(row, own), own)
    gate = {}

    def gate_forward():
        pq = pq_ref[...]
        xq = xq_ref[...]
        pk = pk_ref[...]
        xk = dot(pk, wk[...], ((1,), (0,)))
        rq = lax.rsqrt(jnp.mean(xq * xq, axis=1, keepdims=True) + EPS)
        rk = lax.rsqrt(jnp.mean(xk * xk, axis=1, keepdims=True) + EPS)
        uq = xq * rq
        uk = xk * rk
        gate_scale = 1.0 / math.sqrt(xq.shape[1])
        logits = dot(uq, uk, ((1,), (1,))) * gate_scale
        kblock = ordv[...]
        allowed = (kblock <= qblock) & (kblock * BLK < length)
        weights = jnp.where(allowed, jnp.exp(logits), 0.0)
        soft = weights / jnp.sum(weights, axis=1, keepdims=True)
        gate.update(pq=pq, pkt=jnp.transpose(pk), uq=uq, uk=uk, rq=rq, rk=rk, soft=soft)
        gate.update(scale=gate_scale)

    high, total = scan_keys(
        own, scal, order, [(3, 0, k_ref)], q_ref[...], diag_ref[...], high_ref[...],
        total_ref[...], m_ref, pk_ref, s0, s1, gate_forward,
    )

    log_total = jnp.log2(jnp.sum(total, axis=0, keepdims=True))
    depth = jnp.where(pos + block * BLK < length, (m_ref[...] - high[0:1]) * scale - log_total, MASKED)
    depth = jnp.max(jnp.transpose(depth).reshape(group * own, BLK, blocks), axis=1)
    pad = COUNT - group * own
    depth = jnp.concatenate([depth, jnp.full((pad, blocks), MASKED, jnp.float32)], axis=0)
    pooled = jnp.exp2(depth)
    good = (qblock * BLK < length) & (row < group * own)
    totals = jnp.sum(pooled, axis=1, keepdims=True)
    target = jnp.where(good, pooled / jnp.where(good, totals, 1.0), 0.0)
    place = lax.broadcasted_iota(jnp.int32, (blocks, blocks), 1)
    y, z = place // (4 * own), place // own % 4
    fy, fz = y % 2 != scal[1 + own], z % 2 != scal[2 + own]
    at = jnp.where(fy, 2, 0) + jnp.where(fz, 1, 0)
    at = ((at * 4 + y // 2) * 2 + z // 2) * own + place % own
    pick = jnp.where(lax.broadcasted_iota(jnp.int32, (blocks, blocks), 0) == at, 1.0, 0.0)
    laid = dot(target, pick, ((1,), (0,)))
    for h in range(group):
        t_ref[0, h] = laid[own * h : own * (h + 1)]

    dl = (jnp.where(good, gate["soft"], 0.0) - target) * gate["scale"]
    uq, uk, rq, rk = gate["uq"], gate["uk"], gate["rq"], gate["rk"]
    duq = dot(dl, uk, ((1,), (0,)))
    duk = dot(dl, uq, ((0,), (0,)))
    dxq = rq * (duq - uq * jnp.mean(duq * uq, axis=1, keepdims=True))
    dxk = rk * (duk - uk * jnp.mean(duk * uk, axis=1, keepdims=True))
    g_ref[0:dim, :] = dot(gate["pq"], dxq, ((0,), (0,)))
    g_ref[dim : 4 * dim, :] = dot(gate["pkt"], dxk, ((1,), (0,)))


def split_kernel(g_ref, q_ref, k_ref, sem):
    rows = q_ref.shape[0]
    copies = [
        pltpu.make_async_copy(g_ref.at[pl.ds(0, rows)], q_ref, sem.at[0]),
        pltpu.make_async_copy(g_ref.at[pl.ds(rows, k_ref.shape[0])], k_ref, sem.at[1]),
    ]
    for copy in copies:
        copy.start()
    for copy in copies:
        copy.wait()


def repeat_kernel(x_ref, o_ref, sem):
    copies = [
        pltpu.make_async_copy(x_ref, o_ref.at[i], sem.at[i]) for i in range(o_ref.shape[0])
    ]
    for copy in copies:
        copy.start()
    for copy in copies:
        copy.wait()


def body(queries, key_rows, block_order, conv_len, gate_wq, gate_wk):
    toks = queries.shape[1]
    group = queries.shape[2]
    dim = queries.shape[3]
    own = toks // BLK
    rows = group * toks
    blocks = block_order.shape[0]
    width = gate_wq.shape[1]
    key_own = key_rows[0, :, 0, :]
    ny, nz = lax.axis_size(Y), lax.axis_size(Z)
    spots = jnp.stack([lax.axis_index("yl"), lax.axis_index("zn")])
    peers = ny * nz // len(SETS)
    smem = pl.BlockSpec(memory_space=pltpu.SMEM)
    vmem = pl.BlockSpec(memory_space=pltpu.VMEM)
    anywhere = pl.BlockSpec(memory_space=pl.ANY)
    repeated = pl.pallas_call(
        repeat_kernel,
        out_shape=jax.ShapeDtypeStruct((peers, toks, dim), key_own.dtype),
        in_specs=[vmem],
        out_specs=anywhere,
        scratch_shapes=[pltpu.SemaphoreType.DMA((peers,))],
        name="repeat_keys",
    )(key_own)
    near = lax.all_to_all(repeated, FAR, 0, 0, tiled=True).reshape(peers * toks, dim)
    length = lax.dynamic_index_in_dim(conv_len, lax.axis_index(BATCH))
    mine = lax.dynamic_slice_in_dim(block_order, lax.axis_index(CTX) * own, own)
    scal = jnp.concatenate([length, mine, spots])
    q = jnp.transpose(queries[0], (1, 0, 2)).reshape(rows, dim)

    def f32(*shape):
        return jax.ShapeDtypeStruct(shape, jnp.float32)

    def near_core(*shape):
        return pltpu.VMEM(shape, jnp.float32)

    def pinned(*arrays):
        return [pltpu.with_memory_space_constraint(x, pltpu.VMEM) for x in arrays]

    first = pl.pallas_call(
        functools.partial(first_kernel, group),
        out_shape=(
            near_core(1, rows), near_core(8, rows), pltpu.VMEM((1, blocks), jnp.int32),
            near_core(COUNT, dim), near_core(COUNT, width),
        ),
        in_specs=[smem, smem] + [vmem] * 3,
        out_specs=(vmem,) * 5,
        name="own_block",
    )(scal, block_order, q, key_own, gate_wq)
    near, scal, first = lax.optimization_barrier((near, scal, first))
    high, total, ordv, pq, xq = first
    pairs = []
    for y in range(ny):
        for c in range(2):
            other = y + 1 if y % 2 == c else y - 1
            pairs.append((2 * y + c, 2 * (other % ny) + c))
    turn = [(z, z ^ 1) for z in range(nz)]
    across = [
        ((a // 2 * nz + z) * 2 + a % 2, (b // 2 * nz + (z ^ 1)) * 2 + b % 2)
        for a, b in pairs
        for z in range(nz)
    ]
    by_yz = lax.ppermute(near, Y + Z + ("c",), across)
    by_z = lax.ppermute(near, Z, turn)
    by_y = lax.ppermute(near, Y + ("c",), pairs)
    buffers = [pltpu.VMEM((STEP * BLK, rows), jnp.float32)] * 2
    state = (
        near_core(8, rows), near_core(8, rows), near_core(blocks, rows), near_core(blocks, 3 * dim)
    )
    seen = pl.pallas_call(
        functools.partial(near_kernel, own),
        out_shape=state,
        in_specs=[smem, smem] + [vmem] * 4,
        out_specs=(vmem,) * 4,
        scratch_shapes=buffers,
        name="teacher_near",
    )(scal, block_order, *pinned(q, near, high, total))
    seen = pl.pallas_call(
        functools.partial(far_kernel, own),
        out_shape=state,
        in_specs=[smem, smem] + [vmem] * 8,
        out_specs=(vmem,) * 4,
        scratch_shapes=buffers,
        name="teacher_far",
    )(scal, block_order, *pinned(q, by_z, by_y, high, *seen))
    target, grads = pl.pallas_call(
        functools.partial(kernel, own),
        out_shape=(f32(1, group, own, blocks), near_core(4 * dim, width)),
        in_specs=[smem, smem] + [vmem] * 11,
        out_specs=(vmem, vmem),
        scratch_shapes=[
            pltpu.VMEM((blocks, rows), jnp.float32),
            pltpu.VMEM((blocks, 3 * dim), jnp.float32),
            *buffers,
        ],
        name="teacher_gate",
    )(scal, block_order, *pinned(q, by_yz, ordv, high, *seen, pq, xq, gate_wk))

    parts = lax.axis_size(SCATTER)
    rest = lax.axis_size(REST)
    piece = 4 * dim // parts
    share = lax.all_to_all(grads.reshape(parts, piece, width), SCATTER, 0, 0, tiled=True)
    share = jnp.sum(share, axis=0)
    share = lax.all_to_all(
        jnp.broadcast_to(share[None], (rest, piece, width)), REST, 0, 0, tiled=True
    )
    share = jnp.sum(share, axis=0)
    grads = lax.all_to_all(
        jnp.broadcast_to(share[None], (parts, piece, width)), SCATTER, 0, 0, tiled=True
    ).reshape(4 * dim, width)
    grad_wq, grad_wk = pl.pallas_call(
        split_kernel,
        out_shape=(f32(dim, width), f32(3 * dim, width)),
        in_specs=[vmem],
        out_specs=(anywhere, anywhere),
        scratch_shapes=[pltpu.SemaphoreType.DMA((2,))],
        name="split_grads",
    )(*pinned(grads))
    return target, grad_wq, grad_wk


def solution(mesh):
    names = Y + Z + ("x",) + BATCH
    fine = Mesh(mesh.devices.reshape(4, 2, 2, 2, 4, 2, 2), names)
    rows = P(BATCH, CTX, "x", None)
    return jax.shard_map(
        body,
        mesh=fine,
        in_specs=(rows, rows, P(), P(), P(), P()),
        out_specs=(P(BATCH, "x", CTX, None), P(), P()),
        check_vma=False,
    )
```
